32 devices in a mesh: blk: 4 (over y, x), batch: 8 (over z, core).
Axes of the slice: x: 2, y: 2, z: 4, core: 2. Of those that a mesh axis runs over, the one named last changes fastest.
Arguments:
- hidden_in: bfloat16 [4, 8, 512, 768], P('blk', 'batch'), may hold values from -6 to 6
- lengths: int32 [2, 8], P(None, 'batch'), may hold values from 576 to 1024, as said below
- head_order: int32 [12], replicated, may hold values from 0 to 11, each once
- w_qkv: bfloat16 [768, 2304], replicated, may hold values from -0.21875 to 0.21875
- w_out: bfloat16 [768, 768], replicated, may hold values from -3.5 to 3.5
- ln1_gain: float32 [768], replicated, may hold values from 0.25 to 1.75
- ln1_bias: float32 [768], replicated, may hold values from -3 to 3
- w_up: bfloat16 [768, 3072], replicated, may hold values from -0.21875 to 0.21875
- w_down: bfloat16 [3072, 768], replicated, may hold values from -0.109375 to 0.109375
- ln2_gain: float32 [768], replicated, may hold values from 0.25 to 1.75
- ln2_bias: float32 [768], replicated, may hold values from -3 to 3
- grad_out: bfloat16 [4, 8, 512, 768], P('blk', 'batch'), may hold values from -6 to 6
Outputs:
- hidden_out: bfloat16 [4, 8, 512, 768], P('blk', 'batch')
- grad_in: bfloat16 [4, 8, 512, 768], P('blk', 'batch')
- grad_w_qkv: float32 [768, 2304], P('batch', 'blk')
- grad_w_out: float32 [768, 768], P('batch', 'blk')
- grad_ln1_gain: float32 [768], P('batch')
- grad_ln1_bias: float32 [768], P('batch')
- grad_w_up: float32 [768, 3072], P('batch', 'blk')
- grad_w_down: float32 [3072, 768], P('batch', 'blk')
- grad_ln2_gain: float32 [768], P('batch')
- grad_ln2_bias: float32 [768], P('batch')
The draws below stay inside these ranges and needn't reach their ends.
Inputs may be any that keep to these rules, and one draw needn't show every extreme that they name: `lengths`: real tokens of each sequence out of its 1024 slots; both the least and the most allowed length occur in every draw.
All inputs are finite; a program needn't handle non-finite values.
Results may differ from the reference program's by a relative error of at most 0.015.
Values may be sent and summed in bfloat16 or wider, within the bound.
No kernel may reach another device: no remote copies, remote signals or barrier semaphores. Data moves between devices by JAX's collectives and lax.ppermute only.
A program may use at most 128 MiB of HBM per device.

```python
import math
import jax
import jax.numpy as jnp
from jax import lax

D = 768
H = 12
HD = 64
FF = 3072
BLK = 512
PAIRS = 2
SEQS = 8
N_BLK = 4


def draw_lengths(key, part):
    number = PAIRS * SEQS
    lowest = BLK + BLK // 8
    drawn = jax.random.randint(jax.random.fold_in(key, 11), (number,), lowest, 2 * BLK + 1)
    slot_one = jax.random.randint(jax.random.fold_in(key, 12), (), 0, number)
    slot_two = (slot_one + jax.random.randint(jax.random.fold_in(key, 13), (), 1, number)) % number
    drawn = drawn.at[slot_one].set(2 * BLK).at[slot_two].set(lowest)
    return drawn.reshape(PAIRS, SEQS).astype(jnp.int32)


def block_scale(stream_key, dims, pieces, least, top_value):
    loudness = 1.0
    for dim, shards_of in pieces:
        steps = jax.random.uniform(jax.random.fold_in(jax.random.fold_in(stream_key, 6), dim), (shards_of,), jnp.float32, least / len(pieces), top_value / len(pieces))
        loudness = loudness * jnp.repeat(jnp.exp(steps), dims[dim] // shards_of).reshape((-1,) + (1,) * (len(dims) - 1 - dim))
    return loudness


def scatter_about(key, extent, width, limit, pieces=(), kind=jnp.bfloat16):
    result = jax.random.normal(key, extent, jnp.float32) * width
    if len(pieces) > 0:
        result = block_scale(key, extent, pieces, -0.22, 0.18) * result
    return jnp.clip(result, min=-limit, max=limit).astype(kind)


def setup_inputs(seed: int = 0) -> dict:
    seeds = jax.random.split(jax.random.key(seed), 13)
    hidden_in = scatter_about(seeds[0], (N_BLK, SEQS, BLK, D), 1.0, 6.0, ((0, 4), (1, 8)))
    lengths = draw_lengths(jax.random.fold_in(seeds[12], 71), 0)
    head_order = jax.random.permutation(seeds[2], H).astype(jnp.int32)
    w_qkv = scatter_about(seeds[3], (D, 3 * D), D ** -0.5, 0.21875)
    w_out = scatter_about(seeds[4], (D, D), (max(1, D // 256)) ** -0.5, 3.5)
    ln1_gain = jnp.clip(1.0 + 0.15 * jax.random.normal(seeds[5], (D,), jnp.float32), 0.25, 1.75)
    ln1_bias = scatter_about(seeds[6], (D,), 0.5, 3.0, (), jnp.float32)
    w_up = scatter_about(seeds[7], (D, FF), D ** -0.5, 0.21875)
    w_down = scatter_about(seeds[8], (FF, D), FF ** -0.5, 0.109375)
    ln2_gain = jnp.clip(1.0 + 0.15 * jax.random.normal(seeds[9], (D,), jnp.float32), 0.25, 1.75)
    ln2_bias = scatter_about(seeds[10], (D,), 0.5, 3.0, (), jnp.float32)
    grad_out = scatter_about(seeds[11], (N_BLK, SEQS, BLK, D), 1.0, 6.0, ((0, 4), (1, 8)))
    return dict(hidden_in=hidden_in, lengths=lengths, head_order=head_order, w_qkv=w_qkv, w_out=w_out, ln1_gain=ln1_gain, ln1_bias=ln1_bias, w_up=w_up, w_down=w_down, ln2_gain=ln2_gain, ln2_bias=ln2_bias, grad_out=grad_out)


precise = lax.Precision.HIGHEST

@jax.custom_vjp
def low(v):
    return lax.optimization_barrier(v.astype(jnp.bfloat16)).astype(jnp.float32)

@jax.custom_vjp
def low_back(v):
    return v

def low_keep(v):
    return (low(v), None)

def low_pass(kept, grad):
    return (grad,)

def back_keep(v):
    return (v, None)

def back_low(kept, grad):
    return (low(grad),)
low.defvjp(low_keep, low_pass)
low_back.defvjp(back_keep, back_low)

def layer_norm(hidden, ln_gain, ln_bias):
    row_mean = lax.optimization_barrier(jnp.mean(hidden, axis=-1, keepdims=True))
    centred = hidden - row_mean
    row_var = lax.optimization_barrier(jnp.mean(centred * centred, axis=-1, keepdims=True))
    return centred * lax.rsqrt(row_var + 1e-06) * ln_gain + ln_bias

def reference(hidden_in, lengths, head_order, w_qkv, w_out, ln1_gain, ln1_bias, w_up, w_down, ln2_gain, ln2_bias, grad_out):
    seq_total = PAIRS * SEQS
    group_size = math.gcd(seq_total, 4)
    score_scale = 1.0 / math.sqrt(HD)
    swapped = head_order >= H // 2
    block_ids = jnp.arange(2, dtype=jnp.int32)[:, None]
    key_start = BLK * jnp.where(swapped[None, :], 1 - block_ids, block_ids)
    key_place = key_start[:, :, None, None] + jnp.arange(BLK, dtype=jnp.int32)[None, None, None, :]

    def to_groups(array):
        return array.astype(jnp.float32).reshape(PAIRS, 2, SEQS, BLK, D).transpose(0, 2, 1, 3, 4).reshape(seq_total // group_size, group_size, 2 * BLK, D)

    def from_groups(array):
        return array.reshape(PAIRS, SEQS, 2, BLK, D).transpose(0, 2, 1, 3, 4).reshape(N_BLK, SEQS, BLK, D)

    def attend_seq(seq_item):
        query_all, key_all, value_all, length = seq_item
        raw_scores = low_back(jnp.einsum('bqhd,bkhd->bhqk', query_all, key_all, precision=precise))
        scores = jnp.where(key_place < length, raw_scores * score_scale, -1e+30)
        row_max = lax.optimization_barrier(jnp.max(scores, axis=-1, keepdims=True))
        exp_terms = jnp.exp(scores - row_max)
        probs = exp_terms / lax.optimization_barrier(jnp.sum(exp_terms, axis=-1, keepdims=True))
        context = jnp.einsum('bhqk,bkhd->bqhd', low(probs), value_all, precision=precise)
        return context.reshape(2 * BLK, D)

    def forward(rows_in, length_rows, weights):
        wq_all, wo_all, gain_one, bias_one, wu_all, wd_all, gain_two, bias_two = weights
        tokens = rows_in.reshape(-1, D)
        qkv = low_back(low(jnp.dot(tokens, wq_all, precision=precise)))
        qkv = qkv.reshape(group_size, 2, BLK, 3, H, HD)
        queries = qkv[:, :, :, 0]
        key_rows = qkv[:, :, :, 1]
        value_rows = qkv[:, :, :, 2]
        key_target = jnp.where(swapped[:, None], key_rows[:, ::-1], key_rows)
        value_target = jnp.where(swapped[:, None], value_rows[:, ::-1], value_rows)
        contexts = lax.map(jax.checkpoint(attend_seq), (queries, key_target, value_target, length_rows))
        context = low_back(low(contexts.reshape(-1, D)))
        attn_out = low_back(jnp.dot(context, wo_all, precision=precise))
        normed_one = layer_norm(tokens + attn_out, gain_one, bias_one)
        pre_act = low_back(jnp.dot(low(normed_one), wu_all, precision=precise))
        act_out = low(jax.nn.gelu(pre_act, approximate=False))
        down_out = low_back(jnp.dot(act_out, wd_all, precision=precise))
        normed_two = layer_norm(normed_one + down_out, gain_two, bias_two)
        return normed_two.reshape(group_size, 2 * BLK, D)
    params = (w_qkv.astype(jnp.float32), w_out.astype(jnp.float32), ln1_gain, ln1_bias, w_up.astype(jnp.float32), w_down.astype(jnp.float32), ln2_gain, ln2_bias)
    inputs = to_groups(hidden_in)
    cotangents = to_groups(grad_out)
    length_groups = lengths.reshape(seq_total // group_size, group_size)

    def one_group(totals, group_item):
        rows_in, grads_in, length_rows = group_item

        def forward_of(rows_now, weights):
            return forward(rows_now, length_rows, weights)
        out_rows, pull_back = jax.vjp(forward_of, rows_in, params)
        grad_rows, grad_params = pull_back(grads_in)
        totals = jax.tree.map(jnp.add, totals, grad_params)
        return (totals, (out_rows.astype(jnp.bfloat16), grad_rows.astype(jnp.bfloat16)))
    initial = jax.tree.map(lambda weight_arr: jnp.zeros(weight_arr.shape, jnp.float32), params)
    totals, (out_all, grad_all) = lax.scan(one_group, initial, (inputs, cotangents, length_groups))
    return (from_groups(out_all), from_groups(grad_all), totals[0], totals[1], totals[2], totals[3], totals[4], totals[5], totals[6], totals[7])
```

```python
import math

import jax
import jax.numpy as jnp
from jax import lax
from jax.sharding import PartitionSpec as P


def from_partner(block, axis, stride):
    count = lax.axis_size(axis)
    route = []
    for low in range(count):
        high = low | 1 << stride
        if high != low and high < count:
            route += [(low, high), (high, low)]
    return lax.ppermute(block, axis, route)


def layer_norm(hidden, ln_gain, ln_bias):
    row_mean = jnp.mean(hidden, axis=-1, keepdims=True)
    centred = hidden - row_mean
    row_var = jnp.mean(centred * centred, axis=-1, keepdims=True)
    return centred * lax.rsqrt(row_var + 1e-06) * ln_gain + ln_bias


def exact_gelu(pre_act):
    return jax.nn.gelu(pre_act, approximate=False)


def outer_product(left_rows, right_rows):
    return lax.dot_general(
        left_rows, right_rows, (((0,), (0,)), ((), ())), preferred_element_type=jnp.float32
    )


def through_weight(grad_rows, weight_mat):
    return lax.dot_general(
        grad_rows, weight_mat, (((1,), (1,)), ((), ())), preferred_element_type=jnp.float32
    )


def swap(block, axis, bits):
    return lax.ppermute(block, axis, [(i, i ^ bits) for i in range(lax.axis_size(axis))])


def split_parts(*mats, extra=None):
    blks = lax.axis_size("blk")
    lines = lax.axis_size("batch") // 2
    me = lax.axis_index("blk")
    core = lax.axis_index("batch") % 2
    pieces = []
    for mat in mats:
        rows = mat.shape[0] // (2 * lines)
        pieces.append(mat.astype(jnp.bfloat16).reshape(lines, 2, rows, blks, -1))
    if extra is not None:
        thin = extra.astype(jnp.bfloat16).reshape(lines, 2, rows, 1, -1)
        pieces.append(jnp.broadcast_to(thin, thin.shape[:3] + (blks,) + thin.shape[4:]))
    whole = jnp.concatenate(pieces, axis=4)

    def half(which, distance):
        part = lax.dynamic_index_in_dim(whole, which, 1, keepdims=False)
        return lax.dynamic_index_in_dim(part, me ^ distance, 2, keepdims=False)

    keep = [half(core, distance) for distance in range(blks)]
    send = jnp.stack([half(1 - core, distance) for distance in range(blks)])
    return keep, send


def add_up(*parts):
    total = parts[0].astype(jnp.float32)
    for part in parts[1:]:
        total = total + part.astype(jnp.float32)
    return total


def reduce_parts(keep, send):
    got = swap(send, "batch", 1)
    chip = [add_up(part, got[i]).astype(jnp.bfloat16) for i, part in enumerate(keep)]
    blk = [chip[0]] + [swap(chip[i], "blk", i) for i in range(1, len(chip))]
    total = add_up(*blk)
    lines = total.shape[0]
    line = lax.axis_index("batch") // 2
    while lines > 4:
        half = lines // 2
        low = line // half
        pairs = total.astype(jnp.bfloat16).reshape((2, half) + total.shape[1:])
        mine = lax.dynamic_index_in_dim(pairs, low, 0, keepdims=False)
        theirs = lax.dynamic_index_in_dim(pairs, 1 - low, 0, keepdims=False)
        total = add_up(mine, swap(theirs, "batch", 2 * half))
        line, lines = line % half, half
    total = total.astype(jnp.bfloat16)
    mine = lax.dynamic_index_in_dim(total, line, 0, keepdims=False)
    parts = [mine]
    for i in range(1, lines):
        theirs = lax.dynamic_index_in_dim(total, line ^ i, 0, keepdims=False)
        parts.append(swap(theirs, "batch", 2 * i))
    return add_up(*parts)


def shards(
    hidden_in,
    lengths,
    head_order,
    w_qkv,
    w_out,
    ln1_gain,
    ln1_bias,
    w_up,
    w_down,
    ln2_gain,
    ln2_bias,
    grad_out,
):
    seq_dev = hidden_in.shape[1]
    block_len = hidden_in.shape[2]
    model_width = hidden_in.shape[3]
    head_count = head_order.shape[0]
    head_dim = model_width // head_count
    half_heads = head_count // 2
    row_count = seq_dev * block_len
    score_scale = 1.0 / math.sqrt(head_dim)
    block_half = lax.axis_index("blk") % 2
    seq_lengths = lax.dynamic_index_in_dim(lengths, lax.axis_index("blk") // 2, 0, keepdims=False)
    swapped = head_order >= half_heads
    picked = jnp.where(
        swapped, head_count + head_order - half_heads, jnp.arange(head_count, dtype=jnp.int32)
    )
    sent_heads = jnp.argsort(head_order)[half_heads:]
    key_start = block_len * jnp.where(swapped, 1 - block_half, block_half)
    key_place = key_start[:, None] + jnp.arange(block_len, dtype=jnp.int32)[None, :]

    def outgoing(pair_arrays):
        return jnp.take(pair_arrays, sent_heads, axis=3).reshape(
            2, seq_dev, block_len, half_heads * head_dim
        )

    def gather_heads(local_arrays, partner_arrays):
        partner_arrays = partner_arrays.reshape(2, seq_dev, block_len, half_heads, head_dim)
        return jnp.take(jnp.concatenate([local_arrays, partner_arrays], axis=3), picked, axis=3)

    def scores_of(query_blk, key_blk, length):
        raw_scores = jnp.einsum(
            "qhd,khd->hqk", query_blk, key_blk, preferred_element_type=jnp.float32
        )
        return jnp.where((key_place < length)[:, None, :], raw_scores * score_scale, -1e30)

    inputs = hidden_in.reshape(row_count, model_width)
    qkv = jnp.dot(inputs, w_qkv, preferred_element_type=jnp.float32).astype(jnp.bfloat16)
    qkv = qkv.reshape(seq_dev, block_len, 3, head_count, head_dim)
    queries = qkv[:, :, 0]
    own_pair = jnp.stack([qkv[:, :, 1], qkv[:, :, 2]], axis=0)
    incoming = from_partner(outgoing(own_pair), "blk", 0)
    target_pair = gather_heads(own_pair, incoming)

    def attend(seq_item):
        query_blk, key_blk, value_blk, length = seq_item
        scores = scores_of(query_blk, key_blk, length)
        row_max = jnp.max(scores, axis=-1, keepdims=True)
        exp_terms = jnp.exp(scores - row_max)
        row_total = jnp.sum(exp_terms, axis=-1, keepdims=True)
        probs_low = (exp_terms / row_total).astype(jnp.bfloat16)
        context = jnp.einsum(
            "hqk,khd->qhd", probs_low, value_blk, preferred_element_type=jnp.float32
        )
        return (
            context.astype(jnp.bfloat16).reshape(block_len, model_width),
            (row_max + jnp.log(row_total))[..., 0],
        )

    contexts, log_totals = lax.map(attend, (queries, target_pair[0], target_pair[1], seq_lengths))
    context_rows = contexts.reshape(row_count, model_width)
    attn_out = jnp.dot(context_rows, w_out, preferred_element_type=jnp.float32)
    resid_one = inputs.astype(jnp.float32) + attn_out
    normed_one, ln1_back = jax.vjp(layer_norm, resid_one, ln1_gain, ln1_bias)
    up_in = normed_one.astype(jnp.bfloat16)
    pre_act = jnp.dot(up_in, w_up, preferred_element_type=jnp.float32)
    act_out, gelu_back = jax.vjp(exact_gelu, pre_act)
    act_low = act_out.astype(jnp.bfloat16)
    down_out = jnp.dot(act_low, w_down, preferred_element_type=jnp.float32)
    normed_two, ln2_back = jax.vjp(layer_norm, normed_one + down_out, ln2_gain, ln2_bias)
    hidden_out = normed_two.astype(jnp.bfloat16).reshape(hidden_in.shape)
    d_out = grad_out.reshape(row_count, model_width).astype(jnp.float32)
    d_two, g_gain2, g_bias2 = ln2_back(d_out)
    d_down = d_two.astype(jnp.bfloat16)
    gw_down = outer_product(act_low, d_down)
    (d_pre,) = gelu_back(through_weight(d_down, w_down))
    d_pre_low = d_pre.astype(jnp.bfloat16)
    gw_up = outer_product(up_in, d_pre_low)
    d_one = d_two + through_weight(d_pre_low, w_up)
    d_resid1, g_gain1, g_bias1 = ln1_back(d_one)
    d_attn = d_resid1.astype(jnp.bfloat16)
    gw_out = outer_product(context_rows, d_attn)
    d_context = (
        through_weight(d_attn, w_out)
        .astype(jnp.bfloat16)
        .reshape(seq_dev, block_len, head_count, head_dim)
    )

    def attend_back(seq_item):
        query_blk, key_blk, value_blk, length, log_total, d_ctx = seq_item
        scores = scores_of(query_blk, key_blk, length)
        probs = jnp.exp(scores - log_total[..., None])
        probs_low = probs.astype(jnp.bfloat16)
        d_value = jnp.einsum("hqk,qhd->khd", probs_low, d_ctx, preferred_element_type=jnp.float32)
        d_probs = jnp.einsum("qhd,khd->hqk", d_ctx, value_blk, preferred_element_type=jnp.float32)
        d_scores = (
            probs * (d_probs - jnp.sum(probs * d_probs, axis=-1, keepdims=True)) * score_scale
        )
        d_scores = d_scores.astype(jnp.bfloat16)
        d_query = jnp.einsum("hqk,khd->qhd", d_scores, key_blk, preferred_element_type=jnp.float32)
        d_key = jnp.einsum("hqk,qhd->khd", d_scores, query_blk, preferred_element_type=jnp.float32)
        return (
            d_query.astype(jnp.bfloat16),
            d_key.astype(jnp.bfloat16),
            d_value.astype(jnp.bfloat16),
        )

    d_queries, d_keys, d_values = lax.map(
        attend_back, (queries, target_pair[0], target_pair[1], seq_lengths, log_totals, d_context)
    )
    d_target = jnp.stack([d_keys, d_values], axis=0)
    returned = from_partner(outgoing(d_target), "blk", 0)
    d_own = gather_heads(d_target, returned)
    d_qkv = jnp.stack([d_queries, d_own[0], d_own[1]], axis=2).reshape(row_count, 3 * model_width)
    gw_qkv = outer_product(inputs, d_qkv)
    grad_in = (
        (d_resid1 + through_weight(d_qkv, w_qkv)).astype(jnp.bfloat16).reshape(hidden_in.shape)
    )
    gains = jnp.stack([g_gain1, g_bias1, g_gain2, g_bias2], axis=1)
    own_down = reduce_parts(*split_parts(gw_down))
    own_up = reduce_parts(*split_parts(gw_up, gw_out))
    own_qkv = reduce_parts(*split_parts(gw_qkv, extra=gains))
    qkv_cols = gw_qkv.shape[1] // lax.axis_size("blk")
    up_cols = gw_up.shape[1] // lax.axis_size("blk")
    return (
        hidden_out,
        grad_in,
        own_qkv[:, :qkv_cols],
        own_up[:, up_cols:],
        own_qkv[:, qkv_cols],
        own_qkv[:, qkv_cols + 1],
        own_up[:, :up_cols],
        own_down,
        own_qkv[:, qkv_cols + 2],
        own_qkv[:, qkv_cols + 3],
    )


def solution(mesh):
    return jax.shard_map(
        shards,
        mesh=mesh,
        in_specs=(
            P("blk", "batch", None, None),
            P(None, "batch"),
            P(),
            P(),
            P(),
            P(),
            P(),
            P(),
            P(),
            P(),
            P(),
            P("blk", "batch", None, None),
        ),
        out_specs=(
            P("blk", "batch", None, None),
            P("blk", "batch", None, None),
            P("batch", "blk"),
            P("batch", "blk"),
            P("batch"),
            P("batch"),
            P("batch", "blk"),
            P("batch", "blk"),
            P("batch"),
            P("batch"),
        ),
        check_vma=False,
    )
```

```python
import functools
import math

import jax
import jax.numpy as jnp
from jax import lax
from jax.experimental import pallas as pl
from jax.experimental.pallas import tpu as pltpu
from jax.sharding import PartitionSpec as P

F32 = jnp.float32
BF16 = jnp.bfloat16
VMEM_BYTES = 56 << 20
WIDE = 256
FF_BLOCKS = 8
EPS = 1e-06
NEG = -1e30
LOG2E = math.log2(math.e)


def swap(block, axis, bits):
    return lax.ppermute(block, axis, [(i, i ^ bits) for i in range(lax.axis_size(axis))])


def mm(a, b):
    return lax.dot_general(a, b, (((1,), (0,)), ((), ())), preferred_element_type=F32)


def mm_nt(a, b):
    return lax.dot_general(a, b, (((1,), (1,)), ((), ())), preferred_element_type=F32)


def whole(shape):
    return pl.BlockSpec(shape, lambda *_: (0,) * len(shape), pipeline_mode=pl.Buffered(1))


def cost(flops, moved, exps=0):
    return pl.CostEstimate(flops=flops, bytes_accessed=moved, transcendentals=exps)


def params(**kw):
    return pltpu.CompilerParams(vmem_limit_bytes=VMEM_BYTES, **kw)


def shape_of(shape, dtype):
    return jax.ShapeDtypeStruct(shape, dtype)


def project_kernel(x_ref, w_ref, qkv_ref, xt_ref):
    @pl.when(pl.program_id(0) == 0)
    def _():
        xt_ref[...] = x_ref[...].T

    qkv_ref[...] = mm(x_ref[...], w_ref[...]).astype(BF16)


def project(x, w_qkv):
    rows, width = x.shape
    cols = w_qkv.shape[1]
    blk = width // 2
    return pl.pallas_call(
        project_kernel,
        grid=(cols // blk,),
        in_specs=[whole(x.shape), pl.BlockSpec((width, blk), lambda j: (0, j))],
        out_specs=[pl.BlockSpec((rows, blk), lambda j: (0, j)), whole((width, rows))],
        out_shape=[shape_of((rows, cols), BF16), shape_of((width, rows), BF16)],
        compiler_params=params(),
        cost_estimate=cost(2 * rows * width * cols, 2 * (width * cols + rows * cols)),
    )(x, w_qkv)


def half_of(pair, odd):
    lane = lax.broadcasted_iota(jnp.int32, pair.shape, 1)
    keep = lane >= pair.shape[1] // 2 if odd else lane < pair.shape[1] // 2
    return jnp.where(keep, pair, jnp.zeros_like(pair))


def masked_scores(raw, valid):
    place = lax.broadcasted_iota(jnp.int32, raw.shape, 0)
    return jnp.where(place < valid, raw, NEG)


def attend_kernel(
    scale, head_dim, valid_ref, q_ref, k_ref, v_ref, xp_ref, wk_ref, wv_ref, sel_ref,
    ctx_ref, ctxt_ref, kt_ref, vt_ref, lse_ref, xpt_ref, acc_ref,
):
    step = pl.program_id(0)
    heads = q_ref.shape[1] // head_dim
    pair = 2 * head_dim

    @pl.when(step == 0)
    def _():
        xpt_ref[...] = xp_ref[...].T

    xp = xp_ref[...]
    other = sel_ref[0:1, :] > 0.5
    keys = jnp.where(other, mm(xp, wk_ref[...]), k_ref[...].astype(F32)).astype(BF16)
    values = jnp.where(other, mm(xp, wv_ref[...]), v_ref[...].astype(F32)).astype(BF16)
    kt_ref[...] = keys
    vt_ref[...] = values
    turned = values.T
    coef = scale * LOG2E
    for h in range(heads):
        lo = (h // 2) * pair
        q = half_of(q_ref[:, lo : lo + pair], h % 2)
        raw = mm_nt(keys[:, lo : lo + pair], q)
        raw = masked_scores(raw, valid_ref[step * heads + h])
        top = jnp.max(raw, axis=0, keepdims=True)
        terms = jnp.exp2((raw - top) * coef)
        total = jnp.sum(terms, axis=0, keepdims=True)
        got = mm(turned[h * head_dim : (h + 1) * head_dim], terms.astype(BF16))
        acc_ref[h * head_dim : (h + 1) * head_dim] = got / total
        lse_ref[0, h : h + 1, :] = top * coef + jnp.log2(total)
    low = acc_ref[...].astype(BF16)
    ctxt_ref[...] = low
    ctx_ref[...] = low.T


def attend(valid, qkv, xp, w_qkv, sel, head_dim):
    rows, width = xp.shape
    steps = width // WIDE
    return pl.pallas_call(
        functools.partial(attend_kernel, 1.0 / math.sqrt(head_dim), head_dim),
        grid_spec=pltpu.PrefetchScalarGridSpec(
            num_scalar_prefetch=1,
            grid=(steps,),
            in_specs=[
                pl.BlockSpec((rows, WIDE), lambda j, _: (0, j)),
                pl.BlockSpec((rows, WIDE), lambda j, _: (0, steps + j)),
                pl.BlockSpec((rows, WIDE), lambda j, _: (0, 2 * steps + j)),
                whole(xp.shape),
                pl.BlockSpec((width, WIDE), lambda j, _: (0, steps + j)),
                pl.BlockSpec((width, WIDE), lambda j, _: (0, 2 * steps + j)),
                pl.BlockSpec((8, WIDE), lambda j, _: (0, j)),
            ],
            out_specs=[
                pl.BlockSpec((rows, WIDE), lambda j, _: (0, j)),
                pl.BlockSpec((WIDE, rows), lambda j, _: (j, 0)),
                pl.BlockSpec((rows, WIDE), lambda j, _: (0, j)),
                pl.BlockSpec((rows, WIDE), lambda j, _: (0, j)),
                pl.BlockSpec((1, 8, rows), lambda j, _: (j, 0, 0)),
                whole((width, rows)),
            ],
            scratch_shapes=[pltpu.VMEM((WIDE, rows), F32)],
        ),
        out_shape=[
            shape_of((rows, width), BF16),
            shape_of((width, rows), BF16),
            shape_of((rows, width), BF16),
            shape_of((rows, width), BF16),
            shape_of((steps, 8, rows), F32),
            shape_of((width, rows), BF16),
        ],
        compiler_params=params(),
        cost_estimate=cost(
            4 * rows * width * (width + rows), 2 * (2 * width * width + 7 * rows * width)
        ),
    )(valid, qkv, qkv, qkv, xp, w_qkv, w_qkv, sel)


def norm_stats(hidden):
    mean = jnp.mean(hidden, axis=-1, keepdims=True)
    centred = hidden - mean
    var = jnp.mean(centred * centred, axis=-1, keepdims=True)
    inv = lax.rsqrt(var + EPS)
    return centred * inv, inv


def norm_back(grad, gain, hat, inv):
    scaled = grad * gain
    shift = jnp.mean(scaled, axis=-1, keepdims=True)
    slope = jnp.mean(scaled * hat, axis=-1, keepdims=True)
    back = inv * (scaled - shift - hat * slope)
    return back, jnp.sum(grad * hat, axis=0, keepdims=True), jnp.sum(grad, axis=0, keepdims=True)


class Places:
    def __init__(self, blks, lines):
        self.blks, self.lines = blks, lines


def send_out(both_ref, sems, keep_ref, send_ref):
    return (
        pltpu.make_async_copy(both_ref.at[0], keep_ref, sems.at[0]),
        pltpu.make_async_copy(both_ref.at[1], send_ref, sems.at[1]),
    )


def ffn_kernel(
    blks, lines, where_ref, x_ref, ctx_ref, wo_ref, vec_ref, dout_ref, wu_ref, wd_ref,
    hid_ref, slope_ref, dtwo_ref, upt_ref, resid_ref, gains_ref, *rest,
):
    outs = rest[:2] if lines else rest[:1]
    one_ref, up_ref, acc_ref, act_ref = rest[len(outs) : len(outs) + 4]
    step = pl.program_id(0)
    width = wu_ref.shape[1]

    @pl.when(step == 0)
    def _():
        resid = x_ref[...].astype(F32) + mm(ctx_ref[...], wo_ref[...])
        resid_ref[...] = resid
        hat, _ = norm_stats(resid)
        one = hat * vec_ref[0:1, :] + vec_ref[1:2, :]
        one_ref[...] = one
        low = one.astype(BF16)
        up_ref[...] = low
        upt_ref[...] = low.T
        acc_ref[...] = jnp.zeros_like(acc_ref)

    pre = mm(up_ref[...], wu_ref[...])
    cdf = 0.5 + 0.5 * lax.erf(pre * math.sqrt(0.5))
    pdf = jnp.exp2(pre * pre * (-0.5 * LOG2E)) * (1.0 / math.sqrt(2.0 * math.pi))
    slope_ref[...] = (cdf + pre * pdf).astype(BF16)
    act = (pre * cdf).astype(BF16)
    act_ref[:, pl.ds(pl.multiple_of(step * width, 128), width)] = act
    acc_ref[...] += mm(act, wd_ref[...])

    @pl.when(step == pl.num_programs(0) - 1)
    def _():
        hat, inv = norm_stats(one_ref[...] + acc_ref[...])
        hid_ref[...] = (hat * vec_ref[2:3, :] + vec_ref[3:4, :]).astype(BF16)
        back, gain, bias = norm_back(dout_ref[...].astype(F32), vec_ref[2:3, :], hat, inv)
        dtwo_ref[...] = back
        gains_ref[0:1, :] = gain
        gains_ref[1:2, :] = bias
        turned = back.astype(BF16).T
        if lines:
            both_ref, sems = rest[len(outs) + 4 :]
            me, core = where_ref[0], where_ref[1]
            high = turned.shape[0] // blks
            span = act_ref.shape[1] // (2 * lines)
            copies = send_out(both_ref, sems, *outs)
            for which in (1, 0):
                for z in range(lines):
                    start = (2 * z + (core ^ which)) * span
                    piece = act_ref[:, pl.ds(pl.multiple_of(start, 128), span)]
                    prod = mm(turned, piece).astype(BF16)
                    for k in range(blks):
                        both_ref[which, k ^ me, :, z * span : (z + 1) * span] = prod[
                            k * high : (k + 1) * high
                        ]
                copies[which].start()
            copies[1].wait()
            copies[0].wait()
        else:
            outs[0][...] = mm(turned, act_ref[...]).astype(BF16)


def ffn(where, x, ctx, w_out, vec, dout, w_up, w_down, blks, lines):
    rows, width = x.shape
    inner = w_up.shape[1]
    blk = inner // FF_BLOCKS
    out_shape = [
        shape_of((rows, width), BF16),
        shape_of((rows, inner), BF16),
        shape_of((rows, width), F32),
        shape_of((width, rows), BF16),
        shape_of((rows, width), F32),
        shape_of((8, width), F32),
    ]
    out_specs = [
        whole((rows, width)),
        pl.BlockSpec((rows, blk), lambda j, _: (0, j)),
        whole((rows, width)),
        whole((width, rows)),
        whole((rows, width)),
        whole((8, width)),
    ]
    scratch = [
        pltpu.VMEM((rows, width), F32),
        pltpu.VMEM((rows, width), BF16),
        pltpu.VMEM((rows, width), F32),
        pltpu.VMEM((rows, inner), BF16),
    ]
    if lines:
        part = (blks, width // blks, inner // 2)
        out_shape += [shape_of(part, BF16)] * 2
        out_specs += [pl.BlockSpec(memory_space=pl.ANY)] * 2
        scratch += [pltpu.VMEM((2,) + part, BF16), pltpu.SemaphoreType.DMA((2,))]
    else:
        out_shape += [shape_of((width, inner), BF16)]
        out_specs += [whole((width, inner))]
    return pl.pallas_call(
        functools.partial(ffn_kernel, blks, lines),
        grid_spec=pltpu.PrefetchScalarGridSpec(
            num_scalar_prefetch=1,
            grid=(FF_BLOCKS,),
            in_specs=[
                whole(x.shape),
                whole(ctx.shape),
                whole(w_out.shape),
                whole(vec.shape),
                whole(dout.shape),
                pl.BlockSpec((width, blk), lambda j, _: (0, j)),
                pl.BlockSpec((blk, width), lambda j, _: (j, 0)),
            ],
            out_specs=out_specs,
            scratch_shapes=scratch,
        ),
        out_shape=out_shape,
        compiler_params=params(),
        cost_estimate=cost(
            2 * rows * width * (3 * inner + width), 8 * width * inner + 14 * rows * width
        ),
    )(where, x, ctx, w_out, vec, dout, w_up, w_down)


def ffn_back_kernel(
    blks, lines, where_ref, dtwo_ref, slope_ref, wd_ref, wu_ref, upt_ref, resid_ref, vec_ref,
    gains_ref, wo_ref, ctxt_ref, dres_ref, dctx_ref, *rest,
):
    outs = rest[:2] if lines else rest[:3]
    low_ref, acc_ref = rest[len(outs) : len(outs) + 2]
    step = pl.program_id(0)
    blk = wu_ref.shape[1]
    if lines:
        both_ref, sems = rest[len(outs) + 2 :]
        me, core = where_ref[0], where_ref[1]
        high = upt_ref.shape[0] // (2 * lines)
        per = pl.num_programs(0) // blks

        def place(prod, k, at, span):
            for z in range(lines):
                for p in range(2):
                    row = (2 * z + p) * high
                    both_ref[p ^ core, k ^ me, z * high : (z + 1) * high, pl.ds(at, span)] = prod[
                        row : row + high
                    ]

    @pl.when(step == 0)
    def _():
        low_ref[...] = dtwo_ref[...].astype(BF16)
        acc_ref[...] = dtwo_ref[...]

    dpre = (mm_nt(low_ref[...], wd_ref[...]) * slope_ref[...].astype(F32)).astype(BF16)
    acc_ref[...] += mm_nt(dpre, wu_ref[...])
    prod = mm(upt_ref[...], dpre).astype(BF16)
    if lines:
        place(prod, step // per, pl.multiple_of((step % per) * blk, 128), blk)
    else:
        outs[0][:, pl.ds(pl.multiple_of(step * blk, 128), blk)] = prod

    @pl.when(step == pl.num_programs(0) - 1)
    def _():
        hat, inv = norm_stats(resid_ref[...])
        back, gain, bias = norm_back(acc_ref[...], vec_ref[0:1, :], hat, inv)
        dres_ref[...] = back
        low = back.astype(BF16)
        dctx_ref[...] = mm_nt(low, wo_ref[...]).astype(BF16)
        prod = mm(ctxt_ref[...], low).astype(BF16)
        row = lax.broadcasted_iota(jnp.int32, (128, gain.shape[1]), 0)
        sums = jnp.where(row == 0, gain, jnp.where(row == 1, bias, 0.0))
        sums = jnp.where(row == 2, gains_ref[0:1, :], sums)
        sums = jnp.where(row == 3, gains_ref[1:2, :], sums).T.astype(BF16)
        if lines:
            span = prod.shape[1] // blks
            tail = both_ref.shape[3] - per * blk - span
            for k in range(blks):
                place(prod[:, k * span : (k + 1) * span], k, per * blk, span)
                place(sums[:, :tail], k, per * blk + span, tail)
            copies = send_out(both_ref, sems, *outs)
            copies[1].start()
            copies[0].start()
            copies[1].wait()
            copies[0].wait()
        else:
            outs[1][...] = prod
            outs[2][...] = sums


def ffn_back(where, dtwo, slope, w_down, w_up, upt, resid, vec, gains, w_out, ctxt, blks, lines):
    rows, width = dtwo.shape
    inner = w_up.shape[1]
    blk = inner // FF_BLOCKS
    out_shape = [shape_of((rows, width), F32), shape_of((rows, width), BF16)]
    out_specs = [whole((rows, width)), whole((rows, width))]
    scratch = [pltpu.VMEM((rows, width), BF16), pltpu.VMEM((rows, width), F32)]
    if lines:
        used = (inner + width) // blks + 4
        part = (blks, width // 2, -(-used // 128) * 128)
        out_shape += [shape_of(part, BF16)] * 2
        out_specs += [pl.BlockSpec(memory_space=pl.ANY)] * 2
        scratch += [pltpu.VMEM((2,) + part, BF16), pltpu.SemaphoreType.DMA((2,))]
    else:
        for shape in ((width, inner), (width, width), (width, 128)):
            out_shape += [shape_of(shape, BF16)]
            out_specs += [whole(shape)]
    return pl.pallas_call(
        functools.partial(ffn_back_kernel, blks, lines),
        grid_spec=pltpu.PrefetchScalarGridSpec(
            num_scalar_prefetch=1,
            grid=(FF_BLOCKS,),
            in_specs=[
                whole(dtwo.shape),
                pl.BlockSpec((rows, blk), lambda j, _: (0, j)),
                pl.BlockSpec((blk, width), lambda j, _: (j, 0)),
                pl.BlockSpec((width, blk), lambda j, _: (0, j)),
                whole(upt.shape),
                whole(resid.shape),
                whole(vec.shape),
                whole(gains.shape),
                whole(w_out.shape),
                whole(ctxt.shape),
            ],
            out_specs=out_specs,
            scratch_shapes=scratch,
        ),
        out_shape=out_shape,
        compiler_params=params(),
        cost_estimate=cost(
            2 * rows * width * (3 * inner + 2 * width), 8 * width * inner + 14 * rows * width
        ),
    )(where, dtwo, slope, w_down, w_up, upt, resid, vec, gains, w_out, ctxt)


def attend_back_kernel(
    scale, head_dim, blks, lines, where_ref, valid_ref, q_ref, k_ref, v_ref, dctx_ref, lse_ref,
    sel_ref, wq_ref, wk_ref, wv_ref, xt_ref, xpt_ref, dres_ref, own_ref, give_ref, *rest,
):
    outs = rest[:2] if lines else rest[:1]
    dqt_ref, send_ref, gw_ref = rest[len(outs) : len(outs) + 3]
    step = pl.program_id(0)
    steps = pl.num_programs(0)
    heads = q_ref.shape[1] // head_dim
    pair = 2 * head_dim
    width = xt_ref.shape[0]
    coef = scale * LOG2E

    @pl.when(step == 0)
    def _():
        own_ref[...] = dres_ref[...]
        send_ref[...] = jnp.zeros_like(send_ref)

    keys = k_ref[...]
    kturned = keys.T
    dks, dvs = [], []
    for h in range(heads):
        lo = (h // 2) * pair
        q = half_of(q_ref[:, lo : lo + pair], h % 2)
        dctx = half_of(dctx_ref[:, lo : lo + pair], h % 2)
        raw = mm_nt(keys[:, lo : lo + pair], q)
        raw = masked_scores(raw, valid_ref[step * heads + h])
        probs = jnp.exp2(raw * coef - lse_ref[0, h : h + 1, :])
        dprobs = mm_nt(v_ref[:, lo : lo + pair], dctx)
        dv = mm(probs.astype(BF16), dctx)
        delta = jnp.sum(probs * dprobs, axis=0, keepdims=True)
        draw = (probs * (dprobs - delta)).astype(BF16)
        dk = mm(draw, q)
        dqt_ref[h * head_dim : (h + 1) * head_dim] = mm(
            kturned[h * head_dim : (h + 1) * head_dim], draw
        )
        if h % 2 == 0:
            dks.append(dk)
            dvs.append(dv)
        else:
            dks[-1] = dks[-1] + dk
            dvs[-1] = dvs[-1] + dv
    dq = (dqt_ref[...] * scale).astype(BF16).T
    dk = (jnp.concatenate(dks, axis=1) * scale).astype(BF16)
    dv = jnp.concatenate(dvs, axis=1).astype(BF16)
    other = sel_ref[0:1, :] > 0.5
    away = jnp.broadcast_to(other, dk.shape)
    zero = jnp.zeros_like(dk)
    own = mm_nt(dq, wq_ref[...])
    own += mm_nt(jnp.where(away, zero, dk), wk_ref[...])
    own += mm_nt(jnp.where(away, zero, dv), wv_ref[...])
    own_ref[...] += own
    give = mm_nt(jnp.where(away, dk, zero), wk_ref[...])
    give += mm_nt(jnp.where(away, dv, zero), wv_ref[...])
    send_ref[...] += give
    for part, grad in enumerate((dq, dk, dv)):
        prod = mm(xt_ref[...], grad)
        if part > 0:
            prod = jnp.where(other, mm(xpt_ref[...], grad), prod)
        at = pl.multiple_of(part * width + step * WIDE, 128)
        gw_ref[:, pl.ds(at, WIDE)] = prod.astype(BF16)

    @pl.when(step == steps - 1)
    def _():
        give_ref[...] = send_ref[...].astype(BF16)
        if lines:
            both_ref, sems = rest[len(outs) + 3 :]
            me, core = where_ref[0], where_ref[1]
            high = width // (2 * lines)
            span = gw_ref.shape[1] // blks
            copies = send_out(both_ref, sems, *outs)
            for which in (1, 0):
                for z in range(lines):
                    row = pl.multiple_of((2 * z + (core ^ which)) * high, 16)
                    for k in range(blks):
                        both_ref[which, k ^ me, z * high : (z + 1) * high, 0:span] = gw_ref[
                            pl.ds(row, high), k * span : (k + 1) * span
                        ]
                copies[which].start()
            copies[1].wait()
            copies[0].wait()
        else:
            outs[0][...] = gw_ref[...]


def attend_back(
    where, valid, qkv, keys, values, dctx, lse, sel, w_qkv, xt, xpt, dres, head_dim, blks, lines
):
    rows, width = dres.shape
    cols = w_qkv.shape[1]
    steps = width // WIDE
    out_shape = [shape_of((rows, width), F32), shape_of((rows, width), BF16)]
    out_specs = [whole((rows, width)), whole((rows, width))]
    scratch = [
        pltpu.VMEM((WIDE, rows), F32),
        pltpu.VMEM((rows, width), F32),
        pltpu.VMEM((width, cols), BF16),
    ]
    if lines:
        part = (blks, width // 2, -(-(cols // blks) // 128) * 128)
        out_shape += [shape_of(part, BF16)] * 2
        out_specs += [pl.BlockSpec(memory_space=pl.ANY)] * 2
        scratch += [pltpu.VMEM((2,) + part, BF16), pltpu.SemaphoreType.DMA((2,))]
    else:
        out_shape += [shape_of((width, cols), BF16)]
        out_specs += [whole((width, cols))]
    col = lambda first: pl.BlockSpec((rows, WIDE), lambda j, *_: (0, first + j))
    wcol = lambda first: pl.BlockSpec((width, WIDE), lambda j, *_: (0, first + j))
    return pl.pallas_call(
        functools.partial(attend_back_kernel, 1.0 / math.sqrt(head_dim), head_dim, blks, lines),
        grid_spec=pltpu.PrefetchScalarGridSpec(
            num_scalar_prefetch=2,
            grid=(steps,),
            in_specs=[
                col(0),
                col(0),
                col(0),
                col(0),
                pl.BlockSpec((1, 8, rows), lambda j, *_: (j, 0, 0)),
                pl.BlockSpec((8, WIDE), lambda j, *_: (0, j)),
                wcol(0),
                wcol(steps),
                wcol(2 * steps),
                whole(xt.shape),
                whole(xpt.shape),
                whole(dres.shape),
            ],
            out_specs=out_specs,
            scratch_shapes=scratch,
        ),
        out_shape=out_shape,
        compiler_params=params(),
        cost_estimate=cost(
            2 * rows * width * (10 * width + 5 * rows), 2 * (6 * width * width + 12 * rows * width)
        ),
    )(where, valid, qkv, keys, values, dctx, lse, sel, w_qkv, w_qkv, w_qkv, xt, xpt, dres)


def add_up(*parts):
    total = parts[0].astype(F32)
    for part in parts[1:]:
        total = total + part.astype(F32)
    return total


def core_sum_kernel(keep_ref, got_ref, *outs):
    for i, out in enumerate(outs):
        out[...] = add_up(keep_ref[i], got_ref[i]).astype(BF16)


def core_sum(keep, got):
    blks, rows, cols = keep.shape
    blk = rows // 4
    return pl.pallas_call(
        core_sum_kernel,
        grid=(rows // blk,),
        in_specs=[pl.BlockSpec((blks, blk, cols), lambda j: (0, j, 0))] * 2,
        out_specs=[pl.BlockSpec((blk, cols), lambda j: (j, 0))] * blks,
        out_shape=[shape_of((rows, cols), BF16)] * blks,
        compiler_params=params(),
        cost_estimate=cost(keep.size, 6 * keep.size),
    )(keep, got)


def line_sum_kernel(along, where_ref, *refs):
    ins, outs = refs[: len(refs) // 2], refs[len(refs) // 2 :]
    size = outs[0].shape[along]
    for i, out in enumerate(outs):
        at = pl.ds(pl.multiple_of((where_ref[2] ^ i) * size, 128 if along else 16), size)
        out[...] = add_up(*(ref[:, at] if along else ref[at] for ref in ins)).astype(BF16)


def line_sum(where, parts, along, lines):
    shape = list(parts[0].shape)
    shape[along] //= lines
    return pl.pallas_call(
        functools.partial(line_sum_kernel, along),
        in_specs=[pl.BlockSpec(memory_space=pltpu.SMEM)]
        + [pl.BlockSpec(memory_space=pltpu.VMEM)] * len(parts),
        out_specs=[pl.BlockSpec(memory_space=pltpu.VMEM)] * lines,
        out_shape=[shape_of(tuple(shape), BF16)] * lines,
        compiler_params=params(),
        cost_estimate=cost(4 * parts[0].size, 10 * parts[0].size),
    )(where, *parts)


def reduce_fast(where, keep, send, along, lines):
    chip = core_sum(keep, swap(send, "batch", 1))
    blk = [chip[0]] + [swap(chip[i], "blk", i) for i in range(1, len(chip))]
    mine = line_sum(where, blk, along, lines)
    return add_up(mine[0], *(swap(mine[i], "batch", 2 * i) for i in range(1, lines)))


def reduce_any(mats, thin=None):
    blks = lax.axis_size("blk")
    lines = lax.axis_size("batch") // 2
    me = lax.axis_index("blk")
    core = lax.axis_index("batch") % 2
    line = lax.axis_index("batch") // 2
    pieces = []
    for mat in mats:
        rows = mat.shape[0] // (2 * lines)
        pieces.append(mat.reshape(lines, 2, rows, blks, -1))
    if thin is not None:
        thin = thin.reshape(lines, 2, rows, 1, -1)
        pieces.append(jnp.broadcast_to(thin, thin.shape[:3] + (blks,) + thin.shape[4:]))
    every = jnp.concatenate(pieces, axis=4)

    def half(which, distance):
        part = lax.dynamic_index_in_dim(every, which, 1, keepdims=False)
        return lax.dynamic_index_in_dim(part, me ^ distance, 2, keepdims=False)

    keep = [half(core, distance) for distance in range(blks)]
    got = swap(jnp.stack([half(1 - core, i) for i in range(blks)]), "batch", 1)
    chip = [add_up(part, got[i]).astype(BF16) for i, part in enumerate(keep)]
    total = add_up(chip[0], *(swap(chip[i], "blk", i) for i in range(1, blks)))
    while lines > 1:
        lines //= 2
        upper = line // lines
        pairs = total.astype(BF16).reshape((2, lines) + total.shape[1:])
        mine = lax.dynamic_index_in_dim(pairs, upper, 0, keepdims=False)
        theirs = lax.dynamic_index_in_dim(pairs, 1 - upper, 0, keepdims=False)
        total = add_up(mine, swap(theirs, "batch", 2 * lines))
        line = line % lines
    return total[0]


def shards(
    hidden_in, lengths, head_order, w_qkv, w_out, ln1_gain, ln1_bias, w_up, w_down, ln2_gain,
    ln2_bias, grad_out,
):
    _, _, rows, width = hidden_in.shape
    heads = head_order.shape[0]
    head_dim = width // heads
    blks = lax.axis_size("blk")
    batch = lax.axis_size("batch")
    inner = w_up.shape[1]
    me = lax.axis_index("blk")
    at = lax.axis_index("batch")
    fast = 2 * 4 == batch and blks == 4 and width % (16 * batch) == 0
    lines = batch // 2 if fast else 0

    x = hidden_in.reshape(rows, width)
    dout = grad_out.reshape(rows, width)
    xp = swap(x, "blk", 1)
    where = jnp.stack([me, at % 2, at // 2]).astype(jnp.int32)
    swapped = head_order >= heads // 2
    target = jnp.where(swapped, 1 - me % 2, me % 2)
    length = lax.dynamic_index_in_dim(lengths[:, 0], me // 2, 0, keepdims=False)
    valid = (length - rows * target).astype(jnp.int32)
    sel = jnp.broadcast_to(jnp.repeat(swapped.astype(F32), head_dim)[None, :], (8, width))
    vec = jnp.stack([ln1_gain, ln1_bias, ln2_gain, ln2_bias] * 2)

    qkv, xt = project(x, w_qkv)
    ctx, ctxt, keys, values, lse, xpt = attend(valid, qkv, xp, w_qkv, sel, head_dim)
    hid, slope, dtwo, upt, resid, gains, *down = ffn(
        where, x, ctx, w_out, vec, dout, w_up, w_down, blks, lines
    )
    dres, dctx, *up = ffn_back(
        where, dtwo, slope, w_down, w_up, upt, resid, vec, gains, w_out, ctxt, blks, lines
    )
    own, give, *proj = attend_back(
        where, valid, qkv, keys, values, dctx, lse, sel, w_qkv, xt, xpt, dres, head_dim, blks, lines
    )
    got = swap(give, "blk", 1)
    grad_in = (own + got.astype(F32)).astype(BF16)
    up_cols, out_cols, qkv_cols = (n // blks for n in (inner, width, w_qkv.shape[1]))
    if fast:
        own_down = reduce_fast(where, *down, 1, lines).T
        own_up = reduce_fast(where, *up, 0, lines)
        own_qkv = reduce_fast(where, *proj, 0, lines)
    else:
        own_down = reduce_any([down[0].T])
        own_up = reduce_any(up[:2], up[2][:, :4])
        own_qkv = reduce_any(proj)
    sums = own_up[:, up_cols + out_cols :]
    return (
        hid.reshape(hidden_in.shape),
        grad_in.reshape(hidden_in.shape),
        own_qkv[:, :qkv_cols],
        own_up[:, up_cols : up_cols + out_cols],
        sums[:, 0],
        sums[:, 1],
        own_up[:, :up_cols],
        own_down,
        sums[:, 2],
        sums[:, 3],
    )


def solution(mesh):
    rows = P("blk", "batch", None, None)
    both = P("batch", "blk")
    return jax.shard_map(
        shards,
        mesh=mesh,
        in_specs=(rows, P(None, "batch")) + (P(),) * 9 + (rows,),
        out_specs=(rows, rows, both, both, P("batch"), P("batch"), both, both)
        + (P("batch"), P("batch")),
        check_vma=False,
    )
```

```python
import functools
import math

import jax
import jax.numpy as jnp
from jax import lax
from jax.experimental import pallas as pl
from jax.experimental.pallas import tpu as pltpu
from jax.sharding import PartitionSpec as P

F32 = jnp.float32
BF16 = jnp.bfloat16
MIB = 1 << 20
EPS = 1e-06
NEG = -1e30
LOG2E = math.log2(math.e)
FF_BLOCKS = 4
ME, CORE, LINE, NEAR, FAR, ORDER = range(6)


def swap(block, axis, bits):
    return lax.ppermute(block, axis, [(i, i ^ bits) for i in range(lax.axis_size(axis))])


def nn(a, b):
    return lax.dot_general(a, b, (((1,), (0,)), ((), ())), preferred_element_type=F32)


def nt(a, b):
    return lax.dot_general(a, b, (((1,), (1,)), ((), ())), preferred_element_type=F32)


def tn(a, b):
    return lax.dot_general(a, b, (((0,), (0,)), ((), ())), preferred_element_type=F32)


def call(kernel, scalars, ins, outs, scratch=(), mib=16, us=5):
    vmem = pl.BlockSpec(memory_space=pltpu.VMEM)
    return pl.pallas_call(
        kernel,
        in_specs=[pl.BlockSpec(memory_space=pltpu.SMEM)] + [vmem] * len(ins),
        out_specs=[vmem] * len(outs),
        out_shape=[jax.ShapeDtypeStruct(shape, dtype) for shape, dtype in outs],
        scratch_shapes=[pltpu.VMEM(shape, dtype) for shape, dtype in scratch],
        compiler_params=pltpu.CompilerParams(vmem_limit_bytes=mib * MIB),
        cost_estimate=pl.CostEstimate(
            flops=us * 1150000000, bytes_accessed=us * 1000000, transcendentals=0
        ),
    )(scalars, *ins)


def rows_of(index, size):
    return pl.ds(pl.multiple_of(index * size, size), size)


def stacked(first, *rows):
    spare = lax.broadcasted_iota(jnp.int32, (16, first.shape[1]), 0)
    extra = jnp.zeros(spare.shape, F32)
    for i, row in enumerate(rows):
        extra = jnp.where(spare == i, row, extra)
    return jnp.concatenate([first, extra.astype(BF16)], axis=0)


def key_bias(valid, keys):
    place = lax.broadcasted_iota(jnp.int32, (1, keys), 1)
    return jnp.where(place < valid, 0.0, NEG)


def attend_head(coef, q, k, v, bias):
    dim = q.shape[0]
    raw = nn(stacked(k, bias).T, stacked(q, 1.0))
    top = jnp.max(raw, axis=0, keepdims=True)
    terms = jnp.exp2((raw - top) * coef).astype(BF16)
    got = nn(stacked(v, 1.0), terms)
    total = got[dim : dim + 1]
    return (got[:dim] / total).astype(BF16), top * coef + jnp.log2(total)


def attend_head_back(coef, scale, q, k, v, bias, lse, ctx, dctx):
    delta = jnp.sum(dctx.astype(F32) * ctx.astype(F32), axis=0, keepdims=True)
    raw = nn(stacked(k, bias).T, stacked(q, 1.0))
    probs = jnp.exp2(raw * coef - lse)
    draw = (probs * (nn(v.T, dctx) - delta)).astype(BF16)
    dv = nt(dctx, probs.astype(BF16)).astype(BF16)
    dk = (nt(q, draw) * scale).astype(BF16)
    dq = (nn(k, draw) * scale).astype(BF16)
    return dq, dk, dv


def norm_stats(hidden):
    mean = jnp.mean(hidden, axis=-1, keepdims=True)
    centred = hidden - mean
    var = jnp.mean(centred * centred, axis=-1, keepdims=True)
    inv = lax.rsqrt(var + EPS)
    return centred * inv, inv


def norm_back(grad, gain, hat, inv):
    scaled = grad * gain
    shift = jnp.mean(scaled, axis=-1, keepdims=True)
    slope = jnp.mean(scaled * hat, axis=-1, keepdims=True)
    back = inv * (scaled - shift - hat * slope)
    return back, jnp.sum(grad * hat, axis=0, keepdims=True), jnp.sum(grad, axis=0, keepdims=True)


def by_core(mat, core, lines):
    span = mat.shape[1] // (2 * lines)
    halves = [
        jnp.concatenate(
            [mat[:, (2 * z + p) * span : (2 * z + p + 1) * span] for z in range(lines)], axis=1
        )
        for p in range(2)
    ]
    even = core == 0
    return jnp.where(even, halves[0], halves[1]), jnp.where(even, halves[1], halves[0])


def rows_by_core(ref, core, lines):
    span = ref.shape[0] // (2 * lines)
    return [
        jnp.concatenate([ref[rows_of(2 * z + (core ^ which), span), :] for z in range(lines)], axis=0)
        for which in range(2)
    ]


def near_kernel(heads, lines, s_ref, x_ref, w_ref, qkv_ref, ctx_ref, lse_ref, *rest):
    width = x_ref.shape[1]
    dim = width // heads
    coef = LOG2E / math.sqrt(dim)
    turned = x_ref[...].T
    for part in range(3):
        at = slice(part * width, (part + 1) * width)
        qkv_ref[at, :] = tn(w_ref[:, at], turned).astype(BF16)
    if lines:
        rest[0][0], rest[0][1] = by_core(x_ref[...], s_ref[CORE], lines)
    bias = key_bias(s_ref[NEAR], x_ref.shape[0])

    def one(i, carry):
        head = s_ref[ORDER + i]
        at = rows_of(head, dim)
        ctx_ref[at, :], lse_ref[head] = attend_head(
            coef,
            qkv_ref[at, :],
            qkv_ref[rows_of(heads + head, dim), :],
            qkv_ref[rows_of(2 * heads + head, dim), :],
            bias,
        )
        return carry

    lax.fori_loop(0, heads // 2, one, 0, unroll=3)


def ffn_kernel(
    heads, blks, lines, s_ref, x_ref, xp_ref, w_ref, qkv_ref, near_ref, wo_ref, gain1_ref,
    bias1_ref, gain2_ref, bias2_ref, dout_ref, wu_ref, wd_ref,
    kv_ref, ctx_ref, lse_ref, hid_ref, slope_ref, dtwo_ref, upt_ref, resid_ref, gains_ref, *rest,
):
    act_ref = rest[-1]
    rows, width = x_ref.shape
    dim = width // heads
    coef = LOG2E / math.sqrt(dim)
    me, core = s_ref[ME], s_ref[CORE]
    turned = xp_ref[...].T
    for part in range(2):
        at = slice((part + 1) * width, (part + 2) * width)
        kv_ref[part * width : (part + 1) * width, :] = tn(w_ref[:, at], turned).astype(BF16)
    bias = key_bias(s_ref[FAR], rows)

    def one(i, carry):
        head = s_ref[ORDER + heads // 2 + i]
        at = rows_of(head, dim)
        ctx_ref[at, :], lse_ref[head] = attend_head(
            coef, qkv_ref[at, :], kv_ref[at, :], kv_ref[rows_of(heads + head, dim), :], bias
        )
        mine = rows_of(s_ref[ORDER + i], dim)
        ctx_ref[mine, :] = near_ref[mine, :]
        return carry

    lax.fori_loop(0, heads // 2, one, 0, unroll=3)

    resid = x_ref[...].astype(F32) + tn(ctx_ref[...], wo_ref[...])
    resid_ref[...] = resid
    hat, _ = norm_stats(resid)
    one_in = hat * gain1_ref[...] + bias1_ref[...]
    low = one_in.astype(BF16)
    upt_ref[...] = low.T
    total = one_in
    blk = wu_ref.shape[1] // FF_BLOCKS
    for j in range(FF_BLOCKS):
        at = slice(j * blk, (j + 1) * blk)
        pre = nn(low, wu_ref[:, at])
        cdf = 0.5 + 0.5 * lax.erf(pre * math.sqrt(0.5))
        pdf = jnp.exp2(pre * pre * (-0.5 * LOG2E)) * (1.0 / math.sqrt(2.0 * math.pi))
        slope_ref[:, at] = (cdf + pre * pdf).astype(BF16)
        act = (pre * cdf).astype(BF16)
        act_ref[:, at] = act
        total = total + nn(act, wd_ref[at, :])
    hat, inv = norm_stats(total)
    hid_ref[...] = (hat * gain2_ref[...] + bias2_ref[...]).astype(BF16)
    back, gain, shift = norm_back(dout_ref[...].astype(F32), gain2_ref[...], hat, inv)
    dtwo_ref[...] = back
    gains_ref[0:1, :] = gain
    gains_ref[1:2, :] = shift
    turned = back.astype(BF16).T
    if lines:
        high = width // blks
        span = act_ref.shape[1] // (2 * lines)
        for which in (1, 0):
            for z in range(lines):
                prod = nn(turned, act_ref[:, rows_of(2 * z + (core ^ which), span)]).astype(BF16)
                for k in range(blks):
                    rest[which][k ^ me, :, z * span : (z + 1) * span] = prod[
                        k * high : (k + 1) * high
                    ]
        rest[2][0], rest[2][1] = by_core(xp_ref[...], core, lines)
    else:
        rest[0][...] = nn(turned, act_ref[...]).astype(BF16)


def pre_back_kernel(s_ref, dtwo_ref, slope_ref, wd_ref, wu_ref, dpre_ref, done_ref):
    low = dtwo_ref[...].astype(BF16)
    total = dtwo_ref[...]
    blk = wu_ref.shape[1] // FF_BLOCKS
    for j in range(FF_BLOCKS):
        at = slice(j * blk, (j + 1) * blk)
        dpre = (nt(low, wd_ref[at, :]) * slope_ref[:, at].astype(F32)).astype(BF16)
        dpre_ref[:, at] = dpre
        total = total + nt(dpre, wu_ref[:, at])
    done_ref[...] = total


def norm_back_kernel(
    blks, lines, s_ref, dpre_ref, done_ref, upt_ref, resid_ref, gain1_ref, gains_ref, wo_ref,
    ctx_ref, dres_ref, dctx_ref, *outs,
):
    me, core = s_ref[ME], s_ref[CORE]
    hat, inv = norm_stats(resid_ref[...])
    back, gain, shift = norm_back(done_ref[...], gain1_ref[...], hat, inv)
    dres_ref[...] = back
    turned = back.astype(BF16).T
    dctx_ref[...] = nn(wo_ref[...], turned).astype(BF16)
    row = lax.broadcasted_iota(jnp.int32, (16, gain.shape[1]), 0)
    sums = jnp.where(row == 0, gain, jnp.where(row == 1, shift, 0.0))
    sums = jnp.where(row == 2, gains_ref[0:1, :], sums)
    sums = jnp.where(row == 3, gains_ref[1:2, :], sums).astype(BF16)
    if not lines:
        outs[0][...] = nn(upt_ref[...], dpre_ref[...]).astype(BF16)
        outs[1][...] = nt(turned, ctx_ref[...]).astype(BF16)
        outs[2][...] = sums
        return
    ups = rows_by_core(upt_ref, core, lines)
    ctxs = rows_by_core(ctx_ref, core, lines)
    sums = by_core(sums, core, lines)
    wide = dpre_ref.shape[1] // blks
    half = ups[0].shape[0]
    high = turned.shape[0] // blks
    pieces = wide // half
    for which in (1, 0):
        for k in range(blks):
            prod = nn(ups[which], dpre_ref[:, k * wide : (k + 1) * wide]).astype(BF16)
            for p in range(pieces):
                outs[which][k ^ me, p * half : (p + 1) * half, :] = prod[:, p * half : (p + 1) * half]
        prod = nt(turned, ctxs[which]).astype(BF16)
        for k in range(blks):
            outs[which][k ^ me, wide : wide + high, :] = prod[k * high : (k + 1) * high]
            outs[which][k ^ me, wide + high :, :] = sums[which]


def far_back_kernel(
    heads, s_ref, qkv_ref, kv_ref, ctx_ref, dctx_ref, lse_ref, w_ref, dq_ref, dkv_ref, give_ref,
    wide_ref,
):
    width, rows = ctx_ref.shape
    dim = width // heads
    half = heads // 2
    scale = 1.0 / math.sqrt(dim)
    bias = key_bias(s_ref[FAR], rows)
    wide_ref[...] = jnp.zeros_like(wide_ref)

    def one(i, carry):
        head = s_ref[ORDER + half + i]
        at, low = rows_of(head, dim), rows_of(heads + head, dim)
        dq, dk, dv = attend_head_back(
            LOG2E * scale, scale, qkv_ref[at, :], kv_ref[at, :], kv_ref[low, :], bias,
            lse_ref[head], ctx_ref[at, :], dctx_ref[at, :],
        )
        dq_ref[rows_of(i, dim), :] = dq
        dkv_ref[rows_of(i, dim), :] = dk
        dkv_ref[rows_of(half + i, dim), :] = dv
        wide_ref[at, :] = dk
        wide_ref[low, :] = dv
        return carry

    lax.fori_loop(0, half, one, 0, unroll=3)
    give_ref[...] = nn(w_ref[:, width:], wide_ref[...]).astype(BF16)


def near_back_kernel(
    heads, blks, lines, s_ref, qkv_ref, ctx_ref, dctx_ref, lse_ref, farq_ref, farkv_ref, x_ref,
    xp_ref, dqkv_ref, *rest,
):
    outs, near_ref = rest[:-1], rest[-1]
    width, rows = ctx_ref.shape
    dim = width // heads
    half = heads // 2
    scale = 1.0 / math.sqrt(dim)
    bias = key_bias(s_ref[NEAR], rows)
    me = s_ref[ME]
    dqkv_ref[width:, :] = jnp.zeros((2 * width, rows), BF16)

    def one(i, carry):
        head = s_ref[ORDER + i]
        at = rows_of(head, dim)
        key, value = rows_of(heads + head, dim), rows_of(2 * heads + head, dim)
        dq, dk, dv = attend_head_back(
            LOG2E * scale, scale, qkv_ref[at, :], qkv_ref[key, :], qkv_ref[value, :], bias,
            lse_ref[head], ctx_ref[at, :], dctx_ref[at, :],
        )
        dqkv_ref[at, :] = dq
        dqkv_ref[key, :] = dk
        dqkv_ref[value, :] = dv
        near_ref[rows_of(i, dim), :] = dk
        near_ref[rows_of(half + i, dim), :] = dv
        dqkv_ref[rows_of(s_ref[ORDER + half + i], dim), :] = farq_ref[rows_of(i, dim), :]
        return carry

    lax.fori_loop(0, half, one, 0, unroll=3)
    per = 3 * heads // blks

    def store(out, unit, prod):
        if lines:
            out[(unit // per) ^ me, rows_of(unit % per, dim), :] = prod
        else:
            out[rows_of(unit, dim), :] = prod

    for which in (1, 0) if lines else (0,):
        x = x_ref[which] if lines else x_ref[...]
        xp = xp_ref[which] if lines else xp_ref[...]
        prod = nn(dqkv_ref[:width, :], x).astype(BF16)
        for h in range(heads):
            store(outs[which], h, prod[h * dim : (h + 1) * dim])
        for first, grads, inputs in ((0, near_ref, x), (half, farkv_ref, xp)):
            prod = nn(grads[...], inputs).astype(BF16)
            for i in range(half):
                head = s_ref[ORDER + first + i]
                store(outs[which], heads + head, prod[i * dim : (i + 1) * dim])
                low = (half + i) * dim
                store(outs[which], 2 * heads + head, prod[low : low + dim])


def through_kernel(s_ref, w_ref, dqkv_ref, own_ref):
    own_ref[...] = nn(w_ref[...], dqkv_ref[...])


def input_kernel(s_ref, own_ref, got_ref, dres_ref, out_ref):
    total = own_ref[...] + got_ref[...].astype(F32)
    out_ref[...] = (total.T + dres_ref[...]).astype(BF16)


def add_up(*parts):
    total = parts[0].astype(F32)
    for part in parts[1:]:
        total = total + part.astype(F32)
    return total


def pair_kernel(groups, s_ref, keep_ref, got_ref, *outs):
    for group, out in zip(groups, outs):
        for slot, i in enumerate(group):
            out[slot] = add_up(keep_ref[i], got_ref[i]).astype(BF16)


def pair_sum(scalars, keep, got, groups):
    outs = [((len(group),) + keep.shape[1:], BF16) for group in groups]
    return call(functools.partial(pair_kernel, groups), scalars, (keep, got), outs, mib=4, us=2)


def lines_kernel(pieces, lines, s_ref, *refs):
    ins, outs = refs[:-lines], refs[-lines:]
    for place in range(lines):

        @pl.when(s_ref[LINE] == place)
        def _():
            for i, out in enumerate(outs):
                for src, dst in pieces(place ^ i):
                    out[dst] = add_up(*(ref[(0,) + src] for ref in ins)).astype(BF16)


def lines_sum(scalars, parts, shape, pieces, lines):
    return call(
        functools.partial(lines_kernel, pieces, lines), scalars, parts, [(shape, BF16)] * lines,
        mib=4, us=2,
    )


def over_lines(mine):
    return [mine[0]] + [swap(mine[i], "batch", 2 * i) for i in range(1, len(mine))]


def span_of(index, size):
    return slice(index * size, (index + 1) * size)


def down_pieces(size):
    return lambda z: [((slice(None), span_of(z, size)), (slice(None), slice(None)))]


def up_pieces(wide, half, lines):
    size = half // lines

    def pieces(z):
        found = []
        for p in range(wide // half):
            rows = slice(p * half + z * size, p * half + (z + 1) * size)
            found.append(((rows, slice(None)), (span_of(p, size), slice(0, half))))
        rest = (slice(wide, None), span_of(z, size))
        return found + [(rest, (slice(None), slice(half, half + size)))]

    return pieces


def down_final_kernel(s_ref, *refs):
    refs[-1][...] = add_up(*(ref[...] for ref in refs[:-1])).T


def up_final_kernel(high, half, size, s_ref, *refs):
    up_ref, out_ref, sums_ref = refs[-3:]
    total = add_up(*(ref[...] for ref in refs[:-3]))
    for p in range(high // size):
        up_ref[:, span_of(p, half)] = total[span_of(p, size), :half]
    out_ref[...] = total[:high, half : half + size].T
    sums_ref[...] = total[high : high + 8, half:]


def reduce_any(mats, thin=None):
    blks = lax.axis_size("blk")
    lines = lax.axis_size("batch") // 2
    me = lax.axis_index("blk")
    core = lax.axis_index("batch") % 2
    line = lax.axis_index("batch") // 2
    pieces = []
    for mat in mats:
        rows = mat.shape[0] // (2 * lines)
        pieces.append(mat.reshape(lines, 2, rows, blks, -1))
    if thin is not None:
        thin = thin.reshape(lines, 2, rows, 1, -1)
        pieces.append(jnp.broadcast_to(thin, thin.shape[:3] + (blks,) + thin.shape[4:]))
    every = jnp.concatenate(pieces, axis=4)

    def half(which, distance):
        part = lax.dynamic_index_in_dim(every, which, 1, keepdims=False)
        return lax.dynamic_index_in_dim(part, me ^ distance, 2, keepdims=False)

    keep = [half(core, distance) for distance in range(blks)]
    got = swap(jnp.stack([half(1 - core, i) for i in range(blks)]), "batch", 1)
    chip = [add_up(part, got[i]).astype(BF16) for i, part in enumerate(keep)]
    total = add_up(chip[0], *(swap(chip[i], "blk", i) for i in range(1, blks)))
    while lines > 1:
        lines //= 2
        upper = line // lines
        pairs = total.astype(BF16).reshape((2, lines) + total.shape[1:])
        mine = lax.dynamic_index_in_dim(pairs, upper, 0, keepdims=False)
        theirs = lax.dynamic_index_in_dim(pairs, 1 - upper, 0, keepdims=False)
        total = add_up(mine, swap(theirs, "batch", 2 * lines))
        line = line % lines
    return total[0]


def shards(
    hidden_in, lengths, head_order, w_qkv, w_out, ln1_gain, ln1_bias, w_up, w_down, ln2_gain,
    ln2_bias, grad_out,
):
    _, _, rows, width = hidden_in.shape
    heads = head_order.shape[0]
    blks = lax.axis_size("blk")
    batch = lax.axis_size("batch")
    inner = w_up.shape[1]
    me = lax.axis_index("blk")
    at = lax.axis_index("batch")
    fast = batch == 8 and blks == 4 and width % (16 * batch) == 0
    lines = batch // 2 if fast else 0
    wide = inner // blks
    high = width // blks
    cols = 3 * width // blks

    x = hidden_in.reshape(rows, width)
    dout = grad_out.reshape(rows, width)
    xp = swap(x, "blk", 1)
    gain1, bias1, gain2, bias2 = (
        part.reshape(1, width) for part in (ln1_gain, ln1_bias, ln2_gain, ln2_bias)
    )
    length = lax.dynamic_index_in_dim(lengths[:, 0], me // 2, 0, keepdims=False)
    ids = jnp.arange(heads, dtype=jnp.int32)
    order = jnp.sum(jnp.where(head_order[None, :] == ids[:, None], ids[None, :], 0), axis=1)
    parts = [me, at % 2, at // 2, length - rows * (me % 2), length - rows * (1 - me % 2)]
    s = jnp.concatenate([jnp.stack(parts).astype(jnp.int32), order.astype(jnp.int32)])

    square = ((width, rows), BF16)
    lse = ((heads, 1, rows), F32)
    split = [((2, rows, width // 2), BF16)] if lines else []
    qkv, near_ctx, near_lse, *x_parts = call(
        functools.partial(near_kernel, heads, lines), s, (x, w_qkv),
        [((3 * width, rows), BF16), square, lse] + split, mib=8, us=8,
    )

    if lines:
        down_out = [((blks, high, inner // 2), BF16)] * 2 + split
    else:
        down_out = [((width, inner), BF16)]
    kv, ctx, far_lse, hid, slope, dtwo, upt, resid, gains, *down = call(
        functools.partial(ffn_kernel, heads, blks, lines), s,
        (x, xp, w_qkv, qkv, near_ctx, w_out, gain1, bias1, gain2, bias2, dout, w_up, w_down),
        [((2 * width, rows), BF16), square, lse, ((rows, width), BF16), ((rows, inner), BF16),
         ((rows, width), F32), square, ((rows, width), F32), ((8, width), F32)] + down_out,
        [((rows, inner), BF16)], mib=16, us=24,
    )

    dpre, done = call(
        pre_back_kernel, s, (dtwo, slope, w_down, w_up),
        [((rows, inner), BF16), ((rows, width), F32)], mib=8, us=6,
    )

    if lines:
        got = swap(down[1], "batch", 1)
        low1, high1 = pair_sum(s, down[0], got, ((0, 1), (2, 3)))
        dpre, low1, high1 = lax.optimization_barrier((dpre, low1, high1))
        got1 = swap(high1, "blk", 2)
        up_out = [((blks, wide + high + 16, width // 2), BF16)] * 2
    else:
        up_out = [((width, inner), BF16), ((width, width), BF16), ((16, width), BF16)]
    dres, dctx, *up = call(
        functools.partial(norm_back_kernel, blks, lines), s,
        (dpre, done, upt, resid, gain1, gains, w_out, ctx),
        [((rows, width), F32), square] + up_out, mib=8, us=6,
    )

    far_q, far_kv, give = call(
        functools.partial(far_back_kernel, heads), s, (qkv, kv, ctx, dctx, far_lse, w_qkv),
        [((width // 2, rows), BF16), square, square], [((2 * width, rows), BF16)], mib=8, us=6,
    )

    if lines:
        got = swap(up[1], "batch", 1)
        chip2 = pair_sum(s, up[0], got, tuple((i,) for i in range(blks)))
        far_q, give, *chip2 = lax.optimization_barrier((far_q, give, *chip2))
        blk2 = [chip2[0]] + [swap(chip2[i], "blk", i) for i in range(1, blks)]
        proj_out = [((blks, cols, width // 2), BF16)] * 2
    else:
        proj_out = [((3 * width, width), BF16)]
    give = swap(give, "blk", 1)
    dqkv, *proj = call(
        functools.partial(near_back_kernel, heads, blks, lines), s,
        (qkv, ctx, dctx, near_lse, far_q, far_kv)
        + ((x_parts[0], down[2]) if lines else (x, xp)),
        [((3 * width, rows), BF16)] + proj_out, [square], mib=8, us=10,
    )
    if lines:
        got = swap(proj[1], "batch", 1)
    (own,) = call(through_kernel, s, (w_qkv, dqkv), [((width, rows), F32)], mib=4, us=3)

    if lines:
        low1 = pair_sum(s, low1, got1, ((0,), (1,)))
        mine1 = lines_sum(
            s, (low1[0], swap(low1[1], "blk", 1)), (high, inner // (2 * lines)),
            down_pieces(inner // (2 * lines)), lines,
        )
        size = width // (2 * lines)
        chip3 = pair_sum(s, proj[0], got, tuple((i,) for i in range(blks)))
        blk3 = [chip3[0]] + [swap(chip3[i], "blk", i) for i in range(1, blks)]
        mine2 = lines_sum(
            s, blk2, (high + 16, width // 2 + 128), up_pieces(wide, width // 2, lines), lines
        )
        mine3 = lines_sum(s, blk3, (cols, size), down_pieces(size), lines)
        (own_down,) = call(
            down_final_kernel, s, over_lines(mine1), [((inner // batch, high), F32)], mib=4, us=1
        )
        own_up, own_out, sums = call(
            functools.partial(up_final_kernel, high, width // 2, size), s, over_lines(mine2),
            [((size, wide), F32), ((size, high), F32), ((8, 128), F32)], mib=4, us=1,
        )
        sums = sums[:4, :size]
        (own_qkv,) = call(
            down_final_kernel, s, over_lines(mine3), [((size, cols), F32)], mib=4, us=1
        )
    else:
        own_down = reduce_any([down[0].T])
        both = reduce_any([up[0], up[1].T], up[2][:4].T)
        own_up, own_out, sums = both[:, :wide], both[:, wide : wide + high], both[:, wide + high :].T
        own_qkv = reduce_any([proj[0].T])
    (grad_in,) = call(input_kernel, s, (own, give, dres), [((rows, width), BF16)], mib=4, us=2)
    return (
        hid.reshape(hidden_in.shape),
        grad_in.reshape(hidden_in.shape),
        own_qkv,
        own_out,
        sums[0],
        sums[1],
        own_up,
        own_down,
        sums[2],
        sums[3],
    )


def solution(mesh):
    rows = P("blk", "batch", None, None)
    both = P("batch", "blk")
    return jax.shard_map(
        shards,
        mesh=mesh,
        in_specs=(rows, P(None, "batch")) + (P(),) * 9 + (rows,),
        out_specs=(rows, rows, both, both, P("batch"), P("batch"), both, both)
        + (P("batch"), P("batch")),
        check_vma=False,
    )
```

```python
import functools
import math

import jax
import jax.numpy as jnp
from jax import lax
from jax.experimental import pallas as pl
from jax.experimental.pallas import tpu as pltpu
from jax.sharding import PartitionSpec as P

F32 = jnp.float32
BF16 = jnp.bfloat16
MIB = 1 << 20
EPS = 1e-06
NEG = -1e30
LOG2E = math.log2(math.e)
FF_BLOCKS = 4
STEP = 48
EVERY = slice(None)
ME, CORE, LINE, NEAR, FAR, ORDER = range(6)


def swap(block, axis, bits):
    return lax.ppermute(block, axis, [(i, i ^ bits) for i in range(lax.axis_size(axis))])


def nn(a, b):
    return lax.dot_general(a, b, (((1,), (0,)), ((), ())), preferred_element_type=F32)


def nt(a, b):
    return lax.dot_general(a, b, (((1,), (1,)), ((), ())), preferred_element_type=F32)


def tn(a, b):
    return lax.dot_general(a, b, (((0,), (0,)), ((), ())), preferred_element_type=F32)


def call(kernel, scalars, ins, outs, scratch=(), mib=16, us=0):
    vmem = pl.BlockSpec(memory_space=pltpu.VMEM)
    return pl.pallas_call(
        kernel,
        in_specs=[pl.BlockSpec(memory_space=pltpu.SMEM)] + [vmem] * len(ins),
        out_specs=[vmem] * len(outs),
        out_shape=[jax.ShapeDtypeStruct(shape, dtype) for shape, dtype in outs],
        scratch_shapes=[pltpu.VMEM(shape, dtype) for shape, dtype in scratch],
        compiler_params=pltpu.CompilerParams(vmem_limit_bytes=mib * MIB),
        cost_estimate=pl.CostEstimate(
            flops=1000000 + us * 1150000000, bytes_accessed=10000, transcendentals=0
        ),
    )(scalars, *ins)


def rows_of(index, size):
    return pl.ds(pl.multiple_of(index * size, size), size)


def stacked(first, *rows):
    spare = lax.broadcasted_iota(jnp.int32, (16, first.shape[1]), 0)
    extra = jnp.zeros(spare.shape, F32)
    for i, row in enumerate(rows):
        extra = jnp.where(spare == i, row, extra)
    return jnp.concatenate([first, extra.astype(BF16)], axis=0)


def key_bias(valid, keys):
    place = lax.broadcasted_iota(jnp.int32, (1, keys), 1)
    return jnp.where(place < valid, 0.0, NEG)


def attend_head(coef, q, k, v, bias):
    dim = q.shape[0]
    raw = nn(stacked(k, bias).T, stacked(q, 1.0))
    top = jnp.max(raw, axis=0, keepdims=True)
    terms = jnp.exp2((raw - top) * coef).astype(BF16)
    got = nn(stacked(v, 1.0), terms)
    total = got[dim : dim + 1]
    return (got[:dim] / total).astype(BF16), top * coef + jnp.log2(total)


def attend_head_back(coef, scale, q, k, v, bias, lse, ctx, dctx):
    delta = jnp.sum(dctx.astype(F32) * ctx.astype(F32), axis=0, keepdims=True)
    raw = nn(stacked(k, bias).T, stacked(q, 1.0))
    probs = jnp.exp2(raw * coef - lse)
    draw = (probs * (nn(v.T, dctx) - delta)).astype(BF16)
    dv = nt(dctx, probs.astype(BF16)).astype(BF16)
    dk = (nt(q, draw) * scale).astype(BF16)
    dq = (nn(k, draw) * scale).astype(BF16)
    return dq, dk, dv


def norm_stats(hidden):
    mean = jnp.mean(hidden, axis=-1, keepdims=True)
    centred = hidden - mean
    var = jnp.mean(centred * centred, axis=-1, keepdims=True)
    inv = lax.rsqrt(var + EPS)
    return centred * inv, inv


def norm_back(grad, gain, hat, inv):
    scaled = grad * gain
    shift = jnp.mean(scaled, axis=-1, keepdims=True)
    slope = jnp.mean(scaled * hat, axis=-1, keepdims=True)
    back = inv * (scaled - shift - hat * slope)
    return back, jnp.sum(grad * hat, axis=0, keepdims=True), jnp.sum(grad, axis=0, keepdims=True)


def by_core(mat, core, lines):
    span = mat.shape[1] // (2 * lines)
    halves = [
        jnp.concatenate(
            [mat[:, (2 * z + p) * span : (2 * z + p + 1) * span] for z in range(lines)], axis=1
        )
        for p in range(2)
    ]
    even = core == 0
    return jnp.where(even, halves[0], halves[1]), jnp.where(even, halves[1], halves[0])


def rows_by_core(ref, core, lines):
    span = ref.shape[0] // (2 * lines)
    return [
        jnp.concatenate([ref[rows_of(2 * z + (core ^ which), span), :] for z in range(lines)], axis=0)
        for which in range(2)
    ]


def near_kernel(heads, lines, s_ref, x_ref, w_ref, qkv_ref, ctx_ref, lse_ref, *rest):
    width = x_ref.shape[1]
    dim = width // heads
    coef = LOG2E / math.sqrt(dim)
    turned = x_ref[...].T
    for part in range(3):
        at = slice(part * width, (part + 1) * width)
        qkv_ref[at, :] = tn(w_ref[:, at], turned).astype(BF16)
    if lines:
        rest[0][0], rest[0][1] = by_core(x_ref[...], s_ref[CORE], lines)
    bias = key_bias(s_ref[NEAR], x_ref.shape[0])

    def one(i, carry):
        head = s_ref[ORDER + i]
        at = rows_of(head, dim)
        ctx_ref[at, :], lse_ref[head] = attend_head(
            coef,
            qkv_ref[at, :],
            qkv_ref[rows_of(heads + head, dim), :],
            qkv_ref[rows_of(2 * heads + head, dim), :],
            bias,
        )
        return carry

    lax.fori_loop(0, heads // 2, one, 0, unroll=3)


def ffn_kernel(
    heads, blks, lines, s_ref, x_ref, xp_ref, w_ref, qkv_ref, near_ref, wo_ref, gain1_ref,
    bias1_ref, gain2_ref, bias2_ref, dout_ref, wu_ref, wd_ref,
    kv_ref, ctx_ref, lse_ref, hid_ref, slope_ref, dtwo_ref, upt_ref, resid_ref, gains_ref, *rest,
):
    act_ref = rest[-1]
    rows, width = x_ref.shape
    dim = width // heads
    coef = LOG2E / math.sqrt(dim)
    me, core = s_ref[ME], s_ref[CORE]
    turned = xp_ref[...].T
    for part in range(2):
        at = slice((part + 1) * width, (part + 2) * width)
        kv_ref[part * width : (part + 1) * width, :] = tn(w_ref[:, at], turned).astype(BF16)
    bias = key_bias(s_ref[FAR], rows)

    def one(i, carry):
        head = s_ref[ORDER + heads // 2 + i]
        at = rows_of(head, dim)
        ctx_ref[at, :], lse_ref[head] = attend_head(
            coef, qkv_ref[at, :], kv_ref[at, :], kv_ref[rows_of(heads + head, dim), :], bias
        )
        mine = rows_of(s_ref[ORDER + i], dim)
        ctx_ref[mine, :] = near_ref[mine, :]
        return carry

    lax.fori_loop(0, heads // 2, one, 0, unroll=3)

    resid = x_ref[...].astype(F32) + tn(ctx_ref[...], wo_ref[...])
    resid_ref[...] = resid
    hat, _ = norm_stats(resid)
    one_in = hat * gain1_ref[...] + bias1_ref[...]
    low = one_in.astype(BF16)
    upt_ref[...] = low.T
    total = one_in
    blk = wu_ref.shape[1] // FF_BLOCKS
    for j in range(FF_BLOCKS):
        at = slice(j * blk, (j + 1) * blk)
        pre = nn(low, wu_ref[:, at])
        cdf = 0.5 + 0.5 * lax.erf(pre * math.sqrt(0.5))
        pdf = jnp.exp2(pre * pre * (-0.5 * LOG2E)) * (1.0 / math.sqrt(2.0 * math.pi))
        slope_ref[:, at] = (cdf + pre * pdf).astype(BF16)
        act = (pre * cdf).astype(BF16)
        act_ref[:, at] = act
        total = total + nn(act, wd_ref[at, :])
    hat, inv = norm_stats(total)
    hid_ref[...] = (hat * gain2_ref[...] + bias2_ref[...]).astype(BF16)
    back, gain, shift = norm_back(dout_ref[...].astype(F32), gain2_ref[...], hat, inv)
    dtwo_ref[...] = back
    gains_ref[0:1, :] = gain
    gains_ref[1:2, :] = shift
    turned = back.astype(BF16).T
    if lines:
        high = width // blks
        span = act_ref.shape[1] // (2 * lines)
        for which in (1, 0):
            for z in range(lines):
                prod = nn(turned, act_ref[:, rows_of(2 * z + (core ^ which), span)]).astype(BF16)
                for k in range(blks):
                    rest[which][k ^ me, :, z * span : (z + 1) * span] = prod[
                        k * high : (k + 1) * high
                    ]
        rest[2][0], rest[2][1] = by_core(xp_ref[...], core, lines)
    else:
        rest[0][...] = nn(turned, act_ref[...]).astype(BF16)


def pre_back_kernel(s_ref, dtwo_ref, slope_ref, wd_ref, wu_ref, dpre_ref, done_ref):
    low = dtwo_ref[...].astype(BF16)
    total = dtwo_ref[...]
    blk = wu_ref.shape[1] // FF_BLOCKS
    for j in range(FF_BLOCKS):
        at = slice(j * blk, (j + 1) * blk)
        dpre = (nt(low, wd_ref[at, :]) * slope_ref[:, at].astype(F32)).astype(BF16)
        dpre_ref[:, at] = dpre
        total = total + nt(dpre, wu_ref[:, at])
    done_ref[...] = total


def norm_back_kernel(
    blks, lines, s_ref, dpre_ref, done_ref, upt_ref, resid_ref, gain1_ref, gains_ref, wo_ref,
    ctx_ref, dres_ref, dctx_ref, *outs,
):
    me, core = s_ref[ME], s_ref[CORE]
    hat, inv = norm_stats(resid_ref[...])
    back, gain, shift = norm_back(done_ref[...], gain1_ref[...], hat, inv)
    dres_ref[...] = back
    turned = back.astype(BF16).T
    dctx_ref[...] = nn(wo_ref[...], turned).astype(BF16)
    row = lax.broadcasted_iota(jnp.int32, (16, gain.shape[1]), 0)
    sums = jnp.where(row == 0, gain, jnp.where(row == 1, shift, 0.0))
    sums = jnp.where(row == 2, gains_ref[0:1, :], sums)
    sums = jnp.where(row == 3, gains_ref[1:2, :], sums).astype(BF16)
    if not lines:
        outs[0][...] = nn(upt_ref[...], dpre_ref[...]).astype(BF16)
        outs[1][...] = nt(turned, ctx_ref[...]).astype(BF16)
        outs[2][...] = sums
        return
    keep_ref, sends = outs[0], outs[1:]
    ups = rows_by_core(upt_ref, core, lines)
    ctxs = rows_by_core(ctx_ref, core, lines)
    sums = by_core(sums, core, lines)
    wide = dpre_ref.shape[1] // blks
    half = ups[0].shape[0]
    high = turned.shape[0] // blks
    pieces = wide // half
    for which in (1, 0):
        for k in range(blks):
            prod = nn(ups[which], dpre_ref[:, k * wide : (k + 1) * wide]).astype(BF16)
            for p in range(pieces):
                part = prod[:, p * half : (p + 1) * half]
                if which:
                    sends[p][k ^ me] = part
                else:
                    keep_ref[k ^ me, p * half : (p + 1) * half, :] = part
        prod = nt(turned, ctxs[which]).astype(BF16)
        for k in range(blks):
            part = jnp.concatenate([prod[k * high : (k + 1) * high], sums[which]], axis=0)
            if which:
                sends[pieces][k ^ me] = part
            else:
                keep_ref[k ^ me, wide:, :] = part


def far_back_kernel(
    heads, s_ref, qkv_ref, kv_ref, ctx_ref, dctx_ref, lse_ref, w_ref, dq_ref, dkv_ref, give_ref,
    wide_ref,
):
    width, rows = ctx_ref.shape
    dim = width // heads
    half = heads // 2
    scale = 1.0 / math.sqrt(dim)
    bias = key_bias(s_ref[FAR], rows)
    wide_ref[...] = jnp.zeros_like(wide_ref)

    def one(i, carry):
        head = s_ref[ORDER + half + i]
        at, low = rows_of(head, dim), rows_of(heads + head, dim)
        dq, dk, dv = attend_head_back(
            LOG2E * scale, scale, qkv_ref[at, :], kv_ref[at, :], kv_ref[low, :], bias,
            lse_ref[head], ctx_ref[at, :], dctx_ref[at, :],
        )
        dq_ref[rows_of(i, dim), :] = dq
        dkv_ref[rows_of(i, dim), :] = dk
        dkv_ref[rows_of(half + i, dim), :] = dv
        wide_ref[at, :] = dk
        wide_ref[low, :] = dv
        return carry

    lax.fori_loop(0, half, one, 0, unroll=3)
    give_ref[...] = nn(w_ref[:, width:], wide_ref[...]).astype(BF16)


def near_back_kernel(
    heads, blks, lines, s_ref, qkv_ref, ctx_ref, dctx_ref, lse_ref, farq_ref, farkv_ref, x_ref,
    xp_ref, dqkv_ref, *rest,
):
    outs, near_ref = rest[:-1], rest[-1]
    width, rows = ctx_ref.shape
    dim = width // heads
    half = heads // 2
    scale = 1.0 / math.sqrt(dim)
    bias = key_bias(s_ref[NEAR], rows)
    me = s_ref[ME]
    dqkv_ref[width:, :] = jnp.zeros((2 * width, rows), BF16)

    def one(i, carry):
        head = s_ref[ORDER + i]
        at = rows_of(head, dim)
        key, value = rows_of(heads + head, dim), rows_of(2 * heads + head, dim)
        dq, dk, dv = attend_head_back(
            LOG2E * scale, scale, qkv_ref[at, :], qkv_ref[key, :], qkv_ref[value, :], bias,
            lse_ref[head], ctx_ref[at, :], dctx_ref[at, :],
        )
        dqkv_ref[at, :] = dq
        dqkv_ref[key, :] = dk
        dqkv_ref[value, :] = dv
        near_ref[rows_of(i, dim), :] = dk
        near_ref[rows_of(half + i, dim), :] = dv
        dqkv_ref[rows_of(s_ref[ORDER + half + i], dim), :] = farq_ref[rows_of(i, dim), :]
        return carry

    lax.fori_loop(0, half, one, 0, unroll=3)
    per = 3 * heads // blks

    def store(which, unit, prod):
        at = ((unit // per) ^ me, rows_of(unit % per, dim), EVERY)
        if not lines:
            outs[0][rows_of(unit, dim), :] = prod
        elif which:
            for i, out in enumerate(outs[1:]):
                out[at] = prod[:, i * 128 : (i + 1) * 128]
        else:
            outs[0][at] = prod

    for which in (1, 0) if lines else (0,):
        x = x_ref[which] if lines else x_ref[...]
        xp = xp_ref[which] if lines else xp_ref[...]
        prod = nn(dqkv_ref[:width, :], x).astype(BF16)
        for h in range(heads):
            store(which, h, prod[h * dim : (h + 1) * dim])
        for first, grads, inputs in ((0, near_ref, x), (half, farkv_ref, xp)):
            prod = nn(grads[...], inputs).astype(BF16)
            for i in range(half):
                head = s_ref[ORDER + first + i]
                store(which, heads + head, prod[i * dim : (i + 1) * dim])
                low = (half + i) * dim
                store(which, 2 * heads + head, prod[low : low + dim])


def through_kernel(s_ref, w_ref, dqkv_ref, own_ref):
    own_ref[...] = nn(w_ref[...], dqkv_ref[...])


def input_kernel(s_ref, own_ref, got_ref, dres_ref, out_ref):
    total = own_ref[...] + got_ref[...].astype(F32)
    out_ref[...] = (total.T + dres_ref[...]).astype(BF16)


def add_up(*parts):
    total = parts[0].astype(F32)
    for part in parts[1:]:
        total = total + part.astype(F32)
    return total


def after(scalars, *arrays):
    return lax.optimization_barrier((scalars,) + arrays)[0]


def block_at(ref, at):
    at = tuple(at) + (EVERY,) * (len(ref.shape) - len(at))
    first, last, _ = at[-2].indices(ref.shape[-2])
    return at[:-2], first, last - first, at[-1]


def sums_kernel(plan, lines, inputs, s_ref, *refs):
    ins, outs = refs[:inputs], refs[inputs:]

    def run(place):
        for out, dst, terms in plan(place):
            lead, first, rows, cols = block_at(outs[out], dst)
            found = [(ins[i],) + block_at(ins[i], src) for i, src in terms]

            def add(at, size):
                total = add_up(
                    *(ref[leads + (pl.ds(at + row, size), col)] for ref, leads, row, _, col in found)
                )
                outs[out][lead + (pl.ds(at + first, size), cols)] = total.astype(outs[out].dtype)

            def body(i, carry):
                add(pl.multiple_of(i * STEP, STEP), STEP)
                return carry

            if rows >= 2 * STEP:
                lax.fori_loop(0, rows // STEP, body, 0)
                if rows % STEP:
                    add(rows // STEP * STEP, rows % STEP)
            else:
                add(0, rows)

    if lines:
        for place in range(lines):
            pl.when(s_ref[LINE] == place)(functools.partial(run, place))
    else:
        run(s_ref[LINE])


def sums(scalars, ins, shapes, plan, lines=0):
    kernel = functools.partial(sums_kernel, plan, lines, len(ins))
    return call(kernel, scalars, ins, [(shape, BF16) for shape in shapes], mib=4)


def span_of(index, size):
    return slice(index * size, (index + 1) * size)


class Halves:
    def __init__(self, cut, rows, cols):
        self.cut, self.rows, self.cols = cut, rows, cols
        self.sizes = (cut, rows - cut)
        self.at = (slice(0, cut), slice(cut, rows))

    def first(self, s, keep, gots, where):
        shapes = [(2, size, self.cols) for size in self.sizes for _ in range(2)]
        picks = ((0, 0, (0, 2)), (1, 0, (1, 3)), (2, 1, (0, 1)), (3, 1, (2, 3)))

        def plan(_):
            return [
                (out, (slot, here, col), [(0, (j, kept, col)), (1 + i, (j, rows, EVERY))])
                for out, half, group in picks
                for slot, j in enumerate(group)
                for i, kept, rows, here, col in where(half)
            ]

        return sums(s, (keep,) + tuple(gots), shapes, plan)

    def second(self, s, chip):
        got = (swap(chip[1], "blk", 1), swap(chip[3], "blk", 2))
        shapes = [(size, self.cols) for size in self.sizes for _ in range(2)]

        def plan(_):
            return [
                (2 * half + slot, (EVERY,), [(half, (slot,)), (2 + half, (slot,))])
                for half in range(2)
                for slot in range(2)
            ]

        return sums(s, (chip[0], chip[2]) + got, shapes, plan)

    def third(self, s, pair, shape, pieces, lines):
        got = (swap(pair[1], "blk", 2), swap(pair[3], "blk", 1))

        def plan(place):
            return [
                (out, (slot,) + dst, [(half, src), (2 + half, src)])
                for out in range(2)
                for slot in range(2)
                for half, src, dst in pieces(place ^ (out + 2 * slot))
            ]

        return sums(s, (pair[0], pair[2]) + got, [(2,) + shape] * 2, plan, lines)


def fourth(s, mine):
    got = swap(mine[1], "batch", 2)

    def plan(_):
        return [(i, (EVERY,), [(0, (i,)), (1, (i,))]) for i in range(2)]

    return sums(s, (mine[0], got), [mine[0].shape[1:]] * 2, plan)


def dealt(s, keep, send):
    def plan(_):
        return [
            (out, (slot,), [(i, (2 * out + slot,)) for i in range(2)])
            for out in range(2)
            for slot in range(2)
        ]

    return sums(s, (keep, send), [(2,) + keep.shape[1:]] * 2, plan)


def paired(s, keep, got):
    def plan(_):
        return [(i, (EVERY,), [(0, (i,)), (1, (i,))]) for i in range(2)]

    return sums(s, (keep, got), [keep.shape[1:]] * 2, plan)


def by_lanes(parts):
    return lambda half: [
        (i, parts.at[half], parts.at[half], EVERY, slice(i * 128, (i + 1) * 128))
        for i in range(parts.cols // 128)
    ]


def by_rows(parts, wide):
    size = parts.cols
    found = [[(0, slice(0, size), EVERY, EVERY, EVERY)], []]
    for p in range(1, wide // size):
        at = slice((p - 1) * size, p * size)
        found[1].append((p, slice(p * size, (p + 1) * size), EVERY, at, EVERY))
    found[1].append((wide // size, slice(wide, None), EVERY, slice(wide - size, None), EVERY))
    return lambda half: found[half]


def proj_pieces(parts, size):
    def pieces(z):
        return [(half, (EVERY, span_of(z, size)), (parts.at[half], EVERY)) for half in range(2)]

    return pieces


def up_pieces(parts, wide, size):
    half = parts.cols

    def pieces(z):
        found = []
        for p in range(wide // half):
            row = p * half + z * size
            which = int(row >= parts.cut)
            row -= which * parts.cut
            found.append(
                (which, (slice(row, row + size), EVERY), (span_of(p, size), slice(0, half)))
            )
        rest = (slice(wide - parts.cut, None), span_of(z, size))
        return found + [(1, rest, (EVERY, slice(half, half + size)))]

    return pieces


def down_first(s, keep, got, lines):
    blks, high, cols = keep.shape
    size = cols // lines

    def plan(place):
        return [
            (out, (slot, j), [(i, (j, EVERY, rows_of(place ^ (out + 2 * slot), size))) for i in range(2)])
            for out in range(2)
            for slot in range(2)
            for j in range(blks)
        ]

    return sums(s, (keep, got), [(2, blks, high, size)] * 2, plan)


def turned_final_kernel(s_ref, *refs):
    refs[-1][...] = add_up(*(ref[...] for ref in refs[:-1])).T


def up_final_kernel(high, half, size, s_ref, *refs):
    up_ref, out_ref, sums_ref = refs[-3:]
    total = add_up(*(ref[...] for ref in refs[:-3]))
    for p in range(high // size):
        up_ref[:, span_of(p, half)] = total[span_of(p, size), :half]
    out_ref[...] = total[:high, half : half + size].T
    sums_ref[...] = total[high : high + 8, half:]


def reduce_any(mats, thin=None):
    blks = lax.axis_size("blk")
    lines = lax.axis_size("batch") // 2
    me = lax.axis_index("blk")
    core = lax.axis_index("batch") % 2
    line = lax.axis_index("batch") // 2
    pieces = []
    for mat in mats:
        rows = mat.shape[0] // (2 * lines)
        pieces.append(mat.reshape(lines, 2, rows, blks, -1))
    if thin is not None:
        thin = thin.reshape(lines, 2, rows, 1, -1)
        pieces.append(jnp.broadcast_to(thin, thin.shape[:3] + (blks,) + thin.shape[4:]))
    every = jnp.concatenate(pieces, axis=4)

    def half(which, distance):
        part = lax.dynamic_index_in_dim(every, which, 1, keepdims=False)
        return lax.dynamic_index_in_dim(part, me ^ distance, 2, keepdims=False)

    keep = [half(core, distance) for distance in range(blks)]
    got = swap(jnp.stack([half(1 - core, i) for i in range(blks)]), "batch", 1)
    chip = [add_up(part, got[i]).astype(BF16) for i, part in enumerate(keep)]
    total = add_up(chip[0], *(swap(chip[i], "blk", i) for i in range(1, blks)))
    while lines > 1:
        lines //= 2
        upper = line // lines
        pairs = total.astype(BF16).reshape((2, lines) + total.shape[1:])
        mine = lax.dynamic_index_in_dim(pairs, upper, 0, keepdims=False)
        theirs = lax.dynamic_index_in_dim(pairs, 1 - upper, 0, keepdims=False)
        total = add_up(mine, swap(theirs, "batch", 2 * lines))
        line = line % lines
    return total[0]


def shards(
    hidden_in, lengths, head_order, w_qkv, w_out, ln1_gain, ln1_bias, w_up, w_down, ln2_gain,
    ln2_bias, grad_out,
):
    _, _, rows, width = hidden_in.shape
    heads = head_order.shape[0]
    blks = lax.axis_size("blk")
    batch = lax.axis_size("batch")
    inner = w_up.shape[1]
    me = lax.axis_index("blk")
    at = lax.axis_index("batch")
    fast = batch == 8 and blks == 4 and width % (16 * batch) == 0
    lines = batch // 2 if fast else 0
    wide = inner // blks
    high = width // blks
    cols = 3 * width // blks

    x = hidden_in.reshape(rows, width)
    dout = grad_out.reshape(rows, width)
    xp = swap(x, "blk", 1)
    gain1, bias1, gain2, bias2 = (
        part.reshape(1, width) for part in (ln1_gain, ln1_bias, ln2_gain, ln2_bias)
    )
    length = lax.dynamic_index_in_dim(lengths[:, 0], me // 2, 0, keepdims=False)
    ids = jnp.arange(heads, dtype=jnp.int32)
    order = jnp.sum(jnp.where(head_order[None, :] == ids[:, None], ids[None, :], 0), axis=1)
    parts = [me, at % 2, at // 2, length - rows * (me % 2), length - rows * (1 - me % 2)]
    s = jnp.concatenate([jnp.stack(parts).astype(jnp.int32), order.astype(jnp.int32)])

    square = ((width, rows), BF16)
    lse = ((heads, 1, rows), F32)
    split = [((2, rows, width // 2), BF16)] if lines else []
    qkv, near_ctx, near_lse, *x_parts = call(
        functools.partial(near_kernel, heads, lines), s, (x, w_qkv),
        [((3 * width, rows), BF16), square, lse] + split, mib=8, us=8,
    )

    if lines:
        down_out = [((blks, high, inner // 2), BF16)] * 2 + split
    else:
        down_out = [((width, inner), BF16)]
    kv, ctx, far_lse, hid, slope, dtwo, upt, resid, gains, *down = call(
        functools.partial(ffn_kernel, heads, blks, lines), s,
        (x, xp, w_qkv, qkv, near_ctx, w_out, gain1, bias1, gain2, bias2, dout, w_up, w_down),
        [((2 * width, rows), BF16), square, lse, ((rows, width), BF16), ((rows, inner), BF16),
         ((rows, width), F32), square, ((rows, width), F32), ((8, width), F32)] + down_out,
        [((rows, inner), BF16)], mib=16, us=18,
    )

    s = after(s, dtwo)
    dpre, done = call(
        pre_back_kernel, s, (dtwo, slope, w_down, w_up),
        [((rows, inner), BF16), ((rows, width), F32)], mib=8,
    )
    s = after(s, done)
    if lines:
        chip1 = down_first(s, down[0], swap(down[1], "batch", 1), lines)
        s = after(s, chip1[0])
        half = width // 2
        up_out = [((blks, wide + high + 16, half), BF16)]
        up_out += [((blks, half, half), BF16)] * (wide // half) + [((blks, high + 16, half), BF16)]
        proj_out = [((blks, cols, half), BF16)] + [((blks, cols, 128), BF16)] * (half // 128)
    else:
        up_out = [((width, inner), BF16), ((width, width), BF16), ((16, width), BF16)]
        proj_out = [((3 * width, width), BF16)]
    dres, dctx, *up = call(
        functools.partial(norm_back_kernel, blks, lines), s,
        (dpre, done, upt, resid, gain1, gains, w_out, ctx),
        [((rows, width), F32), square] + up_out, mib=8,
    )
    s = after(s, dctx)
    far_q, far_kv, give = call(
        functools.partial(far_back_kernel, heads), s, (qkv, kv, ctx, dctx, far_lse, w_qkv),
        [((width // 2, rows), BF16), square, square], [((2 * width, rows), BF16)], mib=8,
    )
    s = after(s, far_q)
    if not lines:
        got_in = swap(give, "blk", 1)
    size = width // batch
    if lines:
        ups = Halves(half, wide + high + 16, half)
        projs = Halves(cols // 2, cols, half)
        gots = [swap(part, "batch", 1) for part in up[1:]]
        chip2 = ups.first(s, up[0], gots, by_rows(ups, wide))
        s = after(s, chip2[0])
    dqkv, *proj = call(
        functools.partial(near_back_kernel, heads, blks, lines), s,
        (qkv, ctx, dctx, near_lse, far_q, far_kv)
        + ((x_parts[0], down[2]) if lines else (x, xp)),
        [((3 * width, rows), BF16)] + proj_out, [square], mib=8,
    )
    s = after(s, dqkv)
    (own,) = call(through_kernel, s, (w_qkv, dqkv), [((width, rows), F32)], mib=4)
    s = after(s, own)
    if lines:
        gots = [swap(part, "batch", 1) for part in proj[1:]]
        chip3 = projs.first(s, proj[0], gots, by_lanes(projs))
        s = after(s, chip3[0])
        line1 = fourth(s, chip1)
        s = after(s, line1[0])
        pair2 = ups.second(s, chip2)
        s = after(s, pair2[0])
        pair3 = projs.second(s, chip3)
        s = after(s, pair3[0])
        got_in = swap(lax.optimization_barrier((give, pair3[0]))[0], "blk", 1)
        far1 = dealt(s, line1[0], swap(line1[1], "batch", 4))
        s = after(s, far1[0])
        line2 = ups.third(
            s, pair2, (high + 16, width // 2 + 128), up_pieces(ups, wide, size), lines
        )
        s = after(s, line2[0])
        line3 = projs.third(s, pair3, (cols, size), proj_pieces(projs, size), lines)
        s = after(s, line3[0])
        last1 = paired(s, far1[0], swap(far1[1], "blk", 2))
        s = after(s, last1[0])
        last2 = fourth(s, line2)
        s = after(s, last2[0])
        last3 = fourth(s, line3)
        s = after(s, last3[0])
        (own_down,) = call(
            turned_final_kernel, s, (last1[0], swap(last1[1], "blk", 1)),
            [((inner // batch, high), F32)], mib=4,
        )
        s = after(s, own_down)
    (grad_in,) = call(input_kernel, s, (own, got_in, dres), [((rows, width), BF16)], mib=4)
    if lines:
        s = after(s, grad_in)
        own_up, own_out, thin = call(
            functools.partial(up_final_kernel, high, width // 2, size), s,
            (last2[0], swap(last2[1], "batch", 4)),
            [((size, wide), F32), ((size, high), F32), ((8, 128), F32)], mib=4,
        )
        thin = thin[:4, :size]
        s = after(s, own_up)
        (own_qkv,) = call(
            turned_final_kernel, s, (last3[0], swap(last3[1], "batch", 4)),
            [((size, cols), F32)], mib=4,
        )
    else:
        own_down = reduce_any([down[0].T])
        both = reduce_any([up[0], up[1].T], up[2][:4].T)
        own_up, own_out, thin = both[:, :wide], both[:, wide : wide + high], both[:, wide + high :].T
        own_qkv = reduce_any([proj[0].T])
    return (
        hid.reshape(hidden_in.shape),
        grad_in.reshape(hidden_in.shape),
        own_qkv,
        own_out,
        thin[0],
        thin[1],
        own_up,
        own_down,
        thin[2],
        thin[3],
    )


def solution(mesh):
    rows = P("blk", "batch", None, None)
    both = P("batch", "blk")
    return jax.shard_map(
        shards,
        mesh=mesh,
        in_specs=(rows, P(None, "batch")) + (P(),) * 9 + (rows,),
        out_specs=(rows, rows, both, both, P("batch"), P("batch"), both, both)
        + (P("batch"), P("batch")),
        check_vma=False,
    )
```

```python
import functools
import math

import jax
import jax.numpy as jnp
from jax import lax
from jax.experimental import pallas as pl
from jax.experimental.pallas import tpu as pltpu
from jax.sharding import PartitionSpec as P

F32 = jnp.float32
BF16 = jnp.bfloat16
MIB = 1 << 20
EPS = 1e-06
NEG = -1e30
LOG2E = math.log2(math.e)
FF_BLOCKS = 4
STEP = 48
EVERY = slice(None)
ME, CORE, LINE, NEAR, FAR, ORDER = range(6)


def swap(block, axis, bits):
    return lax.ppermute(block, axis, [(i, i ^ bits) for i in range(lax.axis_size(axis))])


def nn(a, b):
    return lax.dot_general(a, b, (((1,), (0,)), ((), ())), preferred_element_type=F32)


def nt(a, b):
    return lax.dot_general(a, b, (((1,), (1,)), ((), ())), preferred_element_type=F32)


def tn(a, b):
    return lax.dot_general(a, b, (((0,), (0,)), ((), ())), preferred_element_type=F32)


def call(kernel, scalars, ins, outs, scratch=(), mib=16, us=0):
    vmem = pl.BlockSpec(memory_space=pltpu.VMEM)
    return pl.pallas_call(
        kernel,
        in_specs=[pl.BlockSpec(memory_space=pltpu.SMEM)] + [vmem] * len(ins),
        out_specs=[vmem] * len(outs),
        out_shape=[jax.ShapeDtypeStruct(shape, dtype) for shape, dtype in outs],
        scratch_shapes=[pltpu.VMEM(shape, dtype) for shape, dtype in scratch],
        compiler_params=pltpu.CompilerParams(vmem_limit_bytes=mib * MIB),
        cost_estimate=pl.CostEstimate(
            flops=1000000 + us * 1150000000, bytes_accessed=10000, transcendentals=0
        ),
    )(scalars, *ins)


def rows_of(index, size):
    return pl.ds(pl.multiple_of(index * size, size), size)


def stacked(first, *rows):
    spare = lax.broadcasted_iota(jnp.int32, (16, first.shape[1]), 0)
    extra = jnp.zeros(spare.shape, F32)
    for i, row in enumerate(rows):
        extra = jnp.where(spare == i, row, extra)
    return jnp.concatenate([first, extra.astype(BF16)], axis=0)


def key_bias(valid, keys):
    place = lax.broadcasted_iota(jnp.int32, (1, keys), 1)
    return jnp.where(place < valid, 0.0, NEG)


def attend_head(coef, q, k, v, bias):
    dim = q.shape[0]
    raw = nn(stacked(k, bias).T, stacked(q, 1.0))
    top = jnp.max(raw, axis=0, keepdims=True)
    terms = jnp.exp2((raw - top) * coef).astype(BF16)
    got = nn(stacked(v, 1.0), terms)
    total = got[dim : dim + 1]
    return (got[:dim] / total).astype(BF16), top * coef + jnp.log2(total)


def attend_head_back(coef, scale, q, k, v, bias, lse, ctx, dctx):
    delta = jnp.sum(dctx.astype(F32) * ctx.astype(F32), axis=0, keepdims=True)
    raw = nn(stacked(k, bias).T, stacked(q, 1.0))
    probs = jnp.exp2(raw * coef - lse)
    draw = (probs * (nn(v.T, dctx) - delta)).astype(BF16)
    dv = nt(dctx, probs.astype(BF16)).astype(BF16)
    dk = (nt(q, draw) * scale).astype(BF16)
    dq = (nn(k, draw) * scale).astype(BF16)
    return dq, dk, dv


def norm_stats(hidden):
    mean = jnp.mean(hidden, axis=-1, keepdims=True)
    centred = hidden - mean
    var = jnp.mean(centred * centred, axis=-1, keepdims=True)
    inv = lax.rsqrt(var + EPS)
    return centred * inv, inv


def norm_back(grad, gain, hat, inv):
    scaled = grad * gain
    shift = jnp.mean(scaled, axis=-1, keepdims=True)
    slope = jnp.mean(scaled * hat, axis=-1, keepdims=True)
    back = inv * (scaled - shift - hat * slope)
    return back, jnp.sum(grad * hat, axis=0, keepdims=True), jnp.sum(grad, axis=0, keepdims=True)


def by_core(mat, core, lines):
    span = mat.shape[1] // (2 * lines)
    halves = [
        jnp.concatenate(
            [mat[:, (2 * z + p) * span : (2 * z + p + 1) * span] for z in range(lines)], axis=1
        )
        for p in range(2)
    ]
    even = core == 0
    return jnp.where(even, halves[0], halves[1]), jnp.where(even, halves[1], halves[0])


def rows_by_core(ref, core, lines):
    span = ref.shape[0] // (2 * lines)
    return [
        jnp.concatenate([ref[rows_of(2 * z + (core ^ which), span), :] for z in range(lines)], axis=0)
        for which in range(2)
    ]


def near_kernel(heads, lines, s_ref, x_ref, w_ref, qkv_ref, ctx_ref, lse_ref, *rest):
    width = x_ref.shape[1]
    dim = width // heads
    coef = LOG2E / math.sqrt(dim)
    turned = x_ref[...].T
    for part in range(3):
        at = slice(part * width, (part + 1) * width)
        qkv_ref[at, :] = tn(w_ref[:, at], turned).astype(BF16)
    if lines:
        rest[0][0], rest[0][1] = by_core(x_ref[...], s_ref[CORE], lines)
    bias = key_bias(s_ref[NEAR], x_ref.shape[0])

    def one(i, carry):
        head = s_ref[ORDER + i]
        at = rows_of(head, dim)
        ctx_ref[at, :], lse_ref[head] = attend_head(
            coef,
            qkv_ref[at, :],
            qkv_ref[rows_of(heads + head, dim), :],
            qkv_ref[rows_of(2 * heads + head, dim), :],
            bias,
        )
        return carry

    lax.fori_loop(0, heads // 2, one, 0, unroll=3)


def ffn_kernel(
    heads, blks, lines, s_ref, x_ref, xp_ref, w_ref, qkv_ref, near_ref, wo_ref, gain1_ref,
    bias1_ref, gain2_ref, bias2_ref, dout_ref, wu_ref, wd_ref,
    kv_ref, ctx_ref, lse_ref, hid_ref, slope_ref, dtwo_ref, upt_ref, resid_ref, gains_ref, *rest,
):
    act_ref = rest[-1]
    rows, width = x_ref.shape
    dim = width // heads
    coef = LOG2E / math.sqrt(dim)
    me, core = s_ref[ME], s_ref[CORE]
    turned = xp_ref[...].T
    for part in range(2):
        at = slice((part + 1) * width, (part + 2) * width)
        kv_ref[part * width : (part + 1) * width, :] = tn(w_ref[:, at], turned).astype(BF16)
    bias = key_bias(s_ref[FAR], rows)

    def one(i, carry):
        head = s_ref[ORDER + heads // 2 + i]
        at = rows_of(head, dim)
        ctx_ref[at, :], lse_ref[head] = attend_head(
            coef, qkv_ref[at, :], kv_ref[at, :], kv_ref[rows_of(heads + head, dim), :], bias
        )
        mine = rows_of(s_ref[ORDER + i], dim)
        ctx_ref[mine, :] = near_ref[mine, :]
        return carry

    lax.fori_loop(0, heads // 2, one, 0, unroll=3)

    resid = x_ref[...].astype(F32) + tn(ctx_ref[...], wo_ref[...])
    resid_ref[...] = resid
    hat, _ = norm_stats(resid)
    one_in = hat * gain1_ref[...] + bias1_ref[...]
    low = one_in.astype(BF16)
    upt_ref[...] = low.T
    total = one_in
    blk = wu_ref.shape[1] // FF_BLOCKS
    for j in range(FF_BLOCKS):
        at = slice(j * blk, (j + 1) * blk)
        pre = nn(low, wu_ref[:, at])
        cdf = 0.5 + 0.5 * lax.erf(pre * math.sqrt(0.5))
        pdf = jnp.exp2(pre * pre * (-0.5 * LOG2E)) * (1.0 / math.sqrt(2.0 * math.pi))
        slope_ref[:, at] = (cdf + pre * pdf).astype(BF16)
        act = (pre * cdf).astype(BF16)
        act_ref[:, at] = act
        total = total + nn(act, wd_ref[at, :])
    hat, inv = norm_stats(total)
    hid_ref[...] = (hat * gain2_ref[...] + bias2_ref[...]).astype(BF16)
    back, gain, shift = norm_back(dout_ref[...].astype(F32), gain2_ref[...], hat, inv)
    dtwo_ref[...] = back
    gains_ref[0:1, :] = gain
    gains_ref[1:2, :] = shift
    turned = back.astype(BF16).T
    if lines:
        high = width // blks
        span = act_ref.shape[1] // (2 * lines)
        for which in (1, 0):
            for z in range(lines):
                prod = nn(turned, act_ref[:, rows_of(2 * z + (core ^ which), span)]).astype(BF16)
                for k in range(blks):
                    rest[which][k ^ me, :, z * span : (z + 1) * span] = prod[
                        k * high : (k + 1) * high
                    ]
        rest[2][0], rest[2][1] = by_core(xp_ref[...], core, lines)
    else:
        rest[0][...] = nn(turned, act_ref[...]).astype(BF16)


def pre_back_kernel(s_ref, dtwo_ref, slope_ref, wd_ref, wu_ref, dpre_ref, done_ref):
    low = dtwo_ref[...].astype(BF16)
    total = dtwo_ref[...]
    blk = wu_ref.shape[1] // FF_BLOCKS
    for j in range(FF_BLOCKS):
        at = slice(j * blk, (j + 1) * blk)
        dpre = (nt(low, wd_ref[at, :]) * slope_ref[:, at].astype(F32)).astype(BF16)
        dpre_ref[:, at] = dpre
        total = total + nt(dpre, wu_ref[:, at])
    done_ref[...] = total


def norm_back_kernel(
    blks, lines, s_ref, dpre_ref, done_ref, upt_ref, resid_ref, gain1_ref, gains_ref, wo_ref,
    ctx_ref, dres_ref, dctx_ref, *outs,
):
    me, core = s_ref[ME], s_ref[CORE]
    hat, inv = norm_stats(resid_ref[...])
    back, gain, shift = norm_back(done_ref[...], gain1_ref[...], hat, inv)
    dres_ref[...] = back
    turned = back.astype(BF16).T
    dctx_ref[...] = nn(wo_ref[...], turned).astype(BF16)
    row = lax.broadcasted_iota(jnp.int32, (16, gain.shape[1]), 0)
    sums = jnp.where(row == 0, gain, jnp.where(row == 1, shift, 0.0))
    sums = jnp.where(row == 2, gains_ref[0:1, :], sums)
    sums = jnp.where(row == 3, gains_ref[1:2, :], sums).astype(BF16)
    if not lines:
        outs[0][...] = nn(upt_ref[...], dpre_ref[...]).astype(BF16)
        outs[1][...] = nt(turned, ctx_ref[...]).astype(BF16)
        outs[2][...] = sums
        return
    keep_ref, sends = outs[0], outs[1:]
    ups = rows_by_core(upt_ref, core, lines)
    ctxs = rows_by_core(ctx_ref, core, lines)
    sums = by_core(sums, core, lines)
    wide = dpre_ref.shape[1] // blks
    half = ups[0].shape[0]
    high = turned.shape[0] // blks
    pieces = wide // half
    def store(which, k, first, part):
        if not which:
            keep_ref[k ^ me, first : first + part.shape[0], :] = part
            return
        start = 0
        for send in sends:
            end = start + send.shape[1]
            low, up = max(first, start), min(first + part.shape[0], end)
            if low < up:
                send[k ^ me, low - start : up - start, :] = part[low - first : up - first]
            start = end

    for which in (1, 0):
        for k in range(blks):
            prod = nn(ups[which], dpre_ref[:, k * wide : (k + 1) * wide]).astype(BF16)
            for p in range(pieces):
                store(which, k, p * half, prod[:, p * half : (p + 1) * half])
        prod = nt(turned, ctxs[which]).astype(BF16)
        for k in range(blks):
            store(which, k, wide, prod[k * high : (k + 1) * high])
            store(which, k, wide + high, sums[which])


def far_back_kernel(
    heads, s_ref, qkv_ref, kv_ref, ctx_ref, dctx_ref, lse_ref, w_ref, dq_ref, dkv_ref, give_ref,
    wide_ref,
):
    width, rows = ctx_ref.shape
    dim = width // heads
    half = heads // 2
    scale = 1.0 / math.sqrt(dim)
    bias = key_bias(s_ref[FAR], rows)
    wide_ref[...] = jnp.zeros_like(wide_ref)

    def one(i, carry):
        head = s_ref[ORDER + half + i]
        at, low = rows_of(head, dim), rows_of(heads + head, dim)
        dq, dk, dv = attend_head_back(
            LOG2E * scale, scale, qkv_ref[at, :], kv_ref[at, :], kv_ref[low, :], bias,
            lse_ref[head], ctx_ref[at, :], dctx_ref[at, :],
        )
        dq_ref[rows_of(i, dim), :] = dq
        dkv_ref[rows_of(i, dim), :] = dk
        dkv_ref[rows_of(half + i, dim), :] = dv
        wide_ref[at, :] = dk
        wide_ref[low, :] = dv
        return carry

    lax.fori_loop(0, half, one, 0, unroll=3)
    give_ref[...] = nn(w_ref[:, width:], wide_ref[...]).astype(BF16)


def near_back_kernel(
    heads, blks, lines, s_ref, qkv_ref, ctx_ref, dctx_ref, lse_ref, farq_ref, farkv_ref, x_ref,
    xp_ref, dqkv_ref, *rest,
):
    outs, near_ref = rest[:-1], rest[-1]
    width, rows = ctx_ref.shape
    dim = width // heads
    half = heads // 2
    scale = 1.0 / math.sqrt(dim)
    bias = key_bias(s_ref[NEAR], rows)
    me = s_ref[ME]
    dqkv_ref[width:, :] = jnp.zeros((2 * width, rows), BF16)

    def one(i, carry):
        head = s_ref[ORDER + i]
        at = rows_of(head, dim)
        key, value = rows_of(heads + head, dim), rows_of(2 * heads + head, dim)
        dq, dk, dv = attend_head_back(
            LOG2E * scale, scale, qkv_ref[at, :], qkv_ref[key, :], qkv_ref[value, :], bias,
            lse_ref[head], ctx_ref[at, :], dctx_ref[at, :],
        )
        dqkv_ref[at, :] = dq
        dqkv_ref[key, :] = dk
        dqkv_ref[value, :] = dv
        near_ref[rows_of(i, dim), :] = dk
        near_ref[rows_of(half + i, dim), :] = dv
        dqkv_ref[rows_of(s_ref[ORDER + half + i], dim), :] = farq_ref[rows_of(i, dim), :]
        return carry

    lax.fori_loop(0, half, one, 0, unroll=3)
    per = 3 * heads // blks

    def store(which, unit, prod):
        at = ((unit // per) ^ me, rows_of(unit % per, dim), EVERY)
        if not lines:
            outs[0][rows_of(unit, dim), :] = prod
        elif which:
            for i, out in enumerate(outs[1:]):
                out[at] = prod[:, i * 128 : (i + 1) * 128]
        else:
            outs[0][at] = prod

    for which in (1, 0) if lines else (0,):
        x = x_ref[which] if lines else x_ref[...]
        xp = xp_ref[which] if lines else xp_ref[...]
        prod = nn(dqkv_ref[:width, :], x).astype(BF16)
        for h in range(heads):
            store(which, h, prod[h * dim : (h + 1) * dim])
        for first, grads, inputs in ((0, near_ref, x), (half, farkv_ref, xp)):
            prod = nn(grads[...], inputs).astype(BF16)
            for i in range(half):
                head = s_ref[ORDER + first + i]
                store(which, heads + head, prod[i * dim : (i + 1) * dim])
                low = (half + i) * dim
                store(which, 2 * heads + head, prod[low : low + dim])


def through_kernel(s_ref, w_ref, dqkv_ref, own_ref):
    own_ref[...] = nn(w_ref[...], dqkv_ref[...])


def input_kernel(s_ref, own_ref, got_ref, dres_ref, out_ref):
    total = own_ref[...] + got_ref[...].astype(F32)
    out_ref[...] = (total.T + dres_ref[...]).astype(BF16)


def add_up(*parts):
    total = parts[0].astype(F32)
    for part in parts[1:]:
        total = total + part.astype(F32)
    return total


def after(scalars, *arrays):
    return lax.optimization_barrier((scalars,) + arrays)[0]


def block_at(ref, at):
    at = tuple(at) + (EVERY,) * (len(ref.shape) - len(at))
    first, last, _ = at[-2].indices(ref.shape[-2])
    return at[:-2], first, last - first, at[-1]


def sums_kernel(plan, lines, inputs, s_ref, *refs):
    ins, outs = refs[:inputs], refs[inputs:]

    def run(place):
        for out, dst, terms in plan(place):
            lead, first, rows, cols = block_at(outs[out], dst)
            found = [(ins[i],) + block_at(ins[i], src) for i, src in terms]

            def add(at, size):
                total = add_up(
                    *(ref[leads + (pl.ds(at + row, size), col)] for ref, leads, row, _, col in found)
                )
                outs[out][lead + (pl.ds(at + first, size), cols)] = total.astype(outs[out].dtype)

            def body(i, carry):
                add(pl.multiple_of(i * STEP, STEP), STEP)
                return carry

            if rows >= 2 * STEP:
                lax.fori_loop(0, rows // STEP, body, 0)
                if rows % STEP:
                    add(rows // STEP * STEP, rows % STEP)
            else:
                add(0, rows)

    if lines:
        for place in range(lines):
            pl.when(s_ref[LINE] == place)(functools.partial(run, place))
    else:
        run(s_ref[LINE])


def sums(scalars, ins, shapes, plan, lines=0):
    kernel = functools.partial(sums_kernel, plan, lines, len(ins))
    return call(kernel, scalars, ins, [(shape, BF16) for shape in shapes], mib=4)


def span_of(index, size):
    return slice(index * size, (index + 1) * size)


class Halves:
    def __init__(self, cut, rows, cols):
        self.cut, self.rows, self.cols = cut, rows, cols
        self.sizes = (cut, rows - cut)
        self.at = (slice(0, cut), slice(cut, rows))

    def first(self, s, keep, gots, where):
        shapes = [(2, size, self.cols) for size in self.sizes for _ in range(2)]
        picks = ((0, 0, (0, 2)), (1, 0, (1, 3)), (2, 1, (0, 1)), (3, 1, (2, 3)))

        def plan(_):
            return [
                (out, (slot, here, col), [(0, (j, kept, col)), (1 + i, (j, rows, EVERY))])
                for out, half, group in picks
                for slot, j in enumerate(group)
                for i, kept, rows, here, col in where(half)
            ]

        return sums(s, (keep,) + tuple(gots), shapes, plan)

    def second(self, s, chip):
        got = (swap(chip[1], "blk", 1), swap(chip[3], "blk", 2))
        shapes = [(size, self.cols) for size in self.sizes for _ in range(2)]

        def plan(_):
            return [
                (2 * half + slot, (EVERY,), [(half, (slot,)), (2 + half, (slot,))])
                for half in range(2)
                for slot in range(2)
            ]

        return sums(s, (chip[0], chip[2]) + got, shapes, plan)

    def third(self, s, pair, shape, pieces, lines):
        got = (swap(pair[1], "blk", 2), swap(pair[3], "blk", 1))

        def plan(place):
            return [
                (out, (slot,) + dst, [(half, src), (2 + half, src)])
                for out in range(2)
                for slot in range(2)
                for half, src, dst in pieces(place ^ (out + 2 * slot))
            ]

        return sums(s, (pair[0], pair[2]) + got, [(2,) + shape] * 2, plan, lines)


def fourth(s, mine):
    got = swap(mine[1], "batch", 2)

    def plan(_):
        return [(i, (EVERY,), [(0, (i,)), (1, (i,))]) for i in range(2)]

    return sums(s, (mine[0], got), [mine[0].shape[1:]] * 2, plan)


def dealt(s, keep, send):
    def plan(_):
        return [
            (out, (slot,), [(i, (2 * out + slot,)) for i in range(2)])
            for out in range(2)
            for slot in range(2)
        ]

    return sums(s, (keep, send), [(2,) + keep.shape[1:]] * 2, plan)


def paired(s, keep, got):
    def plan(_):
        return [(i, (EVERY,), [(0, (i,)), (1, (i,))]) for i in range(2)]

    return sums(s, (keep, got), [keep.shape[1:]] * 2, plan)


def by_lanes(parts):
    return lambda half: [
        (i, parts.at[half], parts.at[half], EVERY, slice(i * 128, (i + 1) * 128))
        for i in range(parts.cols // 128)
    ]


def by_rows(parts, cuts):
    def where(half):
        found = []
        start, end = parts.at[half].start, parts.at[half].stop
        for i, (first, last) in enumerate(zip(cuts, cuts[1:])):
            low, up = max(first, start), min(last, end)
            if low < up:
                rows, here = slice(low - first, up - first), slice(low - start, up - start)
                found.append((i, slice(low, up), rows, here, EVERY))
        return found

    return where


def proj_pieces(parts, size):
    def pieces(z):
        return [(half, (EVERY, span_of(z, size)), (parts.at[half], EVERY)) for half in range(2)]

    return pieces


def up_pieces(parts, wide, size):
    half = parts.cols

    def pieces(z):
        found = []
        for p in range(wide // half):
            row = p * half + z * size
            which = int(row >= parts.cut)
            row -= which * parts.cut
            found.append(
                (which, (slice(row, row + size), EVERY), (span_of(p, size), slice(0, half)))
            )
        rest = (slice(wide - parts.cut, None), span_of(z, size))
        return found + [(1, rest, (EVERY, slice(half, half + size)))]

    return pieces


def down_first(s, keep, got, lines):
    blks, high, cols = keep.shape
    size = cols // lines

    def plan(place):
        return [
            (out, (slot, j), [(i, (j, EVERY, rows_of(place ^ (out + 2 * slot), size))) for i in range(2)])
            for out in range(2)
            for slot in range(2)
            for j in range(blks)
        ]

    return sums(s, (keep, got), [(2, blks, high, size)] * 2, plan)


def turned_final_kernel(s_ref, *refs):
    refs[-1][...] = add_up(*(ref[...] for ref in refs[:-1])).T


def up_final_kernel(high, half, size, s_ref, *refs):
    up_ref, out_ref, sums_ref = refs[-3:]
    total = add_up(*(ref[...] for ref in refs[:-3]))
    for p in range(high // size):
        up_ref[:, span_of(p, half)] = total[span_of(p, size), :half]
    out_ref[...] = total[:high, half : half + size].T
    sums_ref[...] = total[high : high + 8, half:]


def reduce_any(mats, thin=None):
    blks = lax.axis_size("blk")
    lines = lax.axis_size("batch") // 2
    me = lax.axis_index("blk")
    core = lax.axis_index("batch") % 2
    line = lax.axis_index("batch") // 2
    pieces = []
    for mat in mats:
        rows = mat.shape[0] // (2 * lines)
        pieces.append(mat.reshape(lines, 2, rows, blks, -1))
    if thin is not None:
        thin = thin.reshape(lines, 2, rows, 1, -1)
        pieces.append(jnp.broadcast_to(thin, thin.shape[:3] + (blks,) + thin.shape[4:]))
    every = jnp.concatenate(pieces, axis=4)

    def half(which, distance):
        part = lax.dynamic_index_in_dim(every, which, 1, keepdims=False)
        return lax.dynamic_index_in_dim(part, me ^ distance, 2, keepdims=False)

    keep = [half(core, distance) for distance in range(blks)]
    got = swap(jnp.stack([half(1 - core, i) for i in range(blks)]), "batch", 1)
    chip = [add_up(part, got[i]).astype(BF16) for i, part in enumerate(keep)]
    total = add_up(chip[0], *(swap(chip[i], "blk", i) for i in range(1, blks)))
    while lines > 1:
        lines //= 2
        upper = line // lines
        pairs = total.astype(BF16).reshape((2, lines) + total.shape[1:])
        mine = lax.dynamic_index_in_dim(pairs, upper, 0, keepdims=False)
        theirs = lax.dynamic_index_in_dim(pairs, 1 - upper, 0, keepdims=False)
        total = add_up(mine, swap(theirs, "batch", 2 * lines))
        line = line % lines
    return total[0]


def shards(
    hidden_in, lengths, head_order, w_qkv, w_out, ln1_gain, ln1_bias, w_up, w_down, ln2_gain,
    ln2_bias, grad_out,
):
    _, _, rows, width = hidden_in.shape
    heads = head_order.shape[0]
    blks = lax.axis_size("blk")
    batch = lax.axis_size("batch")
    inner = w_up.shape[1]
    me = lax.axis_index("blk")
    at = lax.axis_index("batch")
    fast = batch == 8 and blks == 4 and width % (16 * batch) == 0
    lines = batch // 2 if fast else 0
    wide = inner // blks
    size = width // batch
    half = width // 2
    high = width // blks
    cols = 3 * width // blks

    x = hidden_in.reshape(rows, width)
    dout = grad_out.reshape(rows, width)
    xp = swap(x, "blk", 1)
    gain1, bias1, gain2, bias2 = (
        part.reshape(1, width) for part in (ln1_gain, ln1_bias, ln2_gain, ln2_bias)
    )
    length = lax.dynamic_index_in_dim(lengths[:, 0], me // 2, 0, keepdims=False)
    ids = jnp.arange(heads, dtype=jnp.int32)
    order = jnp.sum(jnp.where(head_order[None, :] == ids[:, None], ids[None, :], 0), axis=1)
    parts = [me, at % 2, at // 2, length - rows * (me % 2), length - rows * (1 - me % 2)]
    s = jnp.concatenate([jnp.stack(parts).astype(jnp.int32), order.astype(jnp.int32)])

    square = ((width, rows), BF16)
    lse = ((heads, 1, rows), F32)
    split = [((2, rows, width // 2), BF16)] if lines else []
    qkv, near_ctx, near_lse, *x_parts = call(
        functools.partial(near_kernel, heads, lines), s, (x, w_qkv),
        [((3 * width, rows), BF16), square, lse] + split, mib=8, us=8,
    )

    if lines:
        down_out = [((blks, high, inner // 2), BF16)] * 2 + split
    else:
        down_out = [((width, inner), BF16)]
    kv, ctx, far_lse, hid, slope, dtwo, upt, resid, gains, *down = call(
        functools.partial(ffn_kernel, heads, blks, lines), s,
        (x, xp, w_qkv, qkv, near_ctx, w_out, gain1, bias1, gain2, bias2, dout, w_up, w_down),
        [((2 * width, rows), BF16), square, lse, ((rows, width), BF16), ((rows, inner), BF16),
         ((rows, width), F32), square, ((rows, width), F32), ((8, width), F32)] + down_out,
        [((rows, inner), BF16)], mib=16, us=18,
    )

    s = after(s, dtwo)
    dpre, done = call(
        pre_back_kernel, s, (dtwo, slope, w_down, w_up),
        [((rows, inner), BF16), ((rows, width), F32)], mib=8,
    )
    s = after(s, done)
    if lines:
        ups = Halves(half + size, wide + high + 16, half)
        projs = Halves(cols // 2, cols, half)
        cuts = [ups.rows // 64 * 16 * i for i in range(4)] + [ups.rows]
        up_out = [((blks, wide + high + 16, half), BF16)]
        up_out += [((blks, last - first, half), BF16) for first, last in zip(cuts, cuts[1:])]
        proj_out = [((blks, cols, half), BF16)] + [((blks, cols, 128), BF16)] * (half // 128)
    else:
        up_out = [((width, inner), BF16), ((width, width), BF16), ((16, width), BF16)]
        proj_out = [((3 * width, width), BF16)]
    dres, dctx, *up = call(
        functools.partial(norm_back_kernel, blks, lines), s,
        (dpre, done, upt, resid, gain1, gains, w_out, ctx),
        [((rows, width), F32), square] + up_out, mib=8,
    )
    s = after(s, dctx)
    if lines:
        chip1 = down_first(s, down[0], swap(down[1], "batch", 1), lines)
        s = after(s, chip1[0])
        gots = [swap(part, "batch", 1) for part in up[1:]]
        chip2 = ups.first(s, up[0], gots, by_rows(ups, cuts))
        s = after(s, chip2[0])
    far_q, far_kv, give = call(
        functools.partial(far_back_kernel, heads), s, (qkv, kv, ctx, dctx, far_lse, w_qkv),
        [((width // 2, rows), BF16), square, square], [((2 * width, rows), BF16)], mib=8,
    )
    s = after(s, far_q)
    if not lines:
        got_in = swap(give, "blk", 1)
    dqkv, *proj = call(
        functools.partial(near_back_kernel, heads, blks, lines), s,
        (qkv, ctx, dctx, near_lse, far_q, far_kv)
        + ((x_parts[0], down[2]) if lines else (x, xp)),
        [((3 * width, rows), BF16)] + proj_out, [square], mib=8,
    )
    s = after(s, dqkv)
    if lines:
        pair2 = ups.second(s, chip2)
        s = after(s, pair2[0])
        line1 = fourth(s, chip1)
        s = after(s, line1[0])
        gots = [swap(part, "batch", 1) for part in proj[1:]]
        chip3 = projs.first(s, proj[0], gots, by_lanes(projs))
        s = after(s, chip3[0])
        line2 = ups.third(s, pair2, (high + 16, half + 128), up_pieces(ups, wide, size), lines)
        s = after(s, line2[0])
    (own,) = call(through_kernel, s, (w_qkv, dqkv), [((width, rows), F32)], mib=4)
    s = after(s, own)
    if lines:
        got_in = swap(lax.optimization_barrier((give, own))[0], "blk", 1)
        pair3 = projs.second(s, chip3)
        s = after(s, pair3[0])
        far1 = dealt(s, line1[0], swap(line1[1], "batch", 4))
        s = after(s, far1[0])
        line3 = projs.third(s, pair3, (cols, size), proj_pieces(projs, size), lines)
        s = after(s, line3[0])
        last2 = fourth(s, line2)
        s = after(s, last2[0])
        last1 = paired(s, far1[0], swap(far1[1], "blk", 2))
        s = after(s, last1[0])
    (grad_in,) = call(input_kernel, s, (own, got_in, dres), [((rows, width), BF16)], mib=4)
    if lines:
        s = after(s, grad_in)
        last3 = fourth(s, line3)
        s = after(s, last3[0])
        (own_down,) = call(
            turned_final_kernel, s, (last1[0], swap(last1[1], "blk", 1)),
            [((inner // batch, high), F32)], mib=4,
        )
        s = after(s, own_down)
        own_up, own_out, thin = call(
            functools.partial(up_final_kernel, high, half, size), s,
            (last2[0], swap(last2[1], "batch", 4)),
            [((size, wide), F32), ((size, high), F32), ((8, 128), F32)], mib=4,
        )
        thin = thin[:4, :size]
        s = after(s, own_up)
        (own_qkv,) = call(
            turned_final_kernel, s, (last3[0], swap(last3[1], "batch", 4)),
            [((size, cols), F32)], mib=4,
        )
    else:
        own_down = reduce_any([down[0].T])
        both = reduce_any([up[0], up[1].T], up[2][:4].T)
        own_up, own_out, thin = both[:, :wide], both[:, wide : wide + high], both[:, wide + high :].T
        own_qkv = reduce_any([proj[0].T])
    return (
        hid.reshape(hidden_in.shape),
        grad_in.reshape(hidden_in.shape),
        own_qkv,
        own_out,
        thin[0],
        thin[1],
        own_up,
        own_down,
        thin[2],
        thin[3],
    )


def solution(mesh):
    rows = P("blk", "batch", None, None)
    both = P("batch", "blk")
    return jax.shard_map(
        shards,
        mesh=mesh,
        in_specs=(rows, P(None, "batch")) + (P(),) * 9 + (rows,),
        out_specs=(rows, rows, both, both, P("batch"), P("batch"), both, both)
        + (P("batch"), P("batch")),
        check_vma=False,
    )
```

```python
import functools
import math

import jax
import jax.numpy as jnp
from jax import lax
from jax.experimental import pallas as pl
from jax.experimental.pallas import tpu as pltpu
from jax.sharding import PartitionSpec as P

F32 = jnp.float32
BF16 = jnp.bfloat16
MIB = 1 << 20
EPS = 1e-06
NEG = -1e30
LOG2E = math.log2(math.e)
FF_BLOCKS = 4
UP_PARTS = 2
STEP = 48
EVERY = slice(None)
ME, CORE, LINE, NEAR, FAR, ORDER = range(6)


def swap(block, axis, bits):
    return lax.ppermute(block, axis, [(i, i ^ bits) for i in range(lax.axis_size(axis))])


def nn(a, b):
    return lax.dot_general(a, b, (((1,), (0,)), ((), ())), preferred_element_type=F32)


def nt(a, b):
    return lax.dot_general(a, b, (((1,), (1,)), ((), ())), preferred_element_type=F32)


def tn(a, b):
    return lax.dot_general(a, b, (((0,), (0,)), ((), ())), preferred_element_type=F32)


def call(kernel, scalars, ins, outs, scratch=(), mib=16, us=0):
    vmem = pl.BlockSpec(memory_space=pltpu.VMEM)
    return pl.pallas_call(
        kernel,
        in_specs=[pl.BlockSpec(memory_space=pltpu.SMEM)] + [vmem] * len(ins),
        out_specs=[vmem] * len(outs),
        out_shape=[jax.ShapeDtypeStruct(shape, dtype) for shape, dtype in outs],
        scratch_shapes=[pltpu.VMEM(shape, dtype) for shape, dtype in scratch],
        compiler_params=pltpu.CompilerParams(vmem_limit_bytes=mib * MIB),
        cost_estimate=pl.CostEstimate(
            flops=1000000 + us * 1150000000, bytes_accessed=10000, transcendentals=0
        ),
    )(scalars, *ins)


def rows_of(index, size):
    return pl.ds(pl.multiple_of(index * size, size), size)


def stacked(first, *rows):
    spare = lax.broadcasted_iota(jnp.int32, (16, first.shape[1]), 0)
    extra = jnp.zeros(spare.shape, F32)
    for i, row in enumerate(rows):
        extra = jnp.where(spare == i, row, extra)
    return jnp.concatenate([first, extra.astype(BF16)], axis=0)


def key_bias(valid, keys):
    place = lax.broadcasted_iota(jnp.int32, (1, keys), 1)
    return jnp.where(place < valid, 0.0, NEG)


def attend_head(coef, q, k, v, bias):
    dim = q.shape[0]
    raw = nn(stacked(k, bias).T, stacked(q, 1.0))
    top = jnp.max(raw, axis=0, keepdims=True)
    terms = jnp.exp2((raw - top) * coef).astype(BF16)
    got = nn(stacked(v, 1.0), terms)
    total = got[dim : dim + 1]
    return (got[:dim] / total).astype(BF16), top * coef + jnp.log2(total)


def attend_head_back(coef, scale, q, k, v, bias, lse, ctx, dctx):
    delta = jnp.sum(dctx.astype(F32) * ctx.astype(F32), axis=0, keepdims=True)
    raw = nn(stacked(k, bias).T, stacked(q, 1.0))
    probs = jnp.exp2(raw * coef - lse)
    draw = (probs * (nn(v.T, dctx) - delta)).astype(BF16)
    dv = nt(dctx, probs.astype(BF16)).astype(BF16)
    dk = (nt(q, draw) * scale).astype(BF16)
    dq = (nn(k, draw) * scale).astype(BF16)
    return dq, dk, dv


def norm_stats(hidden):
    mean = jnp.mean(hidden, axis=-1, keepdims=True)
    centred = hidden - mean
    var = jnp.mean(centred * centred, axis=-1, keepdims=True)
    inv = lax.rsqrt(var + EPS)
    return centred * inv, inv


def norm_back(grad, gain, hat, inv):
    scaled = grad * gain
    shift = jnp.mean(scaled, axis=-1, keepdims=True)
    slope = jnp.mean(scaled * hat, axis=-1, keepdims=True)
    back = inv * (scaled - shift - hat * slope)
    return back, jnp.sum(grad * hat, axis=0, keepdims=True), jnp.sum(grad, axis=0, keepdims=True)


def by_core(mat, core, lines):
    span = mat.shape[1] // (2 * lines)
    halves = [
        jnp.concatenate(
            [mat[:, (2 * z + p) * span : (2 * z + p + 1) * span] for z in range(lines)], axis=1
        )
        for p in range(2)
    ]
    even = core == 0
    return jnp.where(even, halves[0], halves[1]), jnp.where(even, halves[1], halves[0])


def rows_by_core(ref, core, lines):
    span = ref.shape[0] // (2 * lines)
    return [
        jnp.concatenate([ref[rows_of(2 * z + (core ^ which), span), :] for z in range(lines)], axis=0)
        for which in range(2)
    ]


def near_kernel(heads, lines, s_ref, x_ref, w_ref, qkv_ref, ctx_ref, lse_ref, *rest):
    width = x_ref.shape[1]
    dim = width // heads
    coef = LOG2E / math.sqrt(dim)
    turned = x_ref[...].T
    for part in range(3):
        at = slice(part * width, (part + 1) * width)
        qkv_ref[at, :] = tn(w_ref[:, at], turned).astype(BF16)
    if lines:
        rest[0][0], rest[0][1] = by_core(x_ref[...], s_ref[CORE], lines)
    bias = key_bias(s_ref[NEAR], x_ref.shape[0])

    def one(i, carry):
        head = s_ref[ORDER + i]
        at = rows_of(head, dim)
        ctx_ref[at, :], lse_ref[head] = attend_head(
            coef,
            qkv_ref[at, :],
            qkv_ref[rows_of(heads + head, dim), :],
            qkv_ref[rows_of(2 * heads + head, dim), :],
            bias,
        )
        return carry

    lax.fori_loop(0, heads // 2, one, 0, unroll=3)


def ffn_kernel(
    heads, blks, lines, s_ref, x_ref, xp_ref, w_ref, qkv_ref, near_ref, wo_ref, gain1_ref,
    bias1_ref, gain2_ref, bias2_ref, dout_ref, wu_ref, wd_ref,
    kv_ref, ctx_ref, lse_ref, hid_ref, slope_ref, dtwo_ref, upt_ref, resid_ref, gains_ref, *rest,
):
    act_ref = rest[-1]
    rows, width = x_ref.shape
    dim = width // heads
    coef = LOG2E / math.sqrt(dim)
    me, core = s_ref[ME], s_ref[CORE]
    turned = xp_ref[...].T
    for part in range(2):
        at = slice((part + 1) * width, (part + 2) * width)
        kv_ref[part * width : (part + 1) * width, :] = tn(w_ref[:, at], turned).astype(BF16)
    bias = key_bias(s_ref[FAR], rows)

    def one(i, carry):
        head = s_ref[ORDER + heads // 2 + i]
        at = rows_of(head, dim)
        ctx_ref[at, :], lse_ref[head] = attend_head(
            coef, qkv_ref[at, :], kv_ref[at, :], kv_ref[rows_of(heads + head, dim), :], bias
        )
        mine = rows_of(s_ref[ORDER + i], dim)
        ctx_ref[mine, :] = near_ref[mine, :]
        return carry

    lax.fori_loop(0, heads // 2, one, 0, unroll=3)

    resid = x_ref[...].astype(F32) + tn(ctx_ref[...], wo_ref[...])
    resid_ref[...] = resid
    hat, _ = norm_stats(resid)
    one_in = hat * gain1_ref[...] + bias1_ref[...]
    low = one_in.astype(BF16)
    upt_ref[...] = low.T
    total = one_in
    blk = wu_ref.shape[1] // FF_BLOCKS
    for j in range(FF_BLOCKS):
        at = slice(j * blk, (j + 1) * blk)
        pre = nn(low, wu_ref[:, at])
        cdf = 0.5 + 0.5 * lax.erf(pre * math.sqrt(0.5))
        pdf = jnp.exp2(pre * pre * (-0.5 * LOG2E)) * (1.0 / math.sqrt(2.0 * math.pi))
        slope_ref[:, at] = (cdf + pre * pdf).astype(BF16)
        act = (pre * cdf).astype(BF16)
        act_ref[:, at] = act
        total = total + nn(act, wd_ref[at, :])
    hat, inv = norm_stats(total)
    hid_ref[...] = (hat * gain2_ref[...] + bias2_ref[...]).astype(BF16)
    back, gain, shift = norm_back(dout_ref[...].astype(F32), gain2_ref[...], hat, inv)
    dtwo_ref[...] = back
    gains_ref[0:1, :] = gain
    gains_ref[1:2, :] = shift
    turned = back.astype(BF16).T
    if lines:
        high = width // blks
        span = act_ref.shape[1] // (2 * lines)
        for which in (1, 0):
            for z in range(lines):
                prod = nn(turned, act_ref[:, rows_of(2 * z + (core ^ which), span)]).astype(BF16)
                for k in range(blks):
                    rest[which][k ^ me, :, z * span : (z + 1) * span] = prod[
                        k * high : (k + 1) * high
                    ]
        rest[2][0], rest[2][1] = by_core(xp_ref[...], core, lines)
    else:
        rest[0][...] = nn(turned, act_ref[...]).astype(BF16)


def pre_back_kernel(s_ref, dtwo_ref, slope_ref, wd_ref, wu_ref, dpre_ref, done_ref):
    low = dtwo_ref[...].astype(BF16)
    total = dtwo_ref[...]
    blk = wu_ref.shape[1] // FF_BLOCKS
    for j in range(FF_BLOCKS):
        at = slice(j * blk, (j + 1) * blk)
        dpre = (nt(low, wd_ref[at, :]) * slope_ref[:, at].astype(F32)).astype(BF16)
        dpre_ref[:, at] = dpre
        total = total + nt(dpre, wu_ref[:, at])
    done_ref[...] = total


def norm_back_kernel(
    blks, lines, s_ref, dpre_ref, done_ref, upt_ref, resid_ref, gain1_ref, gains_ref, wo_ref,
    ctx_ref, dres_ref, dctx_ref, *outs,
):
    me, core = s_ref[ME], s_ref[CORE]
    hat, inv = norm_stats(resid_ref[...])
    back, gain, shift = norm_back(done_ref[...], gain1_ref[...], hat, inv)
    dres_ref[...] = back
    turned = back.astype(BF16).T
    dctx_ref[...] = nn(wo_ref[...], turned).astype(BF16)
    row = lax.broadcasted_iota(jnp.int32, (16, gain.shape[1]), 0)
    sums = jnp.where(row == 0, gain, jnp.where(row == 1, shift, 0.0))
    sums = jnp.where(row == 2, gains_ref[0:1, :], sums)
    sums = jnp.where(row == 3, gains_ref[1:2, :], sums).astype(BF16)
    if not lines:
        outs[0][...] = nn(upt_ref[...], dpre_ref[...]).astype(BF16)
        outs[1][...] = nt(turned, ctx_ref[...]).astype(BF16)
        outs[2][...] = sums
        return
    keep_ref, sends = outs[0], outs[1:]
    ups = rows_by_core(upt_ref, core, lines)
    ctxs = rows_by_core(ctx_ref, core, lines)
    sums = by_core(sums, core, lines)
    wide = dpre_ref.shape[1] // blks
    half = ups[0].shape[0]
    high = turned.shape[0] // blks
    pieces = wide // half
    def store(which, k, first, part):
        if not which:
            keep_ref[k ^ me, first : first + part.shape[0], :] = part
            return
        start = 0
        for send in sends:
            end = start + send.shape[1]
            low, up = max(first, start), min(first + part.shape[0], end)
            if low < up:
                send[k ^ me, low - start : up - start, :] = part[low - first : up - first]
            start = end

    for which in (1, 0):
        for k in range(blks):
            prod = nn(ups[which], dpre_ref[:, k * wide : (k + 1) * wide]).astype(BF16)
            for p in range(pieces):
                store(which, k, p * half, prod[:, p * half : (p + 1) * half])
        prod = nt(turned, ctxs[which]).astype(BF16)
        for k in range(blks):
            store(which, k, wide, prod[k * high : (k + 1) * high])
            store(which, k, wide + high, sums[which])


def far_back_kernel(
    heads, s_ref, qkv_ref, kv_ref, ctx_ref, dctx_ref, lse_ref, w_ref, dq_ref, dkv_ref, give_ref,
    rest_ref, wide_ref,
):
    width, rows = ctx_ref.shape
    dim = width // heads
    half = heads // 2
    scale = 1.0 / math.sqrt(dim)
    bias = key_bias(s_ref[FAR], rows)
    wide_ref[...] = jnp.zeros_like(wide_ref)

    def one(i, carry):
        head = s_ref[ORDER + half + i]
        at, low = rows_of(head, dim), rows_of(heads + head, dim)
        dq, dk, dv = attend_head_back(
            LOG2E * scale, scale, qkv_ref[at, :], kv_ref[at, :], kv_ref[low, :], bias,
            lse_ref[head], ctx_ref[at, :], dctx_ref[at, :],
        )
        dq_ref[rows_of(i, dim), :] = dq
        dkv_ref[rows_of(i, dim), :] = dk
        dkv_ref[rows_of(half + i, dim), :] = dv
        wide_ref[at, :] = dk
        wide_ref[low, :] = dv
        return carry

    lax.fori_loop(0, half, one, 0, unroll=3)
    give = nn(w_ref[:, width:], wide_ref[...]).astype(BF16)
    give_ref[...] = give[: give_ref.shape[0]]
    rest_ref[...] = give[give_ref.shape[0] :]


def near_back_kernel(
    heads, blks, lines, s_ref, qkv_ref, ctx_ref, dctx_ref, lse_ref, farq_ref, farkv_ref, x_ref,
    xp_ref, dqkv_ref, *rest,
):
    outs, near_ref = rest[:-1], rest[-1]
    width, rows = ctx_ref.shape
    dim = width // heads
    half = heads // 2
    scale = 1.0 / math.sqrt(dim)
    bias = key_bias(s_ref[NEAR], rows)
    me = s_ref[ME]
    dqkv_ref[width:, :] = jnp.zeros((2 * width, rows), BF16)

    def one(i, carry):
        head = s_ref[ORDER + i]
        at = rows_of(head, dim)
        key, value = rows_of(heads + head, dim), rows_of(2 * heads + head, dim)
        dq, dk, dv = attend_head_back(
            LOG2E * scale, scale, qkv_ref[at, :], qkv_ref[key, :], qkv_ref[value, :], bias,
            lse_ref[head], ctx_ref[at, :], dctx_ref[at, :],
        )
        dqkv_ref[at, :] = dq
        dqkv_ref[key, :] = dk
        dqkv_ref[value, :] = dv
        near_ref[rows_of(i, dim), :] = dk
        near_ref[rows_of(half + i, dim), :] = dv
        dqkv_ref[rows_of(s_ref[ORDER + half + i], dim), :] = farq_ref[rows_of(i, dim), :]
        return carry

    lax.fori_loop(0, half, one, 0, unroll=3)
    per = 3 * heads // blks

    def store(which, unit, prod):
        at = ((unit // per) ^ me, rows_of(unit % per, dim), EVERY)
        if not lines:
            outs[0][rows_of(unit, dim), :] = prod
        elif which:
            for i, out in enumerate(outs[1:]):
                out[at] = prod[:, i * 128 : (i + 1) * 128]
        else:
            outs[0][at] = prod

    for which in (1, 0) if lines else (0,):
        x = x_ref[which] if lines else x_ref[...]
        xp = xp_ref[which] if lines else xp_ref[...]
        prod = nn(dqkv_ref[:width, :], x).astype(BF16)
        for h in range(heads):
            store(which, h, prod[h * dim : (h + 1) * dim])
        for first, grads, inputs in ((0, near_ref, x), (half, farkv_ref, xp)):
            prod = nn(grads[...], inputs).astype(BF16)
            for i in range(half):
                head = s_ref[ORDER + first + i]
                store(which, heads + head, prod[i * dim : (i + 1) * dim])
                low = (half + i) * dim
                store(which, 2 * heads + head, prod[low : low + dim])


def through_kernel(s_ref, w_ref, dqkv_ref, own_ref):
    own_ref[...] = nn(w_ref[...], dqkv_ref[...])


def input_kernel(s_ref, own_ref, got_ref, rest_ref, dres_ref, out_ref):
    cut = got_ref.shape[0]
    for at, got in ((slice(0, cut), got_ref), (slice(cut, None), rest_ref)):
        total = own_ref[at, :] + got[...].astype(F32)
        out_ref[:, at] = (total.T + dres_ref[:, at]).astype(BF16)


def add_up(*parts):
    total = parts[0].astype(F32)
    for part in parts[1:]:
        total = total + part.astype(F32)
    return total


def after(scalars, *arrays):
    return lax.optimization_barrier((scalars,) + arrays)[0]


def block_at(ref, at):
    at = tuple(at) + (EVERY,) * (len(ref.shape) - len(at))
    first, last, _ = at[-2].indices(ref.shape[-2])
    return at[:-2], first, last - first, at[-1]


def sums_kernel(plan, lines, inputs, s_ref, *refs):
    ins, outs = refs[:inputs], refs[inputs:]

    def run(odd, upper):
        for terms, targets in plan(odd, upper) if lines else plan():
            found = [(ins[i],) + block_at(ins[i], src) for i, src in terms]
            places = [(outs[out],) + block_at(outs[out], dst) + (part,) for out, dst, part in targets]
            rows = found[0][3]

            def add(at, size):
                total = add_up(
                    *(ref[leads + (pl.ds(at + row, size), col)] for ref, leads, row, _, col in found)
                ).astype(BF16)
                for ref, leads, row, _, col, part in places:
                    ref[leads + (pl.ds(at + row, size), col)] = total[:, part]

            def body(i, carry):
                add(pl.multiple_of(i * STEP, STEP), STEP)
                return carry

            if rows >= 2 * STEP:
                lax.fori_loop(0, rows // STEP, body, 0)
                if rows % STEP:
                    add(rows // STEP * STEP, rows % STEP)
            else:
                add(0, rows)

    if lines:
        line = s_ref[LINE]
        for odd in range(2):
            pl.when(line % 2 == odd)(functools.partial(run, odd, line // 2))
    else:
        run(0, 0)


def sums(scalars, ins, shapes, plan, lines=False):
    kernel = functools.partial(sums_kernel, plan, lines, len(ins))
    return call(kernel, scalars, ins, [(shape, BF16) for shape in shapes], mib=4)


def span_of(index, size):
    return slice(index * size, (index + 1) * size)


def by_line(z, odd, upper):
    return (z % 2) ^ odd, (z // 2) ^ upper


class Halves:
    def __init__(self, cut, rows, cols):
        self.cut, self.rows, self.cols = cut, rows, cols
        self.sizes = (cut, rows - cut)
        self.at = (slice(0, cut), slice(cut, rows))

    def first(self, s, keep, gots, cuts):
        shapes = [(2, size, self.cols) for size in self.sizes for _ in range(2)]
        picks = ((0, 0, (0, 2)), (1, 0, (1, 3)), (2, 1, (0, 1)), (3, 1, (2, 3)))

        def plan():
            found = []
            for out, half, group in picks:
                start, end = self.at[half].start, self.at[half].stop
                for i, (first, last) in enumerate(zip(cuts, cuts[1:])):
                    low, up = max(first, start), min(last, end)
                    if low < up:
                        for slot, j in enumerate(group):
                            terms = [(0, (j, slice(low, up), EVERY))]
                            terms.append((1 + i, (j, slice(low - first, up - first), EVERY)))
                            here = (slot, slice(low - start, up - start), EVERY)
                            found.append((terms, [(out, here, EVERY)]))
            return found

        return sums(s, (keep,) + tuple(gots), shapes, plan)

    def second(self, s, chip):
        got = (swap(chip[1], "blk", 1), swap(chip[3], "blk", 2))
        shapes = [(size, self.cols) for size in self.sizes for _ in range(2)]

        def plan():
            return [
                ([(half, (slot,)), (2 + half, (slot,))], [(2 * half + slot, (EVERY,), EVERY)])
                for half in range(2)
                for slot in range(2)
            ]

        return sums(s, (chip[0], chip[2]) + got, shapes, plan)

    def third(self, s, pair, wide, size, lines):
        got = (swap(pair[1], "blk", 2), swap(pair[3], "blk", 1))
        half = self.cols
        shape = (self.rows - wide, half + 128)

        def plan(odd, upper):
            found = []
            for p in range(wide // half):
                for z in range(lines):
                    row = p * half + z * size
                    which = int(row >= self.cut)
                    row -= which * self.cut
                    out, slot = by_line(z, odd, upper)
                    src = (slice(row, row + size), EVERY)
                    dst = (slot, span_of(p, size), slice(0, half))
                    found.append(([(which, src), (2 + which, src)], [(out, dst, EVERY)]))
            src = (slice(wide - self.cut, None), EVERY)
            targets = []
            for z in range(lines):
                out, slot = by_line(z, odd, upper)
                targets.append((out, (slot, EVERY, slice(half, half + size)), span_of(z, size)))
            return found + [([(1, src), (3, src)], targets)]

        return sums(s, (pair[0], pair[2]) + got, [(2,) + shape] * 2, plan, True)


def proj_first(s, keep, gots):
    blks, rows, cols = keep.shape

    def plan():
        return [
            ([(0, (j, EVERY, span_of(i, 128))), (1 + i, (j,))], [(j, (EVERY, span_of(i, 128)), EVERY)])
            for j in range(blks)
            for i in range(len(gots))
        ]

    return sums(s, (keep,) + tuple(gots), [(rows, cols)] * blks, plan)


def proj_second(s, chip, lines):
    parts = [chip[0]] + [swap(chip[i], "blk", i) for i in range(1, len(chip))]
    rows, cols = chip[0].shape
    size = cols // lines

    def plan(odd, upper):
        targets = []
        for z in range(lines):
            out, slot = by_line(z, odd, upper)
            targets.append((out, (slot,), span_of(z, size)))
        return [([(i, (EVERY,)) for i in range(len(parts))], targets)]

    return sums(s, parts, [(2, rows, size)] * 2, plan, True)


def fourth(s, mine):
    return paired(s, mine[0], swap(mine[1], "batch", 2))


def dealt(s, keep, got):
    def plan():
        return [
            ([(i, (2 * out + slot,)) for i in range(2)], [(out, (slot,), EVERY)])
            for out in range(2)
            for slot in range(2)
        ]

    return sums(s, (keep, got), [(2,) + keep.shape[1:]] * 2, plan)


def paired(s, keep, got):
    def plan():
        return [([(0, (i,)), (1, (i,))], [(i, (EVERY,), EVERY)]) for i in range(2)]

    return sums(s, (keep, got), [keep.shape[1:]] * 2, plan)


def down_first(s, keep, got, lines):
    blks, high, cols = keep.shape
    size = cols // lines

    def plan(odd, upper):
        found = []
        for z in range(lines):
            out, slot = by_line(z, odd, upper)
            for j in range(blks):
                src = (j, EVERY, span_of(z, size))
                found.append(([(0, src), (1, src)], [(out, (slot, j), EVERY)]))
        return found

    return sums(s, (keep, got), [(2, blks, high, size)] * 2, plan, True)


def down_final_kernel(s_ref, *refs):
    refs[-1][...] = add_up(*(ref[...] for ref in refs[:-1]))


def turned_final_kernel(s_ref, *refs):
    refs[-1][...] = add_up(*(ref[...] for ref in refs[:-1])).T


def up_final_kernel(high, half, size, s_ref, *refs):
    up_ref, out_ref, sums_ref = refs[-3:]
    total = add_up(*(ref[...] for ref in refs[:-3]))
    for p in range(high // size):
        up_ref[:, span_of(p, half)] = total[span_of(p, size), :half]
    out_ref[...] = total[:high, half : half + size].T
    sums_ref[...] = total[high : high + 8, half:]


def reduce_any(mats, thin=None):
    blks = lax.axis_size("blk")
    lines = lax.axis_size("batch") // 2
    me = lax.axis_index("blk")
    core = lax.axis_index("batch") % 2
    line = lax.axis_index("batch") // 2
    pieces = []
    for mat in mats:
        rows = mat.shape[0] // (2 * lines)
        pieces.append(mat.reshape(lines, 2, rows, blks, -1))
    if thin is not None:
        thin = thin.reshape(lines, 2, rows, 1, -1)
        pieces.append(jnp.broadcast_to(thin, thin.shape[:3] + (blks,) + thin.shape[4:]))
    every = jnp.concatenate(pieces, axis=4)

    def half(which, distance):
        part = lax.dynamic_index_in_dim(every, which, 1, keepdims=False)
        return lax.dynamic_index_in_dim(part, me ^ distance, 2, keepdims=False)

    keep = [half(core, distance) for distance in range(blks)]
    got = swap(jnp.stack([half(1 - core, i) for i in range(blks)]), "batch", 1)
    chip = [add_up(part, got[i]).astype(BF16) for i, part in enumerate(keep)]
    total = add_up(chip[0], *(swap(chip[i], "blk", i) for i in range(1, blks)))
    while lines > 1:
        lines //= 2
        upper = line // lines
        pairs = total.astype(BF16).reshape((2, lines) + total.shape[1:])
        mine = lax.dynamic_index_in_dim(pairs, upper, 0, keepdims=False)
        theirs = lax.dynamic_index_in_dim(pairs, 1 - upper, 0, keepdims=False)
        total = add_up(mine, swap(theirs, "batch", 2 * lines))
        line = line % lines
    return total[0]


def shards(
    hidden_in, lengths, head_order, w_qkv, w_out, ln1_gain, ln1_bias, w_up, w_down, ln2_gain,
    ln2_bias, grad_out,
):
    _, _, rows, width = hidden_in.shape
    heads = head_order.shape[0]
    blks = lax.axis_size("blk")
    batch = lax.axis_size("batch")
    inner = w_up.shape[1]
    me = lax.axis_index("blk")
    at = lax.axis_index("batch")
    fast = batch == 8 and blks == 4 and width % (16 * batch) == 0
    lines = batch // 2 if fast else 0
    wide = inner // blks
    size = width // batch
    half = width // 2
    high = width // blks
    cols = 3 * width // blks

    x = hidden_in.reshape(rows, width)
    dout = grad_out.reshape(rows, width)
    xp = swap(x, "blk", 1)
    gain1, bias1, gain2, bias2 = (
        part.reshape(1, width) for part in (ln1_gain, ln1_bias, ln2_gain, ln2_bias)
    )
    length = lax.dynamic_index_in_dim(lengths[:, 0], me // 2, 0, keepdims=False)
    ids = jnp.arange(heads, dtype=jnp.int32)
    order = jnp.sum(jnp.where(head_order[None, :] == ids[:, None], ids[None, :], 0), axis=1)
    parts = [me, at % 2, at // 2, length - rows * (me % 2), length - rows * (1 - me % 2)]
    s = jnp.concatenate([jnp.stack(parts).astype(jnp.int32), order.astype(jnp.int32)])

    square = ((width, rows), BF16)
    lse = ((heads, 1, rows), F32)
    split = [((2, rows, width // 2), BF16)] if lines else []
    qkv, near_ctx, near_lse, *x_parts = call(
        functools.partial(near_kernel, heads, lines), s, (x, w_qkv),
        [((3 * width, rows), BF16), square, lse] + split, mib=8, us=8,
    )

    if lines:
        down_out = [((blks, high, inner // 2), BF16)] * 2 + split
    else:
        down_out = [((width, inner), BF16)]
    kv, ctx, far_lse, hid, slope, dtwo, upt, resid, gains, *down = call(
        functools.partial(ffn_kernel, heads, blks, lines), s,
        (x, xp, w_qkv, qkv, near_ctx, w_out, gain1, bias1, gain2, bias2, dout, w_up, w_down),
        [((2 * width, rows), BF16), square, lse, ((rows, width), BF16), ((rows, inner), BF16),
         ((rows, width), F32), square, ((rows, width), F32), ((8, width), F32)] + down_out,
        [((rows, inner), BF16)], mib=16, us=18,
    )

    s = after(s, dtwo)
    dpre, done = call(
        pre_back_kernel, s, (dtwo, slope, w_down, w_up),
        [((rows, inner), BF16), ((rows, width), F32)], mib=8,
    )
    s = after(s, done)
    if lines:
        ups = Halves(half + size, wide + high + 16, half)
        cuts = [ups.rows // UP_PARTS // 16 * 16 * i for i in range(UP_PARTS)] + [ups.rows]
        up_out = [((blks, wide + high + 16, half), BF16)]
        up_out += [((blks, last - first, half), BF16) for first, last in zip(cuts, cuts[1:])]
        proj_out = [((blks, cols, half), BF16)] + [((blks, cols, 128), BF16)] * (half // 128)
    else:
        up_out = [((width, inner), BF16), ((width, width), BF16), ((16, width), BF16)]
        proj_out = [((3 * width, width), BF16)]
    dres, dctx, *up = call(
        functools.partial(norm_back_kernel, blks, lines), s,
        (dpre, done, upt, resid, gain1, gains, w_out, ctx),
        [((rows, width), F32), square] + up_out, mib=8,
    )
    s = after(s, dctx)
    if lines:
        chip1 = down_first(s, down[0], swap(down[1], "batch", 1), lines)
        s = after(s, chip1[0])
        chip2 = ups.first(s, up[0], [swap(part, "batch", 1) for part in up[1:]], cuts)
        s = after(s, chip2[0])
    far_q, far_kv, *give = call(
        functools.partial(far_back_kernel, heads), s, (qkv, kv, ctx, dctx, far_lse, w_qkv),
        [((width // 2, rows), BF16), square, ((width - 128, rows), BF16), ((128, rows), BF16)],
        [((2 * width, rows), BF16)], mib=8,
    )
    s = after(s, far_q)
    if not lines:
        got_in = [swap(part, "blk", 1) for part in give]
    dqkv, *proj = call(
        functools.partial(near_back_kernel, heads, blks, lines), s,
        (qkv, ctx, dctx, near_lse, far_q, far_kv)
        + ((x_parts[0], down[2]) if lines else (x, xp)),
        [((3 * width, rows), BF16)] + proj_out, [square], mib=8,
    )
    s = after(s, dqkv)
    if lines:
        pair2 = ups.second(s, chip2)
        s = after(s, pair2[0])
        got_in = [swap(part, "blk", 1) for part in lax.optimization_barrier((pair2[0], *give))[1:]]
        line1 = fourth(s, chip1)
        s = after(s, line1[0])
        chip3 = proj_first(s, proj[0], [swap(part, "batch", 1) for part in proj[1:]])
        s = after(s, chip3[0])
        line2 = ups.third(s, pair2, wide, size, lines)
        s = after(s, line2[0])
        far1 = dealt(s, line1[0], swap(line1[1], "batch", 4))
        s = after(s, far1[0])
    (own,) = call(through_kernel, s, (w_qkv, dqkv), [((width, rows), F32)], mib=4)
    s = after(s, own)
    if lines:
        line3 = proj_second(s, chip3, lines)
        s = after(s, line3[0])
        last2 = fourth(s, line2)
        s = after(s, last2[0])
        last1 = paired(s, far1[0], swap(far1[1], "blk", 2))
        s = after(s, last1[0])
        last3 = fourth(s, line3)
        s = after(s, last3[0])
        (own_down,) = call(
            down_final_kernel, s, (last1[0], swap(last1[1], "blk", 1)),
            [((high, inner // batch), F32)], mib=4,
        )
        s = after(s, own_down)
        own_down = own_down.T
        own_up, own_out, thin = call(
            functools.partial(up_final_kernel, high, half, size), s,
            (last2[0], swap(last2[1], "batch", 4)),
            [((size, wide), F32), ((size, high), F32), ((8, 128), F32)], mib=4,
        )
        thin = thin[:4, :size]
        s = after(s, own_up)
    (grad_in,) = call(input_kernel, s, (own, *got_in, dres), [((rows, width), BF16)], mib=4)
    if lines:
        s = after(s, grad_in)
        (own_qkv,) = call(
            turned_final_kernel, s, (last3[0], swap(last3[1], "batch", 4)),
            [((size, cols), F32)], mib=4,
        )
    else:
        own_down = reduce_any([down[0].T])
        both = reduce_any([up[0], up[1].T], up[2][:4].T)
        own_up, own_out, thin = both[:, :wide], both[:, wide : wide + high], both[:, wide + high :].T
        own_qkv = reduce_any([proj[0].T])
    return (
        hid.reshape(hidden_in.shape),
        grad_in.reshape(hidden_in.shape),
        own_qkv,
        own_out,
        thin[0],
        thin[1],
        own_up,
        own_down,
        thin[2],
        thin[3],
    )


def solution(mesh):
    rows = P("blk", "batch", None, None)
    both = P("batch", "blk")
    return jax.shard_map(
        shards,
        mesh=mesh,
        in_specs=(rows, P(None, "batch")) + (P(),) * 9 + (rows,),
        out_specs=(rows, rows, both, both, P("batch"), P("batch"), both, both)
        + (P("batch"), P("batch")),
        check_vma=False,
    )
```

```python
import functools
import math

import jax
import jax.numpy as jnp
from jax import lax
from jax.experimental import pallas as pl
from jax.experimental.pallas import tpu as pltpu
from jax.sharding import PartitionSpec as P

F32 = jnp.float32
BF16 = jnp.bfloat16
MIB = 1 << 20
EPS = 1e-06
NEG = -1e30
LOG2E = math.log2(math.e)
FF_BLOCKS = 4
STEP = 48
EVERY = slice(None)
ME, CORE, LINE, NEAR, FAR, ORDER = range(6)


def swap(block, axis, bits):
    return lax.ppermute(block, axis, [(i, i ^ bits) for i in range(lax.axis_size(axis))])


def nn(a, b):
    return lax.dot_general(a, b, (((1,), (0,)), ((), ())), preferred_element_type=F32)


def nt(a, b):
    return lax.dot_general(a, b, (((1,), (1,)), ((), ())), preferred_element_type=F32)


def tn(a, b):
    return lax.dot_general(a, b, (((0,), (0,)), ((), ())), preferred_element_type=F32)


def call(kernel, scalars, ins, outs, scratch=(), mib=16, us=0):
    vmem = pl.BlockSpec(memory_space=pltpu.VMEM)
    return pl.pallas_call(
        kernel,
        in_specs=[pl.BlockSpec(memory_space=pltpu.SMEM)] + [vmem] * len(ins),
        out_specs=[vmem] * len(outs),
        out_shape=[jax.ShapeDtypeStruct(shape, dtype) for shape, dtype in outs],
        scratch_shapes=[pltpu.VMEM(shape, dtype) for shape, dtype in scratch],
        compiler_params=pltpu.CompilerParams(vmem_limit_bytes=mib * MIB),
        cost_estimate=pl.CostEstimate(
            flops=1000000 + us * 1150000000, bytes_accessed=10000, transcendentals=0
        ),
    )(scalars, *ins)


def rows_of(index, size):
    return pl.ds(pl.multiple_of(index * size, size), size)


def stacked(first, *rows):
    spare = lax.broadcasted_iota(jnp.int32, (16, first.shape[1]), 0)
    extra = jnp.zeros(spare.shape, F32)
    for i, row in enumerate(rows):
        extra = jnp.where(spare == i, row, extra)
    return jnp.concatenate([first, extra.astype(BF16)], axis=0)


def key_bias(valid, keys):
    place = lax.broadcasted_iota(jnp.int32, (1, keys), 1)
    return jnp.where(place < valid, 0.0, NEG)


def attend_head(coef, q, k, v, bias):
    dim = q.shape[0]
    raw = nn(stacked(k, bias).T, stacked(q, 1.0))
    top = jnp.max(raw, axis=0, keepdims=True)
    terms = jnp.exp2((raw - top) * coef).astype(BF16)
    got = nn(stacked(v, 1.0), terms)
    total = got[dim : dim + 1]
    return (got[:dim] / total).astype(BF16), top * coef + jnp.log2(total)


def attend_head_back(coef, scale, q, k, v, bias, lse, ctx, dctx):
    delta = jnp.sum(dctx.astype(F32) * ctx.astype(F32), axis=0, keepdims=True)
    raw = nn(stacked(k, bias).T, stacked(q, 1.0))
    probs = jnp.exp2(raw * coef - lse)
    draw = (probs * (nn(v.T, dctx) - delta)).astype(BF16)
    dv = nt(dctx, probs.astype(BF16)).astype(BF16)
    dk = (nt(q, draw) * scale).astype(BF16)
    dq = (nn(k, draw) * scale).astype(BF16)
    return dq, dk, dv


def norm_stats(hidden):
    mean = jnp.mean(hidden, axis=-1, keepdims=True)
    centred = hidden - mean
    var = jnp.mean(centred * centred, axis=-1, keepdims=True)
    inv = lax.rsqrt(var + EPS)
    return centred * inv, inv


def norm_back(grad, gain, hat, inv):
    scaled = grad * gain
    shift = jnp.mean(scaled, axis=-1, keepdims=True)
    slope = jnp.mean(scaled * hat, axis=-1, keepdims=True)
    back = inv * (scaled - shift - hat * slope)
    return back, jnp.sum(grad * hat, axis=0, keepdims=True), jnp.sum(grad, axis=0, keepdims=True)


def by_core(mat, core, lines):
    span = mat.shape[1] // (2 * lines)
    halves = [
        jnp.concatenate(
            [mat[:, (2 * z + p) * span : (2 * z + p + 1) * span] for z in range(lines)], axis=1
        )
        for p in range(2)
    ]
    even = core == 0
    return jnp.where(even, halves[0], halves[1]), jnp.where(even, halves[1], halves[0])


def rows_by_core(ref, core, lines):
    span = ref.shape[0] // (2 * lines)
    return [
        jnp.concatenate([ref[rows_of(2 * z + (core ^ which), span), :] for z in range(lines)], axis=0)
        for which in range(2)
    ]


def near_kernel(heads, lines, s_ref, x_ref, w_ref, qkv_ref, ctx_ref, lse_ref, *rest):
    width = x_ref.shape[1]
    dim = width // heads
    coef = LOG2E / math.sqrt(dim)
    turned = x_ref[...].T
    for part in range(3):
        at = slice(part * width, (part + 1) * width)
        qkv_ref[at, :] = tn(w_ref[:, at], turned).astype(BF16)
    if lines:
        rest[0][0], rest[0][1] = by_core(x_ref[...], s_ref[CORE], lines)
    bias = key_bias(s_ref[NEAR], x_ref.shape[0])

    def one(i, carry):
        head = s_ref[ORDER + i]
        at = rows_of(head, dim)
        ctx_ref[at, :], lse_ref[head] = attend_head(
            coef,
            qkv_ref[at, :],
            qkv_ref[rows_of(heads + head, dim), :],
            qkv_ref[rows_of(2 * heads + head, dim), :],
            bias,
        )
        return carry

    lax.fori_loop(0, heads // 2, one, 0, unroll=3)


def ffn_kernel(
    heads, blks, lines, s_ref, x_ref, xp_ref, w_ref, qkv_ref, near_ref, wo_ref, gain1_ref,
    bias1_ref, gain2_ref, bias2_ref, dout_ref, wu_ref, wd_ref,
    kv_ref, ctx_ref, lse_ref, hid_ref, slope_ref, dtwo_ref, upt_ref, resid_ref, gains_ref, *rest,
):
    act_ref = rest[-1]
    rows, width = x_ref.shape
    dim = width // heads
    coef = LOG2E / math.sqrt(dim)
    me, core = s_ref[ME], s_ref[CORE]
    turned = xp_ref[...].T
    for part in range(2):
        at = slice((part + 1) * width, (part + 2) * width)
        kv_ref[part * width : (part + 1) * width, :] = tn(w_ref[:, at], turned).astype(BF16)
    bias = key_bias(s_ref[FAR], rows)

    def one(i, carry):
        head = s_ref[ORDER + heads // 2 + i]
        at = rows_of(head, dim)
        ctx_ref[at, :], lse_ref[head] = attend_head(
            coef, qkv_ref[at, :], kv_ref[at, :], kv_ref[rows_of(heads + head, dim), :], bias
        )
        mine = rows_of(s_ref[ORDER + i], dim)
        ctx_ref[mine, :] = near_ref[mine, :]
        return carry

    lax.fori_loop(0, heads // 2, one, 0, unroll=3)

    resid = x_ref[...].astype(F32) + tn(ctx_ref[...], wo_ref[...])
    resid_ref[...] = resid
    hat, _ = norm_stats(resid)
    one_in = hat * gain1_ref[...] + bias1_ref[...]
    low = one_in.astype(BF16)
    upt_ref[...] = low.T
    total = one_in
    blk = wu_ref.shape[1] // FF_BLOCKS
    for j in range(FF_BLOCKS):
        at = slice(j * blk, (j + 1) * blk)
        pre = nn(low, wu_ref[:, at])
        cdf = 0.5 + 0.5 * lax.erf(pre * math.sqrt(0.5))
        pdf = jnp.exp2(pre * pre * (-0.5 * LOG2E)) * (1.0 / math.sqrt(2.0 * math.pi))
        slope_ref[:, at] = (cdf + pre * pdf).astype(BF16)
        act = (pre * cdf).astype(BF16)
        act_ref[:, at] = act
        total = total + nn(act, wd_ref[at, :])
    hat, inv = norm_stats(total)
    hid_ref[...] = (hat * gain2_ref[...] + bias2_ref[...]).astype(BF16)
    back, gain, shift = norm_back(dout_ref[...].astype(F32), gain2_ref[...], hat, inv)
    dtwo_ref[...] = back
    gains_ref[0:1, :] = gain
    gains_ref[1:2, :] = shift
    turned = back.astype(BF16).T
    if lines:
        high = width // blks
        span = act_ref.shape[1] // (2 * lines)
        for which in (1, 0):
            for z in range(0, lines, 2):
                pair = [act_ref[:, rows_of(2 * (z + i) + (core ^ which), span)] for i in range(2)]
                prod = nn(turned, jnp.concatenate(pair, axis=1)).astype(BF16)
                for k in range(blks):
                    rest[which][k ^ me, :, z * span : (z + 2) * span] = prod[
                        k * high : (k + 1) * high
                    ]
        rest[2][0], rest[2][1] = by_core(xp_ref[...], core, lines)
    else:
        rest[0][...] = nn(turned, act_ref[...]).astype(BF16)


def pre_back_kernel(
    blks, lines, s_ref, dtwo_ref, slope_ref, wd_ref, wu_ref, upt_ref, dpre_ref, done_ref, *outs
):
    me, core = s_ref[ME], s_ref[CORE]
    low = dtwo_ref[...].astype(BF16)
    total = dtwo_ref[...]
    blk = wu_ref.shape[1] // blks
    ups = rows_by_core(upt_ref, core, lines) if lines else ()
    for k in range(blks):
        at = slice(k * blk, (k + 1) * blk)
        dpre = (nt(low, wd_ref[at, :]) * slope_ref[:, at].astype(F32)).astype(BF16)
        if not lines:
            dpre_ref[:, at] = dpre
        total = total + nt(dpre, wu_ref[:, at])
        for out, rows in zip(outs, ups):
            prod = nn(rows, dpre).astype(BF16)
            half = prod.shape[0]
            for p in range(blk // half):
                out[k ^ me, p * half : (p + 1) * half, :] = prod[:, p * half : (p + 1) * half]
    done_ref[...] = total
    if not lines:
        outs[0][...] = nn(upt_ref[...], dpre_ref[...]).astype(BF16)


def norm_back_kernel(
    blks, lines, s_ref, done_ref, resid_ref, gain1_ref, gains_ref, wo_ref, ctx_ref, dres_ref,
    dctx_ref, *outs,
):
    me, core = s_ref[ME], s_ref[CORE]
    hat, inv = norm_stats(resid_ref[...])
    back, gain, shift = norm_back(done_ref[...], gain1_ref[...], hat, inv)
    dres_ref[...] = back
    turned = back.astype(BF16).T
    dctx_ref[...] = nn(wo_ref[...], turned).astype(BF16)
    row = lax.broadcasted_iota(jnp.int32, (16, gain.shape[1]), 0)
    sums = jnp.where(row == 0, gain, jnp.where(row == 1, shift, 0.0))
    sums = jnp.where(row == 2, gains_ref[0:1, :], sums)
    sums = jnp.where(row == 3, gains_ref[1:2, :], sums).astype(BF16)
    if not lines:
        outs[0][...] = nt(turned, ctx_ref[...]).astype(BF16)
        outs[1][...] = sums
        return
    ctxs = rows_by_core(ctx_ref, core, lines)
    sums = by_core(sums, core, lines)
    high = turned.shape[0] // blks
    both = nt(turned, jnp.concatenate(ctxs, axis=0)).astype(BF16)
    half = both.shape[1] // 2
    for which, (out, thin) in enumerate(zip(outs, sums)):
        for k in range(blks):
            out[k ^ me, :high, :] = both[k * high : (k + 1) * high, which * half : (which + 1) * half]
            out[k ^ me, high:, :] = thin


def far_back_kernel(
    heads, s_ref, qkv_ref, kv_ref, ctx_ref, dctx_ref, lse_ref, w_ref, dq_ref, dkv_ref, give_ref,
    rest_ref, wide_ref,
):
    width, rows = ctx_ref.shape
    dim = width // heads
    half = heads // 2
    scale = 1.0 / math.sqrt(dim)
    bias = key_bias(s_ref[FAR], rows)
    wide_ref[...] = jnp.zeros_like(wide_ref)

    def one(i, carry):
        head = s_ref[ORDER + half + i]
        at, low = rows_of(head, dim), rows_of(heads + head, dim)
        dq, dk, dv = attend_head_back(
            LOG2E * scale, scale, qkv_ref[at, :], kv_ref[at, :], kv_ref[low, :], bias,
            lse_ref[head], ctx_ref[at, :], dctx_ref[at, :],
        )
        dq_ref[rows_of(i, dim), :] = dq
        dkv_ref[rows_of(i, dim), :] = dk
        dkv_ref[rows_of(half + i, dim), :] = dv
        wide_ref[at, :] = dk
        wide_ref[low, :] = dv
        return carry

    lax.fori_loop(0, half, one, 0, unroll=3)
    give = nn(w_ref[:, width:], wide_ref[...]).astype(BF16)
    give_ref[...] = give[: give_ref.shape[0]]
    rest_ref[...] = give[give_ref.shape[0] :]


def near_back_kernel(
    heads, blks, lines, s_ref, qkv_ref, ctx_ref, dctx_ref, lse_ref, farq_ref, farkv_ref, x_ref,
    xp_ref, dqkv_ref, *rest,
):
    outs, near_ref = rest[:-1], rest[-1]
    width, rows = ctx_ref.shape
    dim = width // heads
    half = heads // 2
    scale = 1.0 / math.sqrt(dim)
    bias = key_bias(s_ref[NEAR], rows)
    me = s_ref[ME]
    dqkv_ref[width:, :] = jnp.zeros((2 * width, rows), BF16)

    def one(i, carry):
        head = s_ref[ORDER + i]
        at = rows_of(head, dim)
        key, value = rows_of(heads + head, dim), rows_of(2 * heads + head, dim)
        dq, dk, dv = attend_head_back(
            LOG2E * scale, scale, qkv_ref[at, :], qkv_ref[key, :], qkv_ref[value, :], bias,
            lse_ref[head], ctx_ref[at, :], dctx_ref[at, :],
        )
        dqkv_ref[at, :] = dq
        dqkv_ref[key, :] = dk
        dqkv_ref[value, :] = dv
        near_ref[rows_of(i, dim), :] = dk
        near_ref[rows_of(half + i, dim), :] = dv
        dqkv_ref[rows_of(s_ref[ORDER + half + i], dim), :] = farq_ref[rows_of(i, dim), :]
        return carry

    lax.fori_loop(0, half, one, 0, unroll=3)
    per = 3 * heads // blks

    def store(unit, prod):
        if not lines:
            outs[0][rows_of(unit, dim), :] = prod
            return
        at = ((unit // per) ^ me, rows_of(unit % per, dim), EVERY)
        keep = outs[0].shape[2]
        outs[0][at] = prod[:, :keep]
        for i, out in enumerate(outs[1:]):
            out[at] = prod[:, keep + i * 128 : keep + (i + 1) * 128]

    x = jnp.concatenate([x_ref[0], x_ref[1]], axis=1) if lines else x_ref[...]
    xp = jnp.concatenate([xp_ref[0], xp_ref[1]], axis=1) if lines else xp_ref[...]
    prod = nn(dqkv_ref[:width, :], x).astype(BF16)
    for h in range(heads):
        store(h, prod[h * dim : (h + 1) * dim])
    for first, grads, inputs in ((0, near_ref, x), (half, farkv_ref, xp)):
        prod = nn(grads[...], inputs).astype(BF16)
        for i in range(half):
            head = s_ref[ORDER + first + i]
            store(heads + head, prod[i * dim : (i + 1) * dim])
            low = (half + i) * dim
            store(2 * heads + head, prod[low : low + dim])


def through_kernel(s_ref, w_ref, dqkv_ref, own_ref):
    own_ref[...] = nn(w_ref[...], dqkv_ref[...])


def input_kernel(s_ref, own_ref, got_ref, rest_ref, dres_ref, out_ref):
    cut = got_ref.shape[0]
    for at, got in ((slice(0, cut), got_ref), (slice(cut, None), rest_ref)):
        total = own_ref[at, :] + got[...].astype(F32)
        out_ref[:, at] = (total.T + dres_ref[:, at]).astype(BF16)


def add_up(*parts):
    total = parts[0].astype(F32)
    for part in parts[1:]:
        total = total + part.astype(F32)
    return total


def after(scalars, *arrays):
    return lax.optimization_barrier((scalars,) + arrays)[0]


def block_at(ref, at):
    at = tuple(at) + (EVERY,) * (len(ref.shape) - len(at))
    first, last, _ = at[-2].indices(ref.shape[-2])
    return at[:-2], first, last - first, at[-1]


def sums_kernel(plan, lines, inputs, s_ref, *refs):
    ins, outs = refs[:inputs], refs[inputs:]

    def run(odd, upper):
        for terms, targets in plan(odd, upper) if lines else plan():
            found = [(ins[i],) + block_at(ins[i], src) for i, src in terms]
            places = [(outs[out],) + block_at(outs[out], dst) + (part,) for out, dst, part in targets]
            rows = found[0][3]

            def add(at, size):
                total = add_up(
                    *(ref[leads + (pl.ds(at + row, size), col)] for ref, leads, row, _, col in found)
                ).astype(BF16)
                for ref, leads, row, _, col, part in places:
                    ref[leads + (pl.ds(at + row, size), col)] = total[:, part]

            def body(i, carry):
                add(pl.multiple_of(i * STEP, STEP), STEP)
                return carry

            if rows >= 2 * STEP:
                lax.fori_loop(0, rows // STEP, body, 0)
                if rows % STEP:
                    add(rows // STEP * STEP, rows % STEP)
            else:
                add(0, rows)

    if lines:
        line = s_ref[LINE]
        for odd in range(2):
            pl.when(line % 2 == odd)(functools.partial(run, odd, line // 2))
    else:
        run(0, 0)


def sums(scalars, ins, shapes, plan, lines=False):
    kernel = functools.partial(sums_kernel, plan, lines, len(ins))
    return call(kernel, scalars, ins, [(shape, BF16) for shape in shapes], mib=4)


def span_of(index, size):
    return slice(index * size, (index + 1) * size)


def by_line(z, odd, upper):
    return (z % 2) ^ odd, (z // 2) ^ upper


class Halves:
    def __init__(self, cut, rows, cols):
        self.cut, self.rows, self.cols = cut, rows, cols
        self.sizes = (cut, rows - cut)
        self.at = (slice(0, cut), slice(cut, rows))

    def first(self, s, keeps, gots, cuts):
        shapes = [(2, size, self.cols) for size in self.sizes for _ in range(2)]
        picks = ((0, 0, (0, 2)), (1, 0, (1, 3)), (2, 1, (0, 1)), (3, 1, (2, 3)))

        def plan():
            found = []
            for out, half, group in picks:
                start, end = self.at[half].start, self.at[half].stop
                for i, (first, last) in enumerate(zip(cuts, cuts[1:])):
                    low, up = max(first, start), min(last, end)
                    if low < up:
                        for slot, j in enumerate(group):
                            src = (j, slice(low - first, up - first), EVERY)
                            here = (slot, slice(low - start, up - start), EVERY)
                            terms = [(i, src), (len(keeps) + i, src)]
                            found.append((terms, [(out, here, EVERY)]))
            return found

        return sums(s, (*keeps, *gots), shapes, plan)

    def second(self, s, chip):
        got = (swap(chip[1], "blk", 1), swap(chip[3], "blk", 2))
        shapes = [(size, self.cols) for size in self.sizes for _ in range(2)]

        def plan():
            return [
                ([(half, (slot,)), (2 + half, (slot,))], [(2 * half + slot, (EVERY,), EVERY)])
                for half in range(2)
                for slot in range(2)
            ]

        return sums(s, (chip[0], chip[2]) + got, shapes, plan)

    def third(self, s, pair, wide, size, lines):
        got = (swap(pair[1], "blk", 2), swap(pair[3], "blk", 1))
        half = self.cols
        shape = (self.rows - wide, half + 128)

        def plan(odd, upper):
            found = []
            for p in range(wide // half):
                for z in range(lines):
                    row = p * half + z * size
                    which = int(row >= self.cut)
                    row -= which * self.cut
                    out, slot = by_line(z, odd, upper)
                    src = (slice(row, row + size), EVERY)
                    dst = (slot, span_of(p, size), slice(0, half))
                    found.append(([(which, src), (2 + which, src)], [(out, dst, EVERY)]))
            src = (slice(wide - self.cut, None), EVERY)
            targets = []
            for z in range(lines):
                out, slot = by_line(z, odd, upper)
                targets.append((out, (slot, EVERY, slice(half, half + size)), span_of(z, size)))
            return found + [([(1, src), (3, src)], targets)]

        return sums(s, (pair[0], pair[2]) + got, [(2,) + shape] * 2, plan, True)


def proj_first(s, keep, gots):
    blks, rows, cols = keep.shape

    def plan():
        return [
            ([(0, (j, EVERY, span_of(i, 128))), (1 + i, (j,))], [(j, (EVERY, span_of(i, 128)), EVERY)])
            for j in range(blks)
            for i in range(len(gots))
        ]

    return sums(s, (keep,) + tuple(gots), [(rows, cols)] * blks, plan)


def proj_second(s, chip, lines):
    parts = [chip[0]] + [swap(chip[i], "blk", i) for i in range(1, len(chip))]
    rows, cols = chip[0].shape
    size = cols // lines

    def plan(odd, upper):
        targets = []
        for z in range(lines):
            out, slot = by_line(z, odd, upper)
            targets.append((out, (slot,), span_of(z, size)))
        return [([(i, (EVERY,)) for i in range(len(parts))], targets)]

    return sums(s, parts, [(2, rows, size)] * 2, plan, True)


def fourth(s, mine):
    return paired(s, mine[0], swap(mine[1], "batch", 2))


def dealt(s, keep, got):
    def plan():
        return [
            ([(i, (2 * out + slot,)) for i in range(2)], [(out, (slot,), EVERY)])
            for out in range(2)
            for slot in range(2)
        ]

    return sums(s, (keep, got), [(2,) + keep.shape[1:]] * 2, plan)


def paired(s, keep, got):
    def plan():
        return [([(0, (i,)), (1, (i,))], [(i, (EVERY,), EVERY)]) for i in range(2)]

    return sums(s, (keep, got), [keep.shape[1:]] * 2, plan)


def down_first(s, keep, got, lines):
    blks, high, cols = keep.shape
    size = cols // lines

    def plan(odd, upper):
        found = []
        for z in range(lines):
            out, slot = by_line(z, odd, upper)
            for j in range(blks):
                src = (j, EVERY, span_of(z, size))
                found.append(([(0, src), (1, src)], [(out, (slot, j), EVERY)]))
        return found

    return sums(s, (keep, got), [(2, blks, high, size)] * 2, plan, True)


def down_final_kernel(s_ref, *refs):
    refs[-1][...] = add_up(*(ref[...] for ref in refs[:-1]))


def turned_final_kernel(s_ref, *refs):
    refs[-1][...] = add_up(*(ref[...] for ref in refs[:-1])).T


def up_final_kernel(high, half, size, s_ref, *refs):
    up_ref, out_ref, sums_ref = refs[-3:]
    total = add_up(*(ref[...] for ref in refs[:-3]))
    for p in range(high // size):
        up_ref[:, span_of(p, half)] = total[span_of(p, size), :half]
    out_ref[...] = total[:high, half : half + size].T
    sums_ref[...] = total[high : high + 8, half:]


def reduce_any(mats, thin=None):
    blks = lax.axis_size("blk")
    lines = lax.axis_size("batch") // 2
    me = lax.axis_index("blk")
    core = lax.axis_index("batch") % 2
    line = lax.axis_index("batch") // 2
    pieces = []
    for mat in mats:
        rows = mat.shape[0] // (2 * lines)
        pieces.append(mat.reshape(lines, 2, rows, blks, -1))
    if thin is not None:
        thin = thin.reshape(lines, 2, rows, 1, -1)
        pieces.append(jnp.broadcast_to(thin, thin.shape[:3] + (blks,) + thin.shape[4:]))
    every = jnp.concatenate(pieces, axis=4)

    def half(which, distance):
        part = lax.dynamic_index_in_dim(every, which, 1, keepdims=False)
        return lax.dynamic_index_in_dim(part, me ^ distance, 2, keepdims=False)

    keep = [half(core, distance) for distance in range(blks)]
    got = swap(jnp.stack([half(1 - core, i) for i in range(blks)]), "batch", 1)
    chip = [add_up(part, got[i]).astype(BF16) for i, part in enumerate(keep)]
    total = add_up(chip[0], *(swap(chip[i], "blk", i) for i in range(1, blks)))
    while lines > 1:
        lines //= 2
        upper = line // lines
        pairs = total.astype(BF16).reshape((2, lines) + total.shape[1:])
        mine = lax.dynamic_index_in_dim(pairs, upper, 0, keepdims=False)
        theirs = lax.dynamic_index_in_dim(pairs, 1 - upper, 0, keepdims=False)
        total = add_up(mine, swap(theirs, "batch", 2 * lines))
        line = line % lines
    return total[0]


def shards(
    hidden_in, lengths, head_order, w_qkv, w_out, ln1_gain, ln1_bias, w_up, w_down, ln2_gain,
    ln2_bias, grad_out,
):
    _, _, rows, width = hidden_in.shape
    heads = head_order.shape[0]
    blks = lax.axis_size("blk")
    batch = lax.axis_size("batch")
    inner = w_up.shape[1]
    me = lax.axis_index("blk")
    at = lax.axis_index("batch")
    fast = batch == 8 and blks == 4 and width % (16 * batch) == 0
    lines = batch // 2 if fast else 0
    wide = inner // blks
    size = width // batch
    half = width // 2
    high = width // blks
    cols = 3 * width // blks

    x = hidden_in.reshape(rows, width)
    dout = grad_out.reshape(rows, width)
    xp = swap(x, "blk", 1)
    gain1, bias1, gain2, bias2 = (
        part.reshape(1, width) for part in (ln1_gain, ln1_bias, ln2_gain, ln2_bias)
    )
    length = lax.dynamic_index_in_dim(lengths[:, 0], me // 2, 0, keepdims=False)
    ids = jnp.arange(heads, dtype=jnp.int32)
    order = jnp.sum(jnp.where(head_order[None, :] == ids[:, None], ids[None, :], 0), axis=1)
    parts = [me, at % 2, at // 2, length - rows * (me % 2), length - rows * (1 - me % 2)]
    s = jnp.concatenate([jnp.stack(parts).astype(jnp.int32), order.astype(jnp.int32)])

    square = ((width, rows), BF16)
    lse = ((heads, 1, rows), F32)
    split = [((2, rows, width // 2), BF16)] if lines else []
    qkv, near_ctx, near_lse, *x_parts = call(
        functools.partial(near_kernel, heads, lines), s, (x, w_qkv),
        [((3 * width, rows), BF16), square, lse] + split, mib=8, us=8,
    )

    if lines:
        down_out = [((blks, high, inner // 2), BF16)] * 2 + split
    else:
        down_out = [((width, inner), BF16)]
    kv, ctx, far_lse, hid, slope, dtwo, upt, resid, gains, *down = call(
        functools.partial(ffn_kernel, heads, blks, lines), s,
        (x, xp, w_qkv, qkv, near_ctx, w_out, gain1, bias1, gain2, bias2, dout, w_up, w_down),
        [((2 * width, rows), BF16), square, lse, ((rows, width), BF16), ((rows, inner), BF16),
         ((rows, width), F32), square, ((rows, width), F32), ((8, width), F32)] + down_out,
        [((rows, inner), BF16)], mib=16, us=18,
    )

    s = after(s, dtwo)
    if lines:
        ups = Halves(half + size, wide + high + 16, half)
        up_out = [((blks, wide, half), BF16)] * 2
        thin_out = [((blks, high + 16, half), BF16)] * 2
        proj_out = [((blks, cols, half), BF16)] + [((blks, cols, 128), BF16)] * (half // 128)
    else:
        up_out = [((width, inner), BF16)]
        thin_out = [((width, width), BF16), ((16, width), BF16)]
        proj_out = [((3 * width, width), BF16)]
    pre_shape = (16, 128) if lines else (rows, inner)
    _, done, *up = call(
        functools.partial(pre_back_kernel, blks, lines), s, (dtwo, slope, w_down, w_up, upt),
        [(pre_shape, BF16), ((rows, width), F32)] + up_out, mib=8,
    )
    s = after(s, done)
    if lines:
        chip1 = down_first(s, down[0], swap(down[1], "batch", 1), lines)
        s = after(s, chip1[0])
    dres, dctx, *thin = call(
        functools.partial(norm_back_kernel, blks, lines), s,
        (done, resid, gain1, gains, w_out, ctx), [((rows, width), F32), square] + thin_out, mib=8,
    )
    s = after(s, dctx)
    if lines:
        gots = [swap(part, "batch", 1) for part in (up[1], thin[1])]
        chip2 = ups.first(s, (up[0], thin[0]), gots, (0, wide, ups.rows))
        s = after(s, chip2[0])
    far_q, far_kv, *give = call(
        functools.partial(far_back_kernel, heads), s, (qkv, kv, ctx, dctx, far_lse, w_qkv),
        [((width // 2, rows), BF16), square, ((width - 128, rows), BF16), ((128, rows), BF16)],
        [((2 * width, rows), BF16)], mib=8,
    )
    s = after(s, far_q)
    if not lines:
        got_in = [swap(part, "blk", 1) for part in give]
    dqkv, *proj = call(
        functools.partial(near_back_kernel, heads, blks, lines), s,
        (qkv, ctx, dctx, near_lse, far_q, far_kv)
        + ((x_parts[0], down[2]) if lines else (x, xp)),
        [((3 * width, rows), BF16)] + proj_out, [square], mib=8,
    )
    s = after(s, dqkv)
    if lines:
        line1 = fourth(s, chip1)
        s = after(s, line1[0])
        pair2 = ups.second(s, chip2)
        s = after(s, pair2[0])
        got_in = [swap(part, "blk", 1) for part in lax.optimization_barrier((pair2[0], *give))[1:]]
        chip3 = proj_first(s, proj[0], [swap(part, "batch", 1) for part in proj[1:]])
        s = after(s, chip3[0])
        line2 = ups.third(s, pair2, wide, size, lines)
        s = after(s, line2[0])
        far1 = dealt(s, line1[0], swap(line1[1], "batch", 4))
        s = after(s, far1[0])
    (own,) = call(through_kernel, s, (w_qkv, dqkv), [((width, rows), F32)], mib=4)
    s = after(s, own)
    if lines:
        line3 = proj_second(s, chip3, lines)
        s = after(s, line3[0])
        last2 = fourth(s, line2)
        s = after(s, last2[0])
        last1 = paired(s, far1[0], swap(far1[1], "blk", 2))
        s = after(s, last1[0])
        last3 = fourth(s, line3)
        s = after(s, last3[0])
        (own_down,) = call(
            down_final_kernel, s, (last1[0], swap(last1[1], "blk", 1)),
            [((high, inner // batch), F32)], mib=4,
        )
        s = after(s, own_down)
        own_down = own_down.T
        own_up, own_out, thin = call(
            functools.partial(up_final_kernel, high, half, size), s,
            (last2[0], swap(last2[1], "batch", 4)),
            [((size, wide), F32), ((size, high), F32), ((8, 128), F32)], mib=4,
        )
        thin = thin[:4, :size]
        s = after(s, own_up)
    (grad_in,) = call(input_kernel, s, (own, *got_in, dres), [((rows, width), BF16)], mib=4)
    if lines:
        s = after(s, grad_in)
        (own_qkv,) = call(
            turned_final_kernel, s, (last3[0], swap(last3[1], "batch", 4)),
            [((size, cols), F32)], mib=4,
        )
    else:
        own_down = reduce_any([down[0].T])
        both = reduce_any([up[0], thin[0].T], thin[1][:4].T)
        own_up, own_out, thin = both[:, :wide], both[:, wide : wide + high], both[:, wide + high :].T
        own_qkv = reduce_any([proj[0].T])
    return (
        hid.reshape(hidden_in.shape),
        grad_in.reshape(hidden_in.shape),
        own_qkv,
        own_out,
        thin[0],
        thin[1],
        own_up,
        own_down,
        thin[2],
        thin[3],
    )


def solution(mesh):
    rows = P("blk", "batch", None, None)
    both = P("batch", "blk")
    return jax.shard_map(
        shards,
        mesh=mesh,
        in_specs=(rows, P(None, "batch")) + (P(),) * 9 + (rows,),
        out_specs=(rows, rows, both, both, P("batch"), P("batch"), both, both)
        + (P("batch"), P("batch")),
        check_vma=False,
    )
```

```python
import functools
import math

import jax
import jax.numpy as jnp
from jax import lax
from jax.experimental import pallas as pl
from jax.experimental.pallas import tpu as pltpu
from jax.sharding import PartitionSpec as P

F32 = jnp.float32
BF16 = jnp.bfloat16
MIB = 1 << 20
EPS = 1e-06
NEG = -1e30
LOG2E = math.log2(math.e)
FF_BLOCKS = 4
STEP = 48
EVERY = slice(None)
ME, CORE, LINE, NEAR, FAR, ORDER = range(6)


def swap(block, axis, bits):
    return lax.ppermute(block, axis, [(i, i ^ bits) for i in range(lax.axis_size(axis))])


def nn(a, b):
    return lax.dot_general(a, b, (((1,), (0,)), ((), ())), preferred_element_type=F32)


def nt(a, b):
    return lax.dot_general(a, b, (((1,), (1,)), ((), ())), preferred_element_type=F32)


def tn(a, b):
    return lax.dot_general(a, b, (((0,), (0,)), ((), ())), preferred_element_type=F32)


def call(kernel, scalars, ins, outs, scratch=(), mib=16, us=0):
    vmem = pl.BlockSpec(memory_space=pltpu.VMEM)
    return pl.pallas_call(
        kernel,
        in_specs=[pl.BlockSpec(memory_space=pltpu.SMEM)] + [vmem] * len(ins),
        out_specs=[vmem] * len(outs),
        out_shape=[jax.ShapeDtypeStruct(shape, dtype) for shape, dtype in outs],
        scratch_shapes=[pltpu.VMEM(shape, dtype) for shape, dtype in scratch],
        compiler_params=pltpu.CompilerParams(vmem_limit_bytes=mib * MIB),
        cost_estimate=pl.CostEstimate(
            flops=1000000 + us * 1150000000, bytes_accessed=10000, transcendentals=0
        ),
    )(scalars, *ins)


def rows_of(index, size):
    return pl.ds(pl.multiple_of(index * size, size), size)


def stacked(first, *rows):
    spare = lax.broadcasted_iota(jnp.int32, (16, first.shape[1]), 0)
    extra = jnp.zeros(spare.shape, F32)
    for i, row in enumerate(rows):
        extra = jnp.where(spare == i, row, extra)
    return jnp.concatenate([first, extra.astype(BF16)], axis=0)


def key_bias(valid, keys):
    place = lax.broadcasted_iota(jnp.int32, (1, keys), 1)
    return jnp.where(place < valid, 0.0, NEG)


def attend_head(coef, q, k, v, bias):
    dim = q.shape[0]
    raw = nn(stacked(k, bias).T, stacked(q, 1.0))
    top = jnp.max(raw, axis=0, keepdims=True)
    terms = jnp.exp2((raw - top) * coef).astype(BF16)
    got = nn(stacked(v, 1.0), terms)
    total = got[dim : dim + 1]
    return (got[:dim] / total).astype(BF16), top * coef + jnp.log2(total)


def attend_head_back(coef, scale, q, k, v, bias, lse, ctx, dctx):
    delta = jnp.sum(dctx.astype(F32) * ctx.astype(F32), axis=0, keepdims=True)
    raw = nn(stacked(k, bias).T, stacked(q, 1.0))
    probs = jnp.exp2(raw * coef - lse)
    draw = (probs * (nn(v.T, dctx) - delta)).astype(BF16)
    dv = nt(dctx, probs.astype(BF16)).astype(BF16)
    dk = (nt(q, draw) * scale).astype(BF16)
    dq = (nn(k, draw) * scale).astype(BF16)
    return dq, dk, dv


def norm_stats(hidden):
    mean = jnp.mean(hidden, axis=-1, keepdims=True)
    centred = hidden - mean
    var = jnp.mean(centred * centred, axis=-1, keepdims=True)
    inv = lax.rsqrt(var + EPS)
    return centred * inv, inv


def norm_back(grad, gain, hat, inv):
    scaled = grad * gain
    shift = jnp.mean(scaled, axis=-1, keepdims=True)
    slope = jnp.mean(scaled * hat, axis=-1, keepdims=True)
    back = inv * (scaled - shift - hat * slope)
    return back, jnp.sum(grad * hat, axis=0, keepdims=True), jnp.sum(grad, axis=0, keepdims=True)


def by_core(mat, core, lines):
    span = mat.shape[1] // (2 * lines)
    halves = [
        jnp.concatenate(
            [mat[:, (2 * z + p) * span : (2 * z + p + 1) * span] for z in range(lines)], axis=1
        )
        for p in range(2)
    ]
    even = core == 0
    return jnp.where(even, halves[0], halves[1]), jnp.where(even, halves[1], halves[0])


def rows_by_core(ref, core, lines):
    span = ref.shape[0] // (2 * lines)
    return [
        jnp.concatenate([ref[rows_of(2 * z + (core ^ which), span), :] for z in range(lines)], axis=0)
        for which in range(2)
    ]


def near_kernel(heads, lines, s_ref, x_ref, w_ref, qkv_ref, ctx_ref, lse_ref, *rest):
    width = x_ref.shape[1]
    dim = width // heads
    coef = LOG2E / math.sqrt(dim)
    turned = x_ref[...].T
    for part in range(3):
        at = slice(part * width, (part + 1) * width)
        qkv_ref[at, :] = tn(w_ref[:, at], turned).astype(BF16)
    if lines:
        rest[0][0], rest[0][1] = by_core(x_ref[...], s_ref[CORE], lines)
    bias = key_bias(s_ref[NEAR], x_ref.shape[0])

    def one(i, carry):
        head = s_ref[ORDER + i]
        at = rows_of(head, dim)
        ctx_ref[at, :], lse_ref[head] = attend_head(
            coef,
            qkv_ref[at, :],
            qkv_ref[rows_of(heads + head, dim), :],
            qkv_ref[rows_of(2 * heads + head, dim), :],
            bias,
        )
        return carry

    lax.fori_loop(0, heads // 2, one, 0, unroll=3)


def ffn_kernel(
    heads, blks, lines, s_ref, x_ref, xp_ref, w_ref, qkv_ref, near_ref, wo_ref, gain1_ref,
    bias1_ref, gain2_ref, bias2_ref, dout_ref, wu_ref, wd_ref,
    kv_ref, ctx_ref, lse_ref, hid_ref, slope_ref, dtwo_ref, upt_ref, resid_ref, gains_ref, *rest,
):
    act_ref = rest[-1]
    rows, width = x_ref.shape
    dim = width // heads
    coef = LOG2E / math.sqrt(dim)
    me, core = s_ref[ME], s_ref[CORE]
    turned = xp_ref[...].T
    for part in range(2):
        at = slice((part + 1) * width, (part + 2) * width)
        kv_ref[part * width : (part + 1) * width, :] = tn(w_ref[:, at], turned).astype(BF16)
    bias = key_bias(s_ref[FAR], rows)

    def one(i, carry):
        head = s_ref[ORDER + heads // 2 + i]
        at = rows_of(head, dim)
        ctx_ref[at, :], lse_ref[head] = attend_head(
            coef, qkv_ref[at, :], kv_ref[at, :], kv_ref[rows_of(heads + head, dim), :], bias
        )
        mine = rows_of(s_ref[ORDER + i], dim)
        ctx_ref[mine, :] = near_ref[mine, :]
        return carry

    lax.fori_loop(0, heads // 2, one, 0, unroll=3)

    resid = x_ref[...].astype(F32) + tn(ctx_ref[...], wo_ref[...])
    resid_ref[...] = resid
    hat, _ = norm_stats(resid)
    one_in = hat * gain1_ref[...] + bias1_ref[...]
    low = one_in.astype(BF16)
    upt_ref[...] = low.T
    total = one_in
    blk = wu_ref.shape[1] // FF_BLOCKS
    for j in range(FF_BLOCKS):
        at = slice(j * blk, (j + 1) * blk)
        pre = nn(low, wu_ref[:, at])
        cdf = 0.5 + 0.5 * lax.erf(pre * math.sqrt(0.5))
        pdf = jnp.exp2(pre * pre * (-0.5 * LOG2E)) * (1.0 / math.sqrt(2.0 * math.pi))
        slope_ref[:, at] = (cdf + pre * pdf).astype(BF16)
        act = (pre * cdf).astype(BF16)
        act_ref[:, at] = act
        total = total + nn(act, wd_ref[at, :])
    hat, inv = norm_stats(total)
    hid_ref[...] = (hat * gain2_ref[...] + bias2_ref[...]).astype(BF16)
    back, gain, shift = norm_back(dout_ref[...].astype(F32), gain2_ref[...], hat, inv)
    dtwo_ref[...] = back
    gains_ref[0:1, :] = gain
    gains_ref[1:2, :] = shift
    turned = back.astype(BF16).T
    if lines:
        high = width // blks
        span = act_ref.shape[1] // (2 * lines)
        for which in (1, 0):
            for z in range(0, lines, 2):
                pair = [act_ref[:, rows_of(2 * (z + i) + (core ^ which), span)] for i in range(2)]
                prod = nn(turned, jnp.concatenate(pair, axis=1)).astype(BF16)
                for k in range(blks):
                    rest[which][k ^ me, :, z * span : (z + 2) * span] = prod[
                        k * high : (k + 1) * high
                    ]
        rest[2][0], rest[2][1] = by_core(xp_ref[...], core, lines)
    else:
        rest[0][...] = nn(turned, act_ref[...]).astype(BF16)


def pre_back_kernel(blks, s_ref, dtwo_ref, slope_ref, wd_ref, wu_ref, dpre_ref, done_ref):
    low = dtwo_ref[...].astype(BF16)
    total = dtwo_ref[...]
    blk = wu_ref.shape[1] // blks
    for k in range(blks):
        at = slice(k * blk, (k + 1) * blk)
        dpre = (nt(low, wd_ref[at, :]) * slope_ref[:, at].astype(F32)).astype(BF16)
        dpre_ref[:, at] = dpre
        total = total + nt(dpre, wu_ref[:, at])
    done_ref[...] = total


def up_kernel(blks, lines, s_ref, dpre_ref, upt_ref, *outs):
    if not lines:
        outs[0][...] = nn(upt_ref[...], dpre_ref[...]).astype(BF16)
        return
    me, core = s_ref[ME], s_ref[CORE]
    blk = dpre_ref.shape[1] // blks
    high = outs[1].shape[1]
    for which, rows in ((1, 1), (0, 0)):
        mine = rows_by_core(upt_ref, core, lines)[rows]
        half = mine.shape[0]
        for k in range(blks):
            prod = nn(mine, dpre_ref[:, k * blk : (k + 1) * blk]).astype(BF16)
            if not which:
                for p in range(blk // half):
                    outs[0][k ^ me, p * half : (p + 1) * half, :] = prod[:, p * half : (p + 1) * half]
                continue
            for i, out in enumerate(outs[1:]):
                for p in range(blk // half):
                    low, end = max(p * half, i * high), min((p + 1) * half, (i + 1) * high)
                    if low < end:
                        out[k ^ me, low - i * high : end - i * high, :] = prod[
                            low - p * half : end - p * half, p * half : (p + 1) * half
                        ]


def norm_back_kernel(
    blks, lines, s_ref, done_ref, resid_ref, gain1_ref, gains_ref, wo_ref, ctx_ref, dres_ref,
    dctx_ref, *outs,
):
    me, core = s_ref[ME], s_ref[CORE]
    hat, inv = norm_stats(resid_ref[...])
    back, gain, shift = norm_back(done_ref[...], gain1_ref[...], hat, inv)
    dres_ref[...] = back
    turned = back.astype(BF16).T
    dctx_ref[...] = nn(wo_ref[...], turned).astype(BF16)
    row = lax.broadcasted_iota(jnp.int32, (16, gain.shape[1]), 0)
    sums = jnp.where(row == 0, gain, jnp.where(row == 1, shift, 0.0))
    sums = jnp.where(row == 2, gains_ref[0:1, :], sums)
    sums = jnp.where(row == 3, gains_ref[1:2, :], sums).astype(BF16)
    if not lines:
        outs[0][...] = nt(turned, ctx_ref[...]).astype(BF16)
        outs[1][...] = sums
        return
    ctxs = rows_by_core(ctx_ref, core, lines)
    sums = by_core(sums, core, lines)
    high = turned.shape[0] // blks
    both = nt(turned, jnp.concatenate(ctxs, axis=0)).astype(BF16)
    half = both.shape[1] // 2
    for which, (out, thin) in enumerate(zip(outs, sums)):
        for k in range(blks):
            out[k ^ me, :high, :] = both[k * high : (k + 1) * high, which * half : (which + 1) * half]
            out[k ^ me, high:, :] = thin


def far_back_kernel(
    heads, s_ref, qkv_ref, kv_ref, ctx_ref, dctx_ref, lse_ref, w_ref, dq_ref, dkv_ref, give_ref,
    rest_ref, wide_ref,
):
    width, rows = ctx_ref.shape
    dim = width // heads
    half = heads // 2
    scale = 1.0 / math.sqrt(dim)
    bias = key_bias(s_ref[FAR], rows)
    wide_ref[...] = jnp.zeros_like(wide_ref)

    def one(i, carry):
        head = s_ref[ORDER + half + i]
        at, low = rows_of(head, dim), rows_of(heads + head, dim)
        dq, dk, dv = attend_head_back(
            LOG2E * scale, scale, qkv_ref[at, :], kv_ref[at, :], kv_ref[low, :], bias,
            lse_ref[head], ctx_ref[at, :], dctx_ref[at, :],
        )
        dq_ref[rows_of(i, dim), :] = dq
        dkv_ref[rows_of(i, dim), :] = dk
        dkv_ref[rows_of(half + i, dim), :] = dv
        wide_ref[at, :] = dk
        wide_ref[low, :] = dv
        return carry

    lax.fori_loop(0, half, one, 0, unroll=3)
    give = nn(w_ref[:, width:], wide_ref[...]).astype(BF16)
    give_ref[...] = give[: give_ref.shape[0]]
    rest_ref[...] = give[give_ref.shape[0] :]


def near_back_kernel(
    heads, blks, lines, s_ref, qkv_ref, ctx_ref, dctx_ref, lse_ref, farq_ref, farkv_ref, x_ref,
    xp_ref, dqkv_ref, *rest,
):
    outs, near_ref = rest[:-1], rest[-1]
    width, rows = ctx_ref.shape
    dim = width // heads
    half = heads // 2
    scale = 1.0 / math.sqrt(dim)
    bias = key_bias(s_ref[NEAR], rows)
    me = s_ref[ME]
    dqkv_ref[width:, :] = jnp.zeros((2 * width, rows), BF16)

    def one(i, carry):
        head = s_ref[ORDER + i]
        at = rows_of(head, dim)
        key, value = rows_of(heads + head, dim), rows_of(2 * heads + head, dim)
        dq, dk, dv = attend_head_back(
            LOG2E * scale, scale, qkv_ref[at, :], qkv_ref[key, :], qkv_ref[value, :], bias,
            lse_ref[head], ctx_ref[at, :], dctx_ref[at, :],
        )
        dqkv_ref[at, :] = dq
        dqkv_ref[key, :] = dk
        dqkv_ref[value, :] = dv
        near_ref[rows_of(i, dim), :] = dk
        near_ref[rows_of(half + i, dim), :] = dv
        dqkv_ref[rows_of(s_ref[ORDER + half + i], dim), :] = farq_ref[rows_of(i, dim), :]
        return carry

    lax.fori_loop(0, half, one, 0, unroll=3)
    per = 3 * heads // blks

    def store(unit, prod):
        if not lines:
            outs[0][rows_of(unit, dim), :] = prod
            return
        at = ((unit // per) ^ me, rows_of(unit % per, dim), EVERY)
        keep = outs[0].shape[2]
        outs[0][at] = prod[:, :keep]
        for i, out in enumerate(outs[1:]):
            out[at] = prod[:, keep + i * 128 : keep + (i + 1) * 128]

    x = jnp.concatenate([x_ref[0], x_ref[1]], axis=1) if lines else x_ref[...]
    xp = jnp.concatenate([xp_ref[0], xp_ref[1]], axis=1) if lines else xp_ref[...]
    prod = nn(dqkv_ref[:width, :], x).astype(BF16)
    for h in range(heads):
        store(h, prod[h * dim : (h + 1) * dim])
    for first, grads, inputs in ((0, near_ref, x), (half, farkv_ref, xp)):
        prod = nn(grads[...], inputs).astype(BF16)
        for i in range(half):
            head = s_ref[ORDER + first + i]
            store(heads + head, prod[i * dim : (i + 1) * dim])
            low = (half + i) * dim
            store(2 * heads + head, prod[low : low + dim])


def through_kernel(s_ref, w_ref, dqkv_ref, own_ref):
    own_ref[...] = nn(w_ref[...], dqkv_ref[...])


def input_kernel(s_ref, own_ref, got_ref, rest_ref, dres_ref, out_ref):
    cut = got_ref.shape[0]
    for at, got in ((slice(0, cut), got_ref), (slice(cut, None), rest_ref)):
        total = own_ref[at, :] + got[...].astype(F32)
        out_ref[:, at] = (total.T + dres_ref[:, at]).astype(BF16)


def add_up(*parts):
    total = parts[0].astype(F32)
    for part in parts[1:]:
        total = total + part.astype(F32)
    return total


def after(scalars, *arrays):
    return lax.optimization_barrier((scalars,) + arrays)[0]


def block_at(ref, at):
    at = tuple(at) + (EVERY,) * (len(ref.shape) - len(at))
    first, last, _ = at[-2].indices(ref.shape[-2])
    return at[:-2], first, last - first, at[-1]


def sums_kernel(plan, lines, inputs, s_ref, *refs):
    ins, outs = refs[:inputs], refs[inputs:]

    def run(odd, upper):
        for terms, targets in plan(odd, upper) if lines else plan():
            found = [(ins[i],) + block_at(ins[i], src) for i, src in terms]
            places = [(outs[out],) + block_at(outs[out], dst) + (part,) for out, dst, part in targets]
            rows = found[0][3]

            def add(at, size):
                blocks = [
                    ref[leads + (pl.ds(at + row, size), col)] for ref, leads, row, _, col in found
                ]
                total = sum(blocks[1:], blocks[0]) if len(blocks) == 2 else add_up(*blocks).astype(BF16)
                for ref, leads, row, _, col, part in places:
                    ref[leads + (pl.ds(at + row, size), col)] = total[:, part]

            def body(i, carry):
                add(pl.multiple_of(i * STEP, STEP), STEP)
                return carry

            if rows >= 2 * STEP:
                lax.fori_loop(0, rows // STEP, body, 0)
                if rows % STEP:
                    add(rows // STEP * STEP, rows % STEP)
            else:
                add(0, rows)

    if lines:
        line = s_ref[LINE]
        for odd in range(2):
            pl.when(line % 2 == odd)(functools.partial(run, odd, line // 2))
    else:
        run(0, 0)


def sums(scalars, ins, shapes, plan, lines=False):
    kernel = functools.partial(sums_kernel, plan, lines, len(ins))
    return call(kernel, scalars, ins, [(shape, BF16) for shape in shapes], mib=4)


def span_of(index, size):
    return slice(index * size, (index + 1) * size)


def by_line(z, odd, upper):
    return (z % 2) ^ odd, (z // 2) ^ upper


class Halves:
    def __init__(self, cut, rows, cols):
        self.cut, self.rows, self.cols = cut, rows, cols
        self.sizes = (cut, rows - cut)
        self.at = (slice(0, cut), slice(cut, rows))

    def first(self, s, keeps, gots):
        shapes = [(2, size, self.cols) for size in self.sizes for _ in range(2)]
        picks = ((0, 0, (0, 2)), (1, 0, (1, 3)), (2, 1, (0, 1)), (3, 1, (2, 3)))
        wide = keeps[0].shape[1]

        def plan():
            found = []
            for out, half, group in picks:
                start, end = self.at[half].start, self.at[half].stop
                first = 0
                for i, got in enumerate(gots):
                    last = first + got.shape[1]
                    low, up = max(first, start), min(last, end)
                    kept = int(low >= wide)
                    for slot, j in enumerate(group) if low < up else ():
                        keep = (kept, (j, slice(low - kept * wide, up - kept * wide), EVERY))
                        other = (len(keeps) + i, (j, slice(low - first, up - first), EVERY))
                        here = (slot, slice(low - start, up - start), EVERY)
                        found.append(([keep, other], [(out, here, EVERY)]))
                    first = last
            return found

        return sums(s, (*keeps, *gots), shapes, plan)

    def second(self, s, chip):
        got = (swap(chip[1], "blk", 1), swap(chip[3], "blk", 2))
        shapes = [(size, self.cols) for size in self.sizes for _ in range(2)]

        def plan():
            return [
                ([(half, (slot,)), (2 + half, (slot,))], [(2 * half + slot, (EVERY,), EVERY)])
                for half in range(2)
                for slot in range(2)
            ]

        return sums(s, (chip[0], chip[2]) + got, shapes, plan)

    def third(self, s, pair, wide, size, lines):
        got = (swap(pair[1], "blk", 2), swap(pair[3], "blk", 1))
        half = self.cols
        shape = (self.rows - wide, half + 128)

        def plan(odd, upper):
            found = []
            for p in range(wide // half):
                for z in range(lines):
                    row = p * half + z * size
                    which = int(row >= self.cut)
                    row -= which * self.cut
                    out, slot = by_line(z, odd, upper)
                    src = (slice(row, row + size), EVERY)
                    dst = (slot, span_of(p, size), slice(0, half))
                    found.append(([(which, src), (2 + which, src)], [(out, dst, EVERY)]))
            src = (slice(wide - self.cut, None), EVERY)
            targets = []
            for z in range(lines):
                out, slot = by_line(z, odd, upper)
                targets.append((out, (slot, EVERY, slice(half, half + size)), span_of(z, size)))
            return found + [([(1, src), (3, src)], targets)]

        return sums(s, (pair[0], pair[2]) + got, [(2,) + shape] * 2, plan, True)


def proj_first(s, keep, gots):
    blks, rows, cols = keep.shape

    def plan():
        return [
            ([(0, (j, EVERY, span_of(i, 128))), (1 + i, (j,))], [(j, (EVERY, span_of(i, 128)), EVERY)])
            for j in range(blks)
            for i in range(len(gots))
        ]

    return sums(s, (keep,) + tuple(gots), [(rows, cols)] * blks, plan)


def proj_second(s, chip, lines):
    parts = [chip[0]] + [swap(chip[i], "blk", i) for i in range(1, len(chip))]
    rows, cols = chip[0].shape
    size = cols // lines

    def plan(odd, upper):
        targets = []
        for z in range(lines):
            out, slot = by_line(z, odd, upper)
            targets.append((out, (slot,), span_of(z, size)))
        return [([(i, (EVERY,)) for i in range(len(parts))], targets)]

    return sums(s, parts, [(2, rows, size)] * 2, plan, True)


def fourth(s, mine):
    return paired(s, mine[0], swap(mine[1], "batch", 2))


def dealt(s, keep, got):
    def plan():
        return [
            ([(i, (2 * out + slot,)) for i in range(2)], [(out, (slot,), EVERY)])
            for out in range(2)
            for slot in range(2)
        ]

    return sums(s, (keep, got), [(2,) + keep.shape[1:]] * 2, plan)


def paired(s, keep, got):
    def plan():
        return [([(0, (i,)), (1, (i,))], [(i, (EVERY,), EVERY)]) for i in range(2)]

    return sums(s, (keep, got), [keep.shape[1:]] * 2, plan)


def down_first(s, keep, got, lines):
    blks, high, cols = keep.shape
    size = cols // lines

    def plan(odd, upper):
        found = []
        for z in range(lines):
            out, slot = by_line(z, odd, upper)
            for j in range(blks):
                src = (j, EVERY, span_of(z, size))
                found.append(([(0, src), (1, src)], [(out, (slot, j), EVERY)]))
        return found

    return sums(s, (keep, got), [(2, blks, high, size)] * 2, plan, True)


def down_final_kernel(s_ref, *refs):
    refs[-1][...] = add_up(*(ref[...] for ref in refs[:-1]))


def turned_final_kernel(s_ref, *refs):
    refs[-1][...] = add_up(*(ref[...] for ref in refs[:-1])).T


def up_final_kernel(high, half, size, s_ref, *refs):
    up_ref, out_ref, sums_ref = refs[-3:]
    total = add_up(*(ref[...] for ref in refs[:-3]))
    for p in range(high // size):
        up_ref[:, span_of(p, half)] = total[span_of(p, size), :half]
    out_ref[...] = total[:high, half : half + size].T
    sums_ref[...] = total[high : high + 8, half:]


def reduce_any(mats, thin=None):
    blks = lax.axis_size("blk")
    lines = lax.axis_size("batch") // 2
    me = lax.axis_index("blk")
    core = lax.axis_index("batch") % 2
    line = lax.axis_index("batch") // 2
    pieces = []
    for mat in mats:
        rows = mat.shape[0] // (2 * lines)
        pieces.append(mat.reshape(lines, 2, rows, blks, -1))
    if thin is not None:
        thin = thin.reshape(lines, 2, rows, 1, -1)
        pieces.append(jnp.broadcast_to(thin, thin.shape[:3] + (blks,) + thin.shape[4:]))
    every = jnp.concatenate(pieces, axis=4)

    def half(which, distance):
        part = lax.dynamic_index_in_dim(every, which, 1, keepdims=False)
        return lax.dynamic_index_in_dim(part, me ^ distance, 2, keepdims=False)

    keep = [half(core, distance) for distance in range(blks)]
    got = swap(jnp.stack([half(1 - core, i) for i in range(blks)]), "batch", 1)
    chip = [add_up(part, got[i]).astype(BF16) for i, part in enumerate(keep)]
    total = add_up(chip[0], *(swap(chip[i], "blk", i) for i in range(1, blks)))
    while lines > 1:
        lines //= 2
        upper = line // lines
        pairs = total.astype(BF16).reshape((2, lines) + total.shape[1:])
        mine = lax.dynamic_index_in_dim(pairs, upper, 0, keepdims=False)
        theirs = lax.dynamic_index_in_dim(pairs, 1 - upper, 0, keepdims=False)
        total = add_up(mine, swap(theirs, "batch", 2 * lines))
        line = line % lines
    return total[0]


def shards(
    hidden_in, lengths, head_order, w_qkv, w_out, ln1_gain, ln1_bias, w_up, w_down, ln2_gain,
    ln2_bias, grad_out,
):
    _, _, rows, width = hidden_in.shape
    heads = head_order.shape[0]
    blks = lax.axis_size("blk")
    batch = lax.axis_size("batch")
    inner = w_up.shape[1]
    me = lax.axis_index("blk")
    at = lax.axis_index("batch")
    fast = batch == 8 and blks == 4 and width % (16 * batch) == 0
    lines = batch // 2 if fast else 0
    wide = inner // blks
    size = width // batch
    half = width // 2
    high = width // blks
    cols = 3 * width // blks

    x = hidden_in.reshape(rows, width)
    dout = grad_out.reshape(rows, width)
    xp = swap(x, "blk", 1)
    gain1, bias1, gain2, bias2 = (
        part.reshape(1, width) for part in (ln1_gain, ln1_bias, ln2_gain, ln2_bias)
    )
    length = lax.dynamic_index_in_dim(lengths[:, 0], me // 2, 0, keepdims=False)
    ids = jnp.arange(heads, dtype=jnp.int32)
    order = jnp.sum(jnp.where(head_order[None, :] == ids[:, None], ids[None, :], 0), axis=1)
    parts = [me, at % 2, at // 2, length - rows * (me % 2), length - rows * (1 - me % 2)]
    s = jnp.concatenate([jnp.stack(parts).astype(jnp.int32), order.astype(jnp.int32)])

    square = ((width, rows), BF16)
    lse = ((heads, 1, rows), F32)
    split = [((2, rows, width // 2), BF16)] if lines else []
    qkv, near_ctx, near_lse, *x_parts = call(
        functools.partial(near_kernel, heads, lines), s, (x, w_qkv),
        [((3 * width, rows), BF16), square, lse] + split, mib=8, us=8,
    )

    if lines:
        down_out = [((blks, high, inner // 2), BF16)] * 2 + split
    else:
        down_out = [((width, inner), BF16)]
    kv, ctx, far_lse, hid, slope, dtwo, upt, resid, gains, *down = call(
        functools.partial(ffn_kernel, heads, blks, lines), s,
        (x, xp, w_qkv, qkv, near_ctx, w_out, gain1, bias1, gain2, bias2, dout, w_up, w_down),
        [((2 * width, rows), BF16), square, lse, ((rows, width), BF16), ((rows, inner), BF16),
         ((rows, width), F32), square, ((rows, width), F32), ((8, width), F32)] + down_out,
        [((rows, inner), BF16)], mib=16, us=18,
    )

    s = after(s, dtwo)
    if lines:
        ups = Halves(half + size, wide + high + 16, half)
        up_out = [((blks, wide, half), BF16)] + [((blks, wide // 3, half), BF16)] * 3
        thin_out = [((blks, high + 16, half), BF16)] * 2
        proj_out = [((blks, cols, half), BF16)] + [((blks, cols, 128), BF16)] * (half // 128)
    else:
        up_out = [((width, inner), BF16)]
        thin_out = [((width, width), BF16), ((16, width), BF16)]
        proj_out = [((3 * width, width), BF16)]
    dpre, done = call(
        functools.partial(pre_back_kernel, blks), s, (dtwo, slope, w_down, w_up),
        [((rows, inner), BF16), ((rows, width), F32)], mib=8,
    )
    s = after(s, done)
    if lines:
        chip1 = down_first(s, down[0], swap(down[1], "batch", 1), lines)
        s = after(s, chip1[0])
    up = call(functools.partial(up_kernel, blks, lines), s, (dpre, upt), up_out, mib=8)
    s = after(s, up[0])
    dres, dctx, *thin = call(
        functools.partial(norm_back_kernel, blks, lines), s,
        (done, resid, gain1, gains, w_out, ctx), [((rows, width), F32), square] + thin_out, mib=8,
    )
    s = after(s, dctx)
    if lines:
        gots = [swap(part, "batch", 1) for part in (*up[1:], thin[1])]
        chip2 = ups.first(s, (up[0], thin[0]), gots)
        s = after(s, chip2[0])
    far_q, far_kv, *give = call(
        functools.partial(far_back_kernel, heads), s, (qkv, kv, ctx, dctx, far_lse, w_qkv),
        [((width // 2, rows), BF16), square, ((width - 128, rows), BF16), ((128, rows), BF16)],
        [((2 * width, rows), BF16)], mib=8,
    )
    s = after(s, far_q)
    if not lines:
        got_in = [swap(part, "blk", 1) for part in give]
    dqkv, *proj = call(
        functools.partial(near_back_kernel, heads, blks, lines), s,
        (qkv, ctx, dctx, near_lse, far_q, far_kv)
        + ((x_parts[0], down[2]) if lines else (x, xp)),
        [((3 * width, rows), BF16)] + proj_out, [square], mib=8,
    )
    s = after(s, dqkv)
    if lines:
        line1 = fourth(s, chip1)
        s = after(s, line1[0])
        pair2 = ups.second(s, chip2)
        s = after(s, pair2[0])
        got_in = [swap(part, "blk", 1) for part in lax.optimization_barrier((pair2[0], *give))[1:]]
        chip3 = proj_first(s, proj[0], [swap(part, "batch", 1) for part in proj[1:]])
        s = after(s, chip3[0])
        line2 = ups.third(s, pair2, wide, size, lines)
        s = after(s, line2[0])
        far1 = dealt(s, line1[0], swap(line1[1], "batch", 4))
        s = after(s, far1[0])
    (own,) = call(through_kernel, s, (w_qkv, dqkv), [((width, rows), F32)], mib=4)
    s = after(s, own)
    if lines:
        line3 = proj_second(s, chip3, lines)
        s = after(s, line3[0])
        last2 = fourth(s, line2)
        s = after(s, last2[0])
        last1 = paired(s, far1[0], swap(far1[1], "blk", 2))
        s = after(s, last1[0])
        last3 = fourth(s, line3)
        s = after(s, last3[0])
        (own_down,) = call(
            down_final_kernel, s, (last1[0], swap(last1[1], "blk", 1)),
            [((high, inner // batch), F32)], mib=4,
        )
        s = after(s, own_down)
        own_down = own_down.T
        own_up, own_out, thin = call(
            functools.partial(up_final_kernel, high, half, size), s,
            (last2[0], swap(last2[1], "batch", 4)),
            [((size, wide), F32), ((size, high), F32), ((8, 128), F32)], mib=4,
        )
        thin = thin[:4, :size]
        s = after(s, own_up)
    (grad_in,) = call(input_kernel, s, (own, *got_in, dres), [((rows, width), BF16)], mib=4)
    if lines:
        s = after(s, grad_in)
        (own_qkv,) = call(
            turned_final_kernel, s, (last3[0], swap(last3[1], "batch", 4)),
            [((size, cols), F32)], mib=4,
        )
    else:
        own_down = reduce_any([down[0].T])
        both = reduce_any([up[0], thin[0].T], thin[1][:4].T)
        own_up, own_out, thin = both[:, :wide], both[:, wide : wide + high], both[:, wide + high :].T
        own_qkv = reduce_any([proj[0].T])
    return (
        hid.reshape(hidden_in.shape),
        grad_in.reshape(hidden_in.shape),
        own_qkv,
        own_out,
        thin[0],
        thin[1],
        own_up,
        own_down,
        thin[2],
        thin[3],
    )


def solution(mesh):
    rows = P("blk", "batch", None, None)
    both = P("batch", "blk")
    return jax.shard_map(
        shards,
        mesh=mesh,
        in_specs=(rows, P(None, "batch")) + (P(),) * 9 + (rows,),
        out_specs=(rows, rows, both, both, P("batch"), P("batch"), both, both)
        + (P("batch"), P("batch")),
        check_vma=False,
    )
```

```python
import functools
import math

import jax
import jax.numpy as jnp
from jax import lax
from jax.experimental import pallas as pl
from jax.experimental.pallas import tpu as pltpu
from jax.sharding import PartitionSpec as P

F32 = jnp.float32
BF16 = jnp.bfloat16
MIB = 1 << 20
EPS = 1e-06
NEG = -1e30
LOG2E = math.log2(math.e)
FF_BLOCKS = 4
STEP = 96
EVERY = slice(None)
ME, CORE, LINE, NEAR, FAR, ORDER = range(6)


def swap(block, axis, bits):
    return lax.ppermute(block, axis, [(i, i ^ bits) for i in range(lax.axis_size(axis))])


def nn(a, b):
    return lax.dot_general(a, b, (((1,), (0,)), ((), ())), preferred_element_type=F32)


def nt(a, b):
    return lax.dot_general(a, b, (((1,), (1,)), ((), ())), preferred_element_type=F32)


def tn(a, b):
    return lax.dot_general(a, b, (((0,), (0,)), ((), ())), preferred_element_type=F32)


def call(kernel, scalars, ins, outs, scratch=(), mib=16, us=0):
    vmem = pl.BlockSpec(memory_space=pltpu.VMEM)
    return pl.pallas_call(
        kernel,
        in_specs=[pl.BlockSpec(memory_space=pltpu.SMEM)] + [vmem] * len(ins),
        out_specs=[vmem] * len(outs),
        out_shape=[jax.ShapeDtypeStruct(shape, dtype) for shape, dtype in outs],
        scratch_shapes=[pltpu.VMEM(shape, dtype) for shape, dtype in scratch],
        compiler_params=pltpu.CompilerParams(vmem_limit_bytes=mib * MIB),
        cost_estimate=pl.CostEstimate(
            flops=1000000 + us * 1150000000, bytes_accessed=10000, transcendentals=0
        ),
    )(scalars, *ins)


def rows_of(index, size):
    return pl.ds(pl.multiple_of(index * size, size), size)


def stacked(first, *rows):
    spare = lax.broadcasted_iota(jnp.int32, (16, first.shape[1]), 0)
    extra = jnp.zeros(spare.shape, F32)
    for i, row in enumerate(rows):
        extra = jnp.where(spare == i, row, extra)
    return jnp.concatenate([first, extra.astype(BF16)], axis=0)


def key_bias(valid, keys):
    place = lax.broadcasted_iota(jnp.int32, (1, keys), 1)
    return jnp.where(place < valid, 0.0, NEG)


def attend_head(coef, q, k, v, bias):
    dim = q.shape[0]
    raw = nn(stacked(k, bias).T, stacked(q, 1.0))
    top = jnp.max(raw, axis=0, keepdims=True)
    terms = jnp.exp2((raw - top) * coef).astype(BF16)
    got = nn(stacked(v, 1.0), terms)
    total = got[dim : dim + 1]
    return (got[:dim] / total).astype(BF16), top * coef + jnp.log2(total)


def attend_head_back(coef, scale, q, k, v, bias, lse, ctx, dctx):
    delta = jnp.sum(dctx.astype(F32) * ctx.astype(F32), axis=0, keepdims=True)
    raw = nn(stacked(k, bias).T, stacked(q, 1.0))
    probs = jnp.exp2(raw * coef - lse)
    draw = (probs * (nn(v.T, dctx) - delta)).astype(BF16)
    dv = nt(dctx, probs.astype(BF16)).astype(BF16)
    dk = (nt(q, draw) * scale).astype(BF16)
    dq = (nn(k, draw) * scale).astype(BF16)
    return dq, dk, dv


def norm_stats(hidden):
    mean = jnp.mean(hidden, axis=-1, keepdims=True)
    centred = hidden - mean
    var = jnp.mean(centred * centred, axis=-1, keepdims=True)
    inv = lax.rsqrt(var + EPS)
    return centred * inv, inv


def norm_back(grad, gain, hat, inv):
    scaled = grad * gain
    shift = jnp.mean(scaled, axis=-1, keepdims=True)
    slope = jnp.mean(scaled * hat, axis=-1, keepdims=True)
    back = inv * (scaled - shift - hat * slope)
    return back, jnp.sum(grad * hat, axis=0, keepdims=True), jnp.sum(grad, axis=0, keepdims=True)


def by_core(mat, core, lines):
    span = mat.shape[1] // (2 * lines)
    halves = [
        jnp.concatenate(
            [mat[:, (2 * z + p) * span : (2 * z + p + 1) * span] for z in range(lines)], axis=1
        )
        for p in range(2)
    ]
    even = core == 0
    return jnp.where(even, halves[0], halves[1]), jnp.where(even, halves[1], halves[0])


def rows_by_core(ref, core, lines):
    span = ref.shape[0] // (2 * lines)
    return [
        jnp.concatenate([ref[rows_of(2 * z + (core ^ which), span), :] for z in range(lines)], axis=0)
        for which in range(2)
    ]


def near_kernel(heads, lines, s_ref, x_ref, w_ref, qkv_ref, ctx_ref, lse_ref, *rest):
    width = x_ref.shape[1]
    dim = width // heads
    coef = LOG2E / math.sqrt(dim)
    turned = x_ref[...].T
    for part in range(3):
        at = slice(part * width, (part + 1) * width)
        qkv_ref[at, :] = tn(w_ref[:, at], turned).astype(BF16)
    if lines:
        rest[0][0], rest[0][1] = by_core(x_ref[...], s_ref[CORE], lines)
    bias = key_bias(s_ref[NEAR], x_ref.shape[0])

    def one(i, carry):
        head = s_ref[ORDER + i]
        at = rows_of(head, dim)
        ctx_ref[at, :], lse_ref[head] = attend_head(
            coef,
            qkv_ref[at, :],
            qkv_ref[rows_of(heads + head, dim), :],
            qkv_ref[rows_of(2 * heads + head, dim), :],
            bias,
        )
        return carry

    lax.fori_loop(0, heads // 2, one, 0, unroll=3)


def ffn_kernel(
    heads, blks, lines, s_ref, x_ref, xp_ref, w_ref, qkv_ref, near_ref, wo_ref, gain1_ref,
    bias1_ref, gain2_ref, bias2_ref, dout_ref, wu_ref, wd_ref,
    kv_ref, ctx_ref, lse_ref, hid_ref, slope_ref, dtwo_ref, upt_ref, resid_ref, gains_ref, *rest,
):
    act_ref = rest[-1]
    rows, width = x_ref.shape
    dim = width // heads
    coef = LOG2E / math.sqrt(dim)
    me, core = s_ref[ME], s_ref[CORE]
    turned = xp_ref[...].T
    for part in range(2):
        at = slice((part + 1) * width, (part + 2) * width)
        kv_ref[part * width : (part + 1) * width, :] = tn(w_ref[:, at], turned).astype(BF16)
    bias = key_bias(s_ref[FAR], rows)

    def one(i, carry):
        head = s_ref[ORDER + heads // 2 + i]
        at = rows_of(head, dim)
        ctx_ref[at, :], lse_ref[head] = attend_head(
            coef, qkv_ref[at, :], kv_ref[at, :], kv_ref[rows_of(heads + head, dim), :], bias
        )
        mine = rows_of(s_ref[ORDER + i], dim)
        ctx_ref[mine, :] = near_ref[mine, :]
        return carry

    lax.fori_loop(0, heads // 2, one, 0, unroll=3)

    resid = x_ref[...].astype(F32) + tn(ctx_ref[...], wo_ref[...])
    resid_ref[...] = resid
    hat, _ = norm_stats(resid)
    one_in = hat * gain1_ref[...] + bias1_ref[...]
    low = one_in.astype(BF16)
    upt_ref[...] = low.T
    total = one_in
    blk = wu_ref.shape[1] // FF_BLOCKS
    for j in range(FF_BLOCKS):
        at = slice(j * blk, (j + 1) * blk)
        pre = nn(low, wu_ref[:, at])
        cdf = 0.5 + 0.5 * lax.erf(pre * math.sqrt(0.5))
        pdf = jnp.exp2(pre * pre * (-0.5 * LOG2E)) * (1.0 / math.sqrt(2.0 * math.pi))
        slope_ref[:, at] = (cdf + pre * pdf).astype(BF16)
        act = (pre * cdf).astype(BF16)
        act_ref[:, at] = act
        total = total + nn(act, wd_ref[at, :])
    hat, inv = norm_stats(total)
    hid_ref[...] = (hat * gain2_ref[...] + bias2_ref[...]).astype(BF16)
    back, gain, shift = norm_back(dout_ref[...].astype(F32), gain2_ref[...], hat, inv)
    dtwo_ref[...] = back
    gains_ref[0:1, :] = gain
    gains_ref[1:2, :] = shift
    turned = back.astype(BF16).T
    if lines:
        high = width // blks
        span = act_ref.shape[1] // (2 * lines)
        for which in (1, 0):
            for z in range(0, lines, 2):
                pair = [act_ref[:, rows_of(2 * (z + i) + (core ^ which), span)] for i in range(2)]
                prod = nn(turned, jnp.concatenate(pair, axis=1)).astype(BF16)
                for k in range(blks):
                    rest[which][k ^ me, :, z * span : (z + 2) * span] = prod[
                        k * high : (k + 1) * high
                    ]
        rest[2][0], rest[2][1] = by_core(xp_ref[...], core, lines)
    else:
        rest[0][...] = nn(turned, act_ref[...]).astype(BF16)


def pre_back_kernel(blks, s_ref, dtwo_ref, slope_ref, wd_ref, wu_ref, dpre_ref, done_ref):
    low = dtwo_ref[...].astype(BF16)
    total = dtwo_ref[...]
    blk = wu_ref.shape[1] // blks
    for k in range(blks):
        at = slice(k * blk, (k + 1) * blk)
        dpre = (nt(low, wd_ref[at, :]) * slope_ref[:, at].astype(F32)).astype(BF16)
        dpre_ref[:, at] = dpre
        total = total + nt(dpre, wu_ref[:, at])
    done_ref[...] = total


def up_kernel(blks, lines, s_ref, dpre_ref, upt_ref, *outs):
    if not lines:
        outs[0][...] = nn(upt_ref[...], dpre_ref[...]).astype(BF16)
        return
    me, core = s_ref[ME], s_ref[CORE]
    blk = dpre_ref.shape[1] // blks
    high = outs[1].shape[1]
    for which, rows in ((1, 1), (0, 0)):
        mine = rows_by_core(upt_ref, core, lines)[rows]
        half = mine.shape[0]
        for k in range(blks):
            prod = nn(mine, dpre_ref[:, k * blk : (k + 1) * blk]).astype(BF16)
            if not which:
                for p in range(blk // half):
                    outs[0][k ^ me, p * half : (p + 1) * half, :] = prod[:, p * half : (p + 1) * half]
                continue
            for i, out in enumerate(outs[1:]):
                for p in range(blk // half):
                    low, end = max(p * half, i * high), min((p + 1) * half, (i + 1) * high)
                    if low < end:
                        out[k ^ me, low - i * high : end - i * high, :] = prod[
                            low - p * half : end - p * half, p * half : (p + 1) * half
                        ]


def norm_back_kernel(
    blks, lines, s_ref, done_ref, resid_ref, gain1_ref, gains_ref, wo_ref, ctx_ref, dres_ref,
    dctx_ref, *outs,
):
    me, core = s_ref[ME], s_ref[CORE]
    hat, inv = norm_stats(resid_ref[...])
    back, gain, shift = norm_back(done_ref[...], gain1_ref[...], hat, inv)
    dres_ref[...] = back
    turned = back.astype(BF16).T
    dctx_ref[...] = nn(wo_ref[...], turned).astype(BF16)
    row = lax.broadcasted_iota(jnp.int32, (16, gain.shape[1]), 0)
    sums = jnp.where(row == 0, gain, jnp.where(row == 1, shift, 0.0))
    sums = jnp.where(row == 2, gains_ref[0:1, :], sums)
    sums = jnp.where(row == 3, gains_ref[1:2, :], sums).astype(BF16)
    if not lines:
        outs[0][...] = nt(turned, ctx_ref[...]).astype(BF16)
        outs[1][...] = sums
        return
    ctxs = rows_by_core(ctx_ref, core, lines)
    sums = by_core(sums, core, lines)
    high = turned.shape[0] // blks
    both = nt(turned, jnp.concatenate(ctxs, axis=0)).astype(BF16)
    half = both.shape[1] // 2
    for which, (out, thin) in enumerate(zip(outs, sums)):
        for k in range(blks):
            out[k ^ me, :high, :] = both[k * high : (k + 1) * high, which * half : (which + 1) * half]
            out[k ^ me, high:, :] = thin


def far_back_kernel(
    heads, s_ref, qkv_ref, kv_ref, ctx_ref, dctx_ref, lse_ref, w_ref, dq_ref, dkv_ref, give_ref,
    rest_ref, wide_ref,
):
    width, rows = ctx_ref.shape
    dim = width // heads
    half = heads // 2
    scale = 1.0 / math.sqrt(dim)
    bias = key_bias(s_ref[FAR], rows)
    wide_ref[...] = jnp.zeros_like(wide_ref)

    def one(i, carry):
        head = s_ref[ORDER + half + i]
        at, low = rows_of(head, dim), rows_of(heads + head, dim)
        dq, dk, dv = attend_head_back(
            LOG2E * scale, scale, qkv_ref[at, :], kv_ref[at, :], kv_ref[low, :], bias,
            lse_ref[head], ctx_ref[at, :], dctx_ref[at, :],
        )
        dq_ref[rows_of(i, dim), :] = dq
        dkv_ref[rows_of(i, dim), :] = dk
        dkv_ref[rows_of(half + i, dim), :] = dv
        wide_ref[at, :] = dk
        wide_ref[low, :] = dv
        return carry

    lax.fori_loop(0, half, one, 0, unroll=3)
    give = nn(w_ref[:, width:], wide_ref[...]).astype(BF16)
    give_ref[...] = give[: give_ref.shape[0]]
    rest_ref[...] = give[give_ref.shape[0] :]


def near_back_kernel(
    heads, blks, lines, s_ref, qkv_ref, ctx_ref, dctx_ref, lse_ref, farq_ref, farkv_ref, x_ref,
    xp_ref, dqkv_ref, *rest,
):
    outs, near_ref = rest[:-1], rest[-1]
    width, rows = ctx_ref.shape
    dim = width // heads
    half = heads // 2
    scale = 1.0 / math.sqrt(dim)
    bias = key_bias(s_ref[NEAR], rows)
    me = s_ref[ME]
    dqkv_ref[width:, :] = jnp.zeros((2 * width, rows), BF16)

    def one(i, carry):
        head = s_ref[ORDER + i]
        at = rows_of(head, dim)
        key, value = rows_of(heads + head, dim), rows_of(2 * heads + head, dim)
        dq, dk, dv = attend_head_back(
            LOG2E * scale, scale, qkv_ref[at, :], qkv_ref[key, :], qkv_ref[value, :], bias,
            lse_ref[head], ctx_ref[at, :], dctx_ref[at, :],
        )
        dqkv_ref[at, :] = dq
        dqkv_ref[key, :] = dk
        dqkv_ref[value, :] = dv
        near_ref[rows_of(i, dim), :] = dk
        near_ref[rows_of(half + i, dim), :] = dv
        dqkv_ref[rows_of(s_ref[ORDER + half + i], dim), :] = farq_ref[rows_of(i, dim), :]
        return carry

    lax.fori_loop(0, half, one, 0, unroll=3)
    per = 3 * heads // blks

    def store(unit, prod):
        if not lines:
            outs[0][rows_of(unit, dim), :] = prod
            return
        at = ((unit // per) ^ me, rows_of(unit % per, dim), EVERY)
        keep = outs[0].shape[2]
        outs[0][at] = prod[:, :keep]
        for i, out in enumerate(outs[1:]):
            out[at] = prod[:, keep + i * 128 : keep + (i + 1) * 128]

    x = jnp.concatenate([x_ref[0], x_ref[1]], axis=1) if lines else x_ref[...]
    xp = jnp.concatenate([xp_ref[0], xp_ref[1]], axis=1) if lines else xp_ref[...]
    prod = nn(dqkv_ref[:width, :], x).astype(BF16)
    for h in range(heads):
        store(h, prod[h * dim : (h + 1) * dim])
    for first, grads, inputs in ((0, near_ref, x), (half, farkv_ref, xp)):
        prod = nn(grads[...], inputs).astype(BF16)
        for i in range(half):
            head = s_ref[ORDER + first + i]
            store(heads + head, prod[i * dim : (i + 1) * dim])
            low = (half + i) * dim
            store(2 * heads + head, prod[low : low + dim])


def through_kernel(s_ref, w_ref, dqkv_ref, own_ref):
    own_ref[...] = nn(w_ref[...], dqkv_ref[...])


def input_kernel(s_ref, own_ref, got_ref, rest_ref, dres_ref, out_ref):
    cut = got_ref.shape[0]
    for at, got in ((slice(0, cut), got_ref), (slice(cut, None), rest_ref)):
        total = own_ref[at, :] + got[...].astype(F32)
        out_ref[:, at] = (total.T + dres_ref[:, at]).astype(BF16)


def add_up(*parts):
    total = parts[0].astype(F32)
    for part in parts[1:]:
        total = total + part.astype(F32)
    return total


def after(scalars, *arrays):
    return lax.optimization_barrier((scalars,) + arrays)[0]


def block_at(ref, at):
    at = tuple(at) + (EVERY,) * (len(ref.shape) - len(at))
    first, last, _ = at[-2].indices(ref.shape[-2])
    return at[:-2], first, last - first, at[-1]


def sums_kernel(plan, lines, inputs, s_ref, *refs):
    ins, outs = refs[:inputs], refs[inputs:]

    def run(odd, upper):
        for terms, targets in plan(odd, upper) if lines else plan():
            found = [(ins[i],) + block_at(ins[i], src) for i, src in terms]
            places = [(outs[out],) + block_at(outs[out], dst) + (part,) for out, dst, part in targets]
            rows = found[0][3]

            def add(at, size):
                blocks = [
                    ref[leads + (pl.ds(at + row, size), col)] for ref, leads, row, _, col in found
                ]
                total = sum(blocks[1:], blocks[0]) if len(blocks) == 2 else add_up(*blocks).astype(BF16)
                for ref, leads, row, _, col, part in places:
                    ref[leads + (pl.ds(at + row, size), col)] = total[:, part]

            def body(i, carry):
                add(pl.multiple_of(i * STEP, STEP), STEP)
                return carry

            if rows >= 2 * STEP:
                lax.fori_loop(0, rows // STEP, body, 0)
                if rows % STEP:
                    add(rows // STEP * STEP, rows % STEP)
            else:
                add(0, rows)

    if lines:
        line = s_ref[LINE]
        for odd in range(2):
            pl.when(line % 2 == odd)(functools.partial(run, odd, line // 2))
    else:
        run(0, 0)


def sums(scalars, ins, shapes, plan, lines=False):
    kernel = functools.partial(sums_kernel, plan, lines, len(ins))
    return call(kernel, scalars, ins, [(shape, BF16) for shape in shapes], mib=4)


def span_of(index, size):
    return slice(index * size, (index + 1) * size)


def by_line(z, odd, upper):
    return (z % 2) ^ odd, (z // 2) ^ upper


class Halves:
    def __init__(self, cut, rows, cols):
        self.cut, self.rows, self.cols = cut, rows, cols
        self.sizes = (cut, rows - cut)
        self.at = (slice(0, cut), slice(cut, rows))

    def first(self, s, keeps, gots):
        shapes = [(2, size, self.cols) for size in self.sizes for _ in range(2)]
        picks = ((0, 0, (0, 2)), (1, 0, (1, 3)), (2, 1, (0, 1)), (3, 1, (2, 3)))
        wide = keeps[0].shape[1]

        def plan():
            found = []
            for out, half, group in picks:
                start, end = self.at[half].start, self.at[half].stop
                first = 0
                for i, got in enumerate(gots):
                    last = first + got.shape[1]
                    low, up = max(first, start), min(last, end)
                    kept = int(low >= wide)
                    for slot, j in enumerate(group) if low < up else ():
                        keep = (kept, (j, slice(low - kept * wide, up - kept * wide), EVERY))
                        other = (len(keeps) + i, (j, slice(low - first, up - first), EVERY))
                        here = (slot, slice(low - start, up - start), EVERY)
                        found.append(([keep, other], [(out, here, EVERY)]))
                    first = last
            return found

        return sums(s, (*keeps, *gots), shapes, plan)

    def second(self, s, chip):
        got = (swap(chip[1], "blk", 1), swap(chip[3], "blk", 2))
        shapes = [(size, self.cols) for size in self.sizes for _ in range(2)]

        def plan():
            return [
                ([(half, (slot,)), (2 + half, (slot,))], [(2 * half + slot, (EVERY,), EVERY)])
                for half in range(2)
                for slot in range(2)
            ]

        return sums(s, (chip[0], chip[2]) + got, shapes, plan)

    def third(self, s, pair, wide, size, lines):
        got = (swap(pair[1], "blk", 2), swap(pair[3], "blk", 1))
        half = self.cols
        shape = (self.rows - wide, half + 128)

        def plan(odd, upper):
            found = []
            for p in range(wide // half):
                for z in range(lines):
                    row = p * half + z * size
                    which = int(row >= self.cut)
                    row -= which * self.cut
                    out, slot = by_line(z, odd, upper)
                    src = (slice(row, row + size), EVERY)
                    dst = (slot, span_of(p, size), slice(0, half))
                    found.append(([(which, src), (2 + which, src)], [(out, dst, EVERY)]))
            src = (slice(wide - self.cut, None), EVERY)
            targets = []
            for z in range(lines):
                out, slot = by_line(z, odd, upper)
                targets.append((out, (slot, EVERY, slice(half, half + size)), span_of(z, size)))
            return found + [([(1, src), (3, src)], targets)]

        return sums(s, (pair[0], pair[2]) + got, [(2,) + shape] * 2, plan, True)


def proj_first(s, keep, gots):
    blks, rows, cols = keep.shape

    def plan():
        return [
            ([(0, (j, EVERY, span_of(i, 128))), (1 + i, (j,))], [(j, (EVERY, span_of(i, 128)), EVERY)])
            for j in range(blks)
            for i in range(len(gots))
        ]

    return sums(s, (keep,) + tuple(gots), [(rows, cols)] * blks, plan)


def proj_second(s, chip, lines):
    parts = [chip[0]] + [swap(chip[i], "blk", i) for i in range(1, len(chip))]
    rows, cols = chip[0].shape
    size = cols // lines

    def plan(odd, upper):
        targets = []
        for z in range(lines):
            out, slot = by_line(z, odd, upper)
            targets.append((out, (slot,), span_of(z, size)))
        return [([(i, (EVERY,)) for i in range(len(parts))], targets)]

    return sums(s, parts, [(2, rows, size)] * 2, plan, True)


def fourth(s, mine):
    return paired(s, mine[0], swap(mine[1], "batch", 2))


def dealt(s, keep, got):
    def plan():
        return [
            ([(i, (2 * out + slot,)) for i in range(2)], [(out, (slot,), EVERY)])
            for out in range(2)
            for slot in range(2)
        ]

    return sums(s, (keep, got), [(2,) + keep.shape[1:]] * 2, plan)


def paired(s, keep, got):
    def plan():
        return [([(0, (i,)), (1, (i,))], [(i, (EVERY,), EVERY)]) for i in range(2)]

    return sums(s, (keep, got), [keep.shape[1:]] * 2, plan)


def down_first(s, keep, got, lines):
    blks, high, cols = keep.shape
    size = cols // lines

    def plan(odd, upper):
        found = []
        for z in range(lines):
            out, slot = by_line(z, odd, upper)
            for j in range(blks):
                src = (j, EVERY, span_of(z, size))
                found.append(([(0, src), (1, src)], [(out, (slot, j), EVERY)]))
        return found

    return sums(s, (keep, got), [(2, blks, high, size)] * 2, plan, True)


def down_final_kernel(s_ref, *refs):
    refs[-1][...] = add_up(*(ref[...] for ref in refs[:-1]))


def turned_final_kernel(s_ref, *refs):
    refs[-1][...] = add_up(*(ref[...] for ref in refs[:-1])).T


def up_final_kernel(high, half, size, s_ref, *refs):
    up_ref, out_ref, sums_ref = refs[-3:]
    total = add_up(*(ref[...] for ref in refs[:-3]))
    for p in range(high // size):
        up_ref[:, span_of(p, half)] = total[span_of(p, size), :half]
    out_ref[...] = total[:high, half : half + size].T
    sums_ref[...] = total[high : high + 8, half:]


def reduce_any(mats, thin=None):
    blks = lax.axis_size("blk")
    lines = lax.axis_size("batch") // 2
    me = lax.axis_index("blk")
    core = lax.axis_index("batch") % 2
    line = lax.axis_index("batch") // 2
    pieces = []
    for mat in mats:
        rows = mat.shape[0] // (2 * lines)
        pieces.append(mat.reshape(lines, 2, rows, blks, -1))
    if thin is not None:
        thin = thin.reshape(lines, 2, rows, 1, -1)
        pieces.append(jnp.broadcast_to(thin, thin.shape[:3] + (blks,) + thin.shape[4:]))
    every = jnp.concatenate(pieces, axis=4)

    def half(which, distance):
        part = lax.dynamic_index_in_dim(every, which, 1, keepdims=False)
        return lax.dynamic_index_in_dim(part, me ^ distance, 2, keepdims=False)

    keep = [half(core, distance) for distance in range(blks)]
    got = swap(jnp.stack([half(1 - core, i) for i in range(blks)]), "batch", 1)
    chip = [add_up(part, got[i]).astype(BF16) for i, part in enumerate(keep)]
    total = add_up(chip[0], *(swap(chip[i], "blk", i) for i in range(1, blks)))
    while lines > 1:
        lines //= 2
        upper = line // lines
        pairs = total.astype(BF16).reshape((2, lines) + total.shape[1:])
        mine = lax.dynamic_index_in_dim(pairs, upper, 0, keepdims=False)
        theirs = lax.dynamic_index_in_dim(pairs, 1 - upper, 0, keepdims=False)
        total = add_up(mine, swap(theirs, "batch", 2 * lines))
        line = line % lines
    return total[0]


def shards(
    hidden_in, lengths, head_order, w_qkv, w_out, ln1_gain, ln1_bias, w_up, w_down, ln2_gain,
    ln2_bias, grad_out,
):
    _, _, rows, width = hidden_in.shape
    heads = head_order.shape[0]
    blks = lax.axis_size("blk")
    batch = lax.axis_size("batch")
    inner = w_up.shape[1]
    me = lax.axis_index("blk")
    at = lax.axis_index("batch")
    fast = batch == 8 and blks == 4 and width % (16 * batch) == 0
    lines = batch // 2 if fast else 0
    wide = inner // blks
    size = width // batch
    half = width // 2
    high = width // blks
    cols = 3 * width // blks

    x = hidden_in.reshape(rows, width)
    dout = grad_out.reshape(rows, width)
    xp = swap(x, "blk", 1)
    gain1, bias1, gain2, bias2 = (
        part.reshape(1, width) for part in (ln1_gain, ln1_bias, ln2_gain, ln2_bias)
    )
    length = lax.dynamic_index_in_dim(lengths[:, 0], me // 2, 0, keepdims=False)
    ids = jnp.arange(heads, dtype=jnp.int32)
    order = jnp.sum(jnp.where(head_order[None, :] == ids[:, None], ids[None, :], 0), axis=1)
    parts = [me, at % 2, at // 2, length - rows * (me % 2), length - rows * (1 - me % 2)]
    s = jnp.concatenate([jnp.stack(parts).astype(jnp.int32), order.astype(jnp.int32)])

    square = ((width, rows), BF16)
    lse = ((heads, 1, rows), F32)
    split = [((2, rows, width // 2), BF16)] if lines else []
    qkv, near_ctx, near_lse, *x_parts = call(
        functools.partial(near_kernel, heads, lines), s, (x, w_qkv),
        [((3 * width, rows), BF16), square, lse] + split, mib=8, us=8,
    )

    if lines:
        down_out = [((blks, high, inner // 2), BF16)] * 2 + split
    else:
        down_out = [((width, inner), BF16)]
    kv, ctx, far_lse, hid, slope, dtwo, upt, resid, gains, *down = call(
        functools.partial(ffn_kernel, heads, blks, lines), s,
        (x, xp, w_qkv, qkv, near_ctx, w_out, gain1, bias1, gain2, bias2, dout, w_up, w_down),
        [((2 * width, rows), BF16), square, lse, ((rows, width), BF16), ((rows, inner), BF16),
         ((rows, width), F32), square, ((rows, width), F32), ((8, width), F32)] + down_out,
        [((rows, inner), BF16)], mib=16, us=18,
    )

    s = after(s, dtwo)
    if lines:
        ups = Halves(half + size, wide + high + 16, half)
        up_out = [((blks, wide, half), BF16)] + [((blks, wide // 3, half), BF16)] * 3
        thin_out = [((blks, high + 16, half), BF16)] * 2
        proj_out = [((blks, cols, half), BF16)] + [((blks, cols, 128), BF16)] * (half // 128)
    else:
        up_out = [((width, inner), BF16)]
        thin_out = [((width, width), BF16), ((16, width), BF16)]
        proj_out = [((3 * width, width), BF16)]
    dpre, done = call(
        functools.partial(pre_back_kernel, blks), s, (dtwo, slope, w_down, w_up),
        [((rows, inner), BF16), ((rows, width), F32)], mib=8,
    )
    s = after(s, done)
    if lines:
        chip1 = down_first(s, down[0], swap(down[1], "batch", 1), lines)
        s = after(s, chip1[0])
    up = call(functools.partial(up_kernel, blks, lines), s, (dpre, upt), up_out, mib=8)
    s = after(s, up[0])
    dres, dctx, *thin = call(
        functools.partial(norm_back_kernel, blks, lines), s,
        (done, resid, gain1, gains, w_out, ctx), [((rows, width), F32), square] + thin_out, mib=8,
    )
    s = after(s, dctx)
    if lines:
        gots = [swap(part, "batch", 1) for part in (*up[1:], thin[1])]
        chip2 = ups.first(s, (up[0], thin[0]), gots)
        s = after(s, chip2[0])
    far_q, far_kv, *give = call(
        functools.partial(far_back_kernel, heads), s, (qkv, kv, ctx, dctx, far_lse, w_qkv),
        [((width // 2, rows), BF16), square, ((width - 128, rows), BF16), ((128, rows), BF16)],
        [((2 * width, rows), BF16)], mib=8,
    )
    s = after(s, far_q)
    if not lines:
        got_in = [swap(part, "blk", 1) for part in give]
    dqkv, *proj = call(
        functools.partial(near_back_kernel, heads, blks, lines), s,
        (qkv, ctx, dctx, near_lse, far_q, far_kv)
        + ((x_parts[0], down[2]) if lines else (x, xp)),
        [((3 * width, rows), BF16)] + proj_out, [square], mib=8,
    )
    s = after(s, dqkv)
    if lines:
        line1 = fourth(s, chip1)
        s = after(s, line1[0])
        pair2 = ups.second(s, chip2)
        s = after(s, pair2[0])
        got_in = [swap(part, "blk", 1) for part in lax.optimization_barrier((pair2[0], *give))[1:]]
        chip3 = proj_first(s, proj[0], [swap(part, "batch", 1) for part in proj[1:]])
        s = after(s, chip3[0])
        line2 = ups.third(s, pair2, wide, size, lines)
        s = after(s, line2[0])
        far1 = dealt(s, line1[0], swap(line1[1], "batch", 4))
        s = after(s, far1[0])
    (own,) = call(through_kernel, s, (w_qkv, dqkv), [((width, rows), F32)], mib=4)
    s = after(s, own)
    if lines:
        line3 = proj_second(s, chip3, lines)
        s = after(s, line3[0])
        last2 = fourth(s, line2)
        s = after(s, last2[0])
        last1 = paired(s, far1[0], swap(far1[1], "blk", 2))
        s = after(s, last1[0])
        last3 = fourth(s, line3)
        s = after(s, last3[0])
        (own_down,) = call(
            down_final_kernel, s, (last1[0], swap(last1[1], "blk", 1)),
            [((high, inner // batch), F32)], mib=4,
        )
        s = after(s, own_down)
        own_down = own_down.T
        own_up, own_out, thin = call(
            functools.partial(up_final_kernel, high, half, size), s,
            (last2[0], swap(last2[1], "batch", 4)),
            [((size, wide), F32), ((size, high), F32), ((8, 128), F32)], mib=4,
        )
        thin = thin[:4, :size]
        s = after(s, own_up)
    (grad_in,) = call(input_kernel, s, (own, *got_in, dres), [((rows, width), BF16)], mib=4)
    if lines:
        s = after(s, grad_in)
        (own_qkv,) = call(
            turned_final_kernel, s, (last3[0], swap(last3[1], "batch", 4)),
            [((size, cols), F32)], mib=4,
        )
    else:
        own_down = reduce_any([down[0].T])
        both = reduce_any([up[0], thin[0].T], thin[1][:4].T)
        own_up, own_out, thin = both[:, :wide], both[:, wide : wide + high], both[:, wide + high :].T
        own_qkv = reduce_any([proj[0].T])
    return (
        hid.reshape(hidden_in.shape),
        grad_in.reshape(hidden_in.shape),
        own_qkv,
        own_out,
        thin[0],
        thin[1],
        own_up,
        own_down,
        thin[2],
        thin[3],
    )


def solution(mesh):
    rows = P("blk", "batch", None, None)
    both = P("batch", "blk")
    return jax.shard_map(
        shards,
        mesh=mesh,
        in_specs=(rows, P(None, "batch")) + (P(),) * 9 + (rows,),
        out_specs=(rows, rows, both, both, P("batch"), P("batch"), both, both)
        + (P("batch"), P("batch")),
        check_vma=False,
    )
```

```python
import functools
import math

import jax
import jax.numpy as jnp
from jax import lax
from jax.experimental import pallas as pl
from jax.experimental.pallas import tpu as pltpu
from jax.sharding import PartitionSpec as P

F32 = jnp.float32
BF16 = jnp.bfloat16
MIB = 1 << 20
EPS = 1e-06
NEG = -1e30
LOG2E = math.log2(math.e)
FF_BLOCKS = 4
STEP = 96
EVERY = slice(None)
ME, CORE, LINE, NEAR, FAR, ORDER = range(6)


def swap(block, axis, bits):
    return lax.ppermute(block, axis, [(i, i ^ bits) for i in range(lax.axis_size(axis))])


def nn(a, b):
    return lax.dot_general(a, b, (((1,), (0,)), ((), ())), preferred_element_type=F32)


def nt(a, b):
    return lax.dot_general(a, b, (((1,), (1,)), ((), ())), preferred_element_type=F32)


def tn(a, b):
    return lax.dot_general(a, b, (((0,), (0,)), ((), ())), preferred_element_type=F32)


def call(kernel, scalars, ins, outs, scratch=(), mib=16, us=0):
    vmem = pl.BlockSpec(memory_space=pltpu.VMEM)
    return pl.pallas_call(
        kernel,
        in_specs=[pl.BlockSpec(memory_space=pltpu.SMEM)] + [vmem] * len(ins),
        out_specs=[vmem] * len(outs),
        out_shape=[jax.ShapeDtypeStruct(shape, dtype) for shape, dtype in outs],
        scratch_shapes=[pltpu.VMEM(shape, dtype) for shape, dtype in scratch],
        compiler_params=pltpu.CompilerParams(vmem_limit_bytes=mib * MIB),
        cost_estimate=pl.CostEstimate(
            flops=1000000 + us * 1150000000, bytes_accessed=10000, transcendentals=0
        ),
    )(scalars, *ins)


def rows_of(index, size):
    return pl.ds(pl.multiple_of(index * size, size), size)


def stacked(first, *rows):
    spare = lax.broadcasted_iota(jnp.int32, (16, first.shape[1]), 0)
    extra = jnp.zeros(spare.shape, F32)
    for i, row in enumerate(rows):
        extra = jnp.where(spare == i, row, extra)
    return jnp.concatenate([first, extra.astype(BF16)], axis=0)


def key_bias(valid, keys):
    place = lax.broadcasted_iota(jnp.int32, (1, keys), 1)
    return jnp.where(place < valid, 0.0, NEG)


def attend_head(coef, q, k, v, bias):
    dim = q.shape[0]
    raw = nn(stacked(k, bias).T, stacked(q, 1.0))
    top = jnp.max(raw, axis=0, keepdims=True)
    terms = jnp.exp2((raw - top) * coef).astype(BF16)
    got = nn(stacked(v, 1.0), terms)
    total = got[dim : dim + 1]
    return (got[:dim] / total).astype(BF16), top * coef + jnp.log2(total)


def attend_head_back(coef, scale, q, k, v, bias, lse, ctx, dctx):
    delta = jnp.sum(dctx.astype(F32) * ctx.astype(F32), axis=0, keepdims=True)
    raw = nn(stacked(k, bias).T, stacked(q, 1.0))
    probs = jnp.exp2(raw * coef - lse)
    draw = (probs * (nn(v.T, dctx) - delta)).astype(BF16)
    dv = nt(dctx, probs.astype(BF16)).astype(BF16)
    dk = (nt(q, draw) * scale).astype(BF16)
    dq = (nn(k, draw) * scale).astype(BF16)
    return dq, dk, dv


def norm_stats(hidden):
    mean = jnp.mean(hidden, axis=-1, keepdims=True)
    centred = hidden - mean
    var = jnp.mean(centred * centred, axis=-1, keepdims=True)
    inv = lax.rsqrt(var + EPS)
    return centred * inv, inv


def norm_back(grad, gain, hat, inv):
    scaled = grad * gain
    shift = jnp.mean(scaled, axis=-1, keepdims=True)
    slope = jnp.mean(scaled * hat, axis=-1, keepdims=True)
    back = inv * (scaled - shift - hat * slope)
    return back, jnp.sum(grad * hat, axis=0, keepdims=True), jnp.sum(grad, axis=0, keepdims=True)


def by_core(mat, core, lines):
    span = mat.shape[1] // (2 * lines)
    halves = [
        jnp.concatenate(
            [mat[:, (2 * z + p) * span : (2 * z + p + 1) * span] for z in range(lines)], axis=1
        )
        for p in range(2)
    ]
    even = core == 0
    return jnp.where(even, halves[0], halves[1]), jnp.where(even, halves[1], halves[0])


def rows_by_core(ref, core, lines):
    span = ref.shape[0] // (2 * lines)
    return [
        jnp.concatenate([ref[rows_of(2 * z + (core ^ which), span), :] for z in range(lines)], axis=0)
        for which in range(2)
    ]


def near_kernel(heads, lines, s_ref, x_ref, w_ref, qkv_ref, ctx_ref, lse_ref, *rest):
    width = x_ref.shape[1]
    dim = width // heads
    coef = LOG2E / math.sqrt(dim)
    turned = x_ref[...].T
    for part in range(3):
        at = slice(part * width, (part + 1) * width)
        qkv_ref[at, :] = tn(w_ref[:, at], turned).astype(BF16)
    if lines:
        rest[0][0], rest[0][1] = by_core(x_ref[...], s_ref[CORE], lines)
    bias = key_bias(s_ref[NEAR], x_ref.shape[0])

    def one(i, carry):
        head = s_ref[ORDER + i]
        at = rows_of(head, dim)
        ctx_ref[at, :], lse_ref[head] = attend_head(
            coef,
            qkv_ref[at, :],
            qkv_ref[rows_of(heads + head, dim), :],
            qkv_ref[rows_of(2 * heads + head, dim), :],
            bias,
        )
        return carry

    lax.fori_loop(0, heads // 2, one, 0, unroll=3)


def ffn_kernel(
    heads, blks, lines, s_ref, x_ref, xp_ref, w_ref, qkv_ref, near_ref, wo_ref, gain1_ref,
    bias1_ref, gain2_ref, bias2_ref, dout_ref, wu_ref, wd_ref,
    kv_ref, ctx_ref, lse_ref, hid_ref, slope_ref, dtwo_ref, upt_ref, resid_ref, gains_ref, *rest,
):
    act_ref = rest[-1]
    rows, width = x_ref.shape
    dim = width // heads
    coef = LOG2E / math.sqrt(dim)
    me, core = s_ref[ME], s_ref[CORE]
    turned = xp_ref[...].T
    for part in range(2):
        at = slice((part + 1) * width, (part + 2) * width)
        kv_ref[part * width : (part + 1) * width, :] = tn(w_ref[:, at], turned).astype(BF16)
    bias = key_bias(s_ref[FAR], rows)

    def one(i, carry):
        head = s_ref[ORDER + heads // 2 + i]
        at = rows_of(head, dim)
        ctx_ref[at, :], lse_ref[head] = attend_head(
            coef, qkv_ref[at, :], kv_ref[at, :], kv_ref[rows_of(heads + head, dim), :], bias
        )
        mine = rows_of(s_ref[ORDER + i], dim)
        ctx_ref[mine, :] = near_ref[mine, :]
        return carry

    lax.fori_loop(0, heads // 2, one, 0, unroll=3)

    resid = x_ref[...].astype(F32) + tn(ctx_ref[...], wo_ref[...])
    resid_ref[...] = resid
    hat, _ = norm_stats(resid)
    one_in = hat * gain1_ref[...] + bias1_ref[...]
    low = one_in.astype(BF16)
    upt_ref[...] = low.T
    total = one_in
    blk = wu_ref.shape[1] // FF_BLOCKS
    for j in range(FF_BLOCKS):
        at = slice(j * blk, (j + 1) * blk)
        pre = nn(low, wu_ref[:, at])
        cdf = 0.5 + 0.5 * lax.erf(pre * math.sqrt(0.5))
        pdf = jnp.exp2(pre * pre * (-0.5 * LOG2E)) * (1.0 / math.sqrt(2.0 * math.pi))
        slope_ref[:, at] = (cdf + pre * pdf).astype(BF16)
        act = (pre * cdf).astype(BF16)
        act_ref[:, at] = act
        total = total + nn(act, wd_ref[at, :])
    hat, inv = norm_stats(total)
    hid_ref[...] = (hat * gain2_ref[...] + bias2_ref[...]).astype(BF16)
    back, gain, shift = norm_back(dout_ref[...].astype(F32), gain2_ref[...], hat, inv)
    dtwo_ref[...] = back
    gains_ref[0:1, :] = gain
    gains_ref[1:2, :] = shift
    turned = back.astype(BF16).T
    if lines:
        high = width // blks
        span = act_ref.shape[1] // (2 * lines)
        for which in (1, 0):
            for z in range(0, lines, 2):
                pair = [act_ref[:, rows_of(2 * (z + i) + (core ^ which), span)] for i in range(2)]
                prod = nn(turned, jnp.concatenate(pair, axis=1)).astype(BF16)
                for k in range(blks):
                    rest[which][k ^ me, :, z * span : (z + 2) * span] = prod[
                        k * high : (k + 1) * high
                    ]
        rest[2][0], rest[2][1] = by_core(xp_ref[...], core, lines)
    else:
        rest[0][...] = nn(turned, act_ref[...]).astype(BF16)


def pre_back_kernel(blks, s_ref, dtwo_ref, slope_ref, wd_ref, wu_ref, dpre_ref, done_ref):
    low = dtwo_ref[...].astype(BF16)
    total = dtwo_ref[...]
    blk = wu_ref.shape[1] // blks
    for k in range(blks):
        at = slice(k * blk, (k + 1) * blk)
        dpre = (nt(low, wd_ref[at, :]) * slope_ref[:, at].astype(F32)).astype(BF16)
        dpre_ref[:, at] = dpre
        total = total + nt(dpre, wu_ref[:, at])
    done_ref[...] = total


def up_kernel(blks, lines, s_ref, dpre_ref, upt_ref, *outs):
    if not lines:
        outs[0][...] = nn(upt_ref[...], dpre_ref[...]).astype(BF16)
        return
    me, core = s_ref[ME], s_ref[CORE]
    blk = dpre_ref.shape[1] // blks
    high = outs[1].shape[1]
    for which, rows in ((1, 1), (0, 0)):
        mine = rows_by_core(upt_ref, core, lines)[rows]
        half = mine.shape[0]
        for k in range(blks):
            prod = nn(mine, dpre_ref[:, k * blk : (k + 1) * blk]).astype(BF16)
            if not which:
                for p in range(blk // half):
                    outs[0][k ^ me, p * half : (p + 1) * half, :] = prod[:, p * half : (p + 1) * half]
                continue
            for i, out in enumerate(outs[1:]):
                for p in range(blk // half):
                    low, end = max(p * half, i * high), min((p + 1) * half, (i + 1) * high)
                    if low < end:
                        out[k ^ me, low - i * high : end - i * high, :] = prod[
                            low - p * half : end - p * half, p * half : (p + 1) * half
                        ]


def norm_back_kernel(
    blks, lines, s_ref, done_ref, resid_ref, gain1_ref, gains_ref, wo_ref, ctx_ref, dres_ref,
    dctx_ref, *outs,
):
    me, core = s_ref[ME], s_ref[CORE]
    hat, inv = norm_stats(resid_ref[...])
    back, gain, shift = norm_back(done_ref[...], gain1_ref[...], hat, inv)
    dres_ref[...] = back
    turned = back.astype(BF16).T
    dctx_ref[...] = nn(wo_ref[...], turned).astype(BF16)
    row = lax.broadcasted_iota(jnp.int32, (16, gain.shape[1]), 0)
    sums = jnp.where(row == 0, gain, jnp.where(row == 1, shift, 0.0))
    sums = jnp.where(row == 2, gains_ref[0:1, :], sums)
    sums = jnp.where(row == 3, gains_ref[1:2, :], sums).astype(BF16)
    if not lines:
        outs[0][...] = nt(turned, ctx_ref[...]).astype(BF16)
        outs[1][...] = sums
        return
    ctxs = rows_by_core(ctx_ref, core, lines)
    sums = by_core(sums, core, lines)
    high = turned.shape[0] // blks
    both = nt(turned, jnp.concatenate(ctxs, axis=0)).astype(BF16)
    half = both.shape[1] // 2
    for which, (out, thin) in enumerate(zip(outs, sums)):
        for k in range(blks):
            out[k ^ me, :high, :] = both[k * high : (k + 1) * high, which * half : (which + 1) * half]
            out[k ^ me, high:, :] = thin


def far_back_kernel(
    heads, s_ref, qkv_ref, kv_ref, ctx_ref, dctx_ref, lse_ref, w_ref, dq_ref, dkv_ref, give_ref,
    rest_ref, wide_ref,
):
    width, rows = ctx_ref.shape
    dim = width // heads
    half = heads // 2
    scale = 1.0 / math.sqrt(dim)
    bias = key_bias(s_ref[FAR], rows)
    wide_ref[...] = jnp.zeros_like(wide_ref)

    def one(i, carry):
        head = s_ref[ORDER + half + i]
        at, low = rows_of(head, dim), rows_of(heads + head, dim)
        dq, dk, dv = attend_head_back(
            LOG2E * scale, scale, qkv_ref[at, :], kv_ref[at, :], kv_ref[low, :], bias,
            lse_ref[head], ctx_ref[at, :], dctx_ref[at, :],
        )
        dq_ref[rows_of(i, dim), :] = dq
        dkv_ref[rows_of(i, dim), :] = dk
        dkv_ref[rows_of(half + i, dim), :] = dv
        wide_ref[at, :] = dk
        wide_ref[low, :] = dv
        return carry

    lax.fori_loop(0, half, one, 0, unroll=3)
    give = nn(w_ref[:, width:], wide_ref[...]).astype(BF16)
    give_ref[...] = give[: give_ref.shape[0]]
    rest_ref[...] = give[give_ref.shape[0] :]


def near_back_kernel(
    heads, blks, lines, s_ref, qkv_ref, ctx_ref, dctx_ref, lse_ref, farq_ref, farkv_ref, x_ref,
    xp_ref, dqkv_ref, *rest,
):
    outs, near_ref = rest[:-1], rest[-1]
    width, rows = ctx_ref.shape
    dim = width // heads
    half = heads // 2
    scale = 1.0 / math.sqrt(dim)
    bias = key_bias(s_ref[NEAR], rows)
    me = s_ref[ME]
    dqkv_ref[width:, :] = jnp.zeros((2 * width, rows), BF16)

    def one(i, carry):
        head = s_ref[ORDER + i]
        at = rows_of(head, dim)
        key, value = rows_of(heads + head, dim), rows_of(2 * heads + head, dim)
        dq, dk, dv = attend_head_back(
            LOG2E * scale, scale, qkv_ref[at, :], qkv_ref[key, :], qkv_ref[value, :], bias,
            lse_ref[head], ctx_ref[at, :], dctx_ref[at, :],
        )
        dqkv_ref[at, :] = dq
        dqkv_ref[key, :] = dk
        dqkv_ref[value, :] = dv
        near_ref[rows_of(i, dim), :] = dk
        near_ref[rows_of(half + i, dim), :] = dv
        dqkv_ref[rows_of(s_ref[ORDER + half + i], dim), :] = farq_ref[rows_of(i, dim), :]
        return carry

    lax.fori_loop(0, half, one, 0, unroll=3)
    per = 3 * heads // blks

    def store(unit, prod):
        if not lines:
            outs[0][rows_of(unit, dim), :] = prod
            return
        at = ((unit // per) ^ me, rows_of(unit % per, dim), EVERY)
        keep = outs[0].shape[2]
        outs[0][at] = prod[:, :keep]
        for i, out in enumerate(outs[1:]):
            out[at] = prod[:, keep + i * 128 : keep + (i + 1) * 128]

    x = jnp.concatenate([x_ref[0], x_ref[1]], axis=1) if lines else x_ref[...]
    xp = jnp.concatenate([xp_ref[0], xp_ref[1]], axis=1) if lines else xp_ref[...]
    prod = nn(dqkv_ref[:width, :], x).astype(BF16)
    for h in range(heads):
        store(h, prod[h * dim : (h + 1) * dim])
    for first, grads, inputs in ((0, near_ref, x), (half, farkv_ref, xp)):
        prod = nn(grads[...], inputs).astype(BF16)
        for i in range(half):
            head = s_ref[ORDER + first + i]
            store(heads + head, prod[i * dim : (i + 1) * dim])
            low = (half + i) * dim
            store(2 * heads + head, prod[low : low + dim])


def through_kernel(s_ref, w_ref, dqkv_ref, own_ref):
    own_ref[...] = nn(w_ref[...], dqkv_ref[...])


def input_kernel(s_ref, own_ref, got_ref, rest_ref, dres_ref, out_ref):
    cut = got_ref.shape[0]
    for at, got in ((slice(0, cut), got_ref), (slice(cut, None), rest_ref)):
        total = own_ref[at, :] + got[...].astype(F32)
        out_ref[:, at] = (total.T + dres_ref[:, at]).astype(BF16)


def add_up(*parts):
    total = parts[0].astype(F32)
    for part in parts[1:]:
        total = total + part.astype(F32)
    return total


def after(scalars, *arrays):
    return lax.optimization_barrier((scalars,) + arrays)[0]


def block_at(ref, at):
    at = tuple(at) + (EVERY,) * (len(ref.shape) - len(at))
    first, last, _ = at[-2].indices(ref.shape[-2])
    return at[:-2], first, last - first, at[-1]


def sums_kernel(plan, lines, inputs, s_ref, *refs):
    ins, outs = refs[:inputs], refs[inputs:]

    def run(odd, upper):
        for terms, targets in plan(odd, upper) if lines else plan():
            found = [(ins[i],) + block_at(ins[i], src) for i, src in terms]
            places = [(outs[out],) + block_at(outs[out], dst) + (part,) for out, dst, part in targets]
            rows = found[0][3]

            def add(at, size):
                blocks = [
                    ref[leads + (pl.ds(at + row, size), col)] for ref, leads, row, _, col in found
                ]
                total = sum(blocks[1:], blocks[0]) if len(blocks) == 2 else add_up(*blocks).astype(BF16)
                for ref, leads, row, _, col, part in places:
                    ref[leads + (pl.ds(at + row, size), col)] = total[:, part]

            def body(i, carry):
                add(pl.multiple_of(i * STEP, STEP), STEP)
                return carry

            if rows >= 2 * STEP:
                lax.fori_loop(0, rows // STEP, body, 0)
                if rows % STEP:
                    add(rows // STEP * STEP, rows % STEP)
            else:
                add(0, rows)

    if lines:
        line = s_ref[LINE]
        for odd in range(2):
            pl.when(line % 2 == odd)(functools.partial(run, odd, line // 2))
    else:
        run(0, 0)


def sums(scalars, ins, shapes, plan, lines=False):
    kernel = functools.partial(sums_kernel, plan, lines, len(ins))
    return call(kernel, scalars, ins, [(shape, BF16) for shape in shapes], mib=4)


def span_of(index, size):
    return slice(index * size, (index + 1) * size)


def by_line(z, odd, upper):
    return (z % 2) ^ odd, (z // 2) ^ upper


class Halves:
    def __init__(self, cut, rows, cols):
        self.cut, self.rows, self.cols = cut, rows, cols
        self.sizes = (cut, rows - cut)
        self.at = (slice(0, cut), slice(cut, rows))

    def first(self, s, keeps, gots):
        shapes = [(2, size, self.cols) for size in self.sizes for _ in range(2)]
        picks = ((0, 0, (0, 2)), (1, 0, (1, 3)), (2, 1, (0, 1)), (3, 1, (2, 3)))
        wide = keeps[0].shape[1]

        def plan():
            found = []
            for out, half, group in picks:
                start, end = self.at[half].start, self.at[half].stop
                first = 0
                for i, got in enumerate(gots):
                    last = first + got.shape[1]
                    low, up = max(first, start), min(last, end)
                    kept = int(low >= wide)
                    for slot, j in enumerate(group) if low < up else ():
                        keep = (kept, (j, slice(low - kept * wide, up - kept * wide), EVERY))
                        other = (len(keeps) + i, (j, slice(low - first, up - first), EVERY))
                        here = (slot, slice(low - start, up - start), EVERY)
                        found.append(([keep, other], [(out, here, EVERY)]))
                    first = last
            return found

        return sums(s, (*keeps, *gots), shapes, plan)

    def second(self, s, chip):
        got = (swap(chip[1], "blk", 1), swap(chip[3], "blk", 2))
        shapes = [(size, self.cols) for size in self.sizes for _ in range(2)]

        def plan():
            return [
                ([(half, (slot,)), (2 + half, (slot,))], [(2 * half + slot, (EVERY,), EVERY)])
                for half in range(2)
                for slot in range(2)
            ]

        return sums(s, (chip[0], chip[2]) + got, shapes, plan)

    def third(self, s, pair, wide, size, lines):
        got = (swap(pair[1], "blk", 2), swap(pair[3], "blk", 1))
        half = self.cols
        shape = (self.rows - wide, half + 128)

        def plan(odd, upper):
            found = []
            for p in range(wide // half):
                for z in range(lines):
                    row = p * half + z * size
                    which = int(row >= self.cut)
                    row -= which * self.cut
                    out, slot = by_line(z, odd, upper)
                    src = (slice(row, row + size), EVERY)
                    dst = (slot, span_of(p, size), slice(0, half))
                    found.append(([(which, src), (2 + which, src)], [(out, dst, EVERY)]))
            src = (slice(wide - self.cut, None), EVERY)
            targets = []
            for z in range(lines):
                out, slot = by_line(z, odd, upper)
                targets.append((out, (slot, EVERY, slice(half, half + size)), span_of(z, size)))
            return found + [([(1, src), (3, src)], targets)]

        return sums(s, (pair[0], pair[2]) + got, [(2,) + shape] * 2, plan, True)


def proj_first(s, keep, gots):
    blks, rows, cols = keep.shape

    def plan():
        return [
            ([(0, (j, EVERY, span_of(i, 128))), (1 + i, (j,))], [(j, (EVERY, span_of(i, 128)), EVERY)])
            for j in range(blks)
            for i in range(len(gots))
        ]

    return sums(s, (keep,) + tuple(gots), [(rows, cols)] * blks, plan)


def proj_second(s, chip, lines):
    parts = [chip[0]] + [swap(chip[i], "blk", i) for i in range(1, len(chip))]
    rows, cols = chip[0].shape
    size = cols // lines

    def plan(odd, upper):
        targets = []
        for z in range(lines):
            out, slot = by_line(z, odd, upper)
            targets.append((out, (slot,), span_of(z, size)))
        return [([(i, (EVERY,)) for i in range(len(parts))], targets)]

    return sums(s, parts, [(2, rows, size)] * 2, plan, True)


def fourth(s, mine):
    return paired(s, mine[0], swap(mine[1], "batch", 2))


def dealt(s, keep, got):
    def plan():
        return [
            ([(i, (2 * out + slot,)) for i in range(2)], [(out, (slot,), EVERY)])
            for out in range(2)
            for slot in range(2)
        ]

    return sums(s, (keep, got), [(2,) + keep.shape[1:]] * 2, plan)


def paired(s, keep, got):
    def plan():
        return [([(0, (i,)), (1, (i,))], [(i, (EVERY,), EVERY)]) for i in range(2)]

    return sums(s, (keep, got), [keep.shape[1:]] * 2, plan)


def down_first(s, keep, got, lines):
    blks, high, cols = keep.shape
    size = cols // lines

    def plan(odd, upper):
        found = []
        for z in range(lines):
            out, slot = by_line(z, odd, upper)
            for j in range(blks):
                src = (j, EVERY, span_of(z, size))
                found.append(([(0, src), (1, src)], [(out, (slot, j), EVERY)]))
        return found

    return sums(s, (keep, got), [(2, blks, high, size)] * 2, plan, True)


def down_final_kernel(s_ref, *refs):
    refs[-1][...] = add_up(*(ref[...] for ref in refs[:-1]))


def turned_final_kernel(s_ref, *refs):
    refs[-1][...] = add_up(*(ref[...] for ref in refs[:-1])).T


def up_final_kernel(high, half, size, s_ref, *refs):
    up_ref, out_ref, sums_ref = refs[-3:]
    total = add_up(*(ref[...] for ref in refs[:-3]))
    for p in range(high // size):
        up_ref[:, span_of(p, half)] = total[span_of(p, size), :half]
    out_ref[...] = total[:high, half : half + size].T
    sums_ref[...] = total[high : high + 8, half:]


def reduce_any(mats, thin=None):
    blks = lax.axis_size("blk")
    lines = lax.axis_size("batch") // 2
    me = lax.axis_index("blk")
    core = lax.axis_index("batch") % 2
    line = lax.axis_index("batch") // 2
    pieces = []
    for mat in mats:
        rows = mat.shape[0] // (2 * lines)
        pieces.append(mat.reshape(lines, 2, rows, blks, -1))
    if thin is not None:
        thin = thin.reshape(lines, 2, rows, 1, -1)
        pieces.append(jnp.broadcast_to(thin, thin.shape[:3] + (blks,) + thin.shape[4:]))
    every = jnp.concatenate(pieces, axis=4)

    def half(which, distance):
        part = lax.dynamic_index_in_dim(every, which, 1, keepdims=False)
        return lax.dynamic_index_in_dim(part, me ^ distance, 2, keepdims=False)

    keep = [half(core, distance) for distance in range(blks)]
    got = swap(jnp.stack([half(1 - core, i) for i in range(blks)]), "batch", 1)
    chip = [add_up(part, got[i]).astype(BF16) for i, part in enumerate(keep)]
    total = add_up(chip[0], *(swap(chip[i], "blk", i) for i in range(1, blks)))
    while lines > 1:
        lines //= 2
        upper = line // lines
        pairs = total.astype(BF16).reshape((2, lines) + total.shape[1:])
        mine = lax.dynamic_index_in_dim(pairs, upper, 0, keepdims=False)
        theirs = lax.dynamic_index_in_dim(pairs, 1 - upper, 0, keepdims=False)
        total = add_up(mine, swap(theirs, "batch", 2 * lines))
        line = line % lines
    return total[0]


def shards(
    hidden_in, lengths, head_order, w_qkv, w_out, ln1_gain, ln1_bias, w_up, w_down, ln2_gain,
    ln2_bias, grad_out,
):
    _, _, rows, width = hidden_in.shape
    heads = head_order.shape[0]
    blks = lax.axis_size("blk")
    batch = lax.axis_size("batch")
    inner = w_up.shape[1]
    me = lax.axis_index("blk")
    at = lax.axis_index("batch")
    fast = batch == 8 and blks == 4 and width % (16 * batch) == 0
    lines = batch // 2 if fast else 0
    wide = inner // blks
    size = width // batch
    half = width // 2
    high = width // blks
    cols = 3 * width // blks

    x = hidden_in.reshape(rows, width)
    dout = grad_out.reshape(rows, width)
    xp = swap(x, "blk", 1)
    gain1, bias1, gain2, bias2 = (
        part.reshape(1, width) for part in (ln1_gain, ln1_bias, ln2_gain, ln2_bias)
    )
    length = lax.dynamic_index_in_dim(lengths[:, 0], me // 2, 0, keepdims=False)
    ids = jnp.arange(heads, dtype=jnp.int32)
    order = jnp.sum(jnp.where(head_order[None, :] == ids[:, None], ids[None, :], 0), axis=1)
    parts = [me, at % 2, at // 2, length - rows * (me % 2), length - rows * (1 - me % 2)]
    s = jnp.concatenate([jnp.stack(parts).astype(jnp.int32), order.astype(jnp.int32)])

    square = ((width, rows), BF16)
    lse = ((heads, 1, rows), F32)
    split = [((2, rows, width // 2), BF16)] if lines else []
    qkv, near_ctx, near_lse, *x_parts = call(
        functools.partial(near_kernel, heads, lines), s, (x, w_qkv),
        [((3 * width, rows), BF16), square, lse] + split, mib=8, us=8,
    )

    if lines:
        down_out = [((blks, high, inner // 2), BF16)] * 2 + split
    else:
        down_out = [((width, inner), BF16)]
    kv, ctx, far_lse, hid, slope, dtwo, upt, resid, gains, *down = call(
        functools.partial(ffn_kernel, heads, blks, lines), s,
        (x, xp, w_qkv, qkv, near_ctx, w_out, gain1, bias1, gain2, bias2, dout, w_up, w_down),
        [((2 * width, rows), BF16), square, lse, ((rows, width), BF16), ((rows, inner), BF16),
         ((rows, width), F32), square, ((rows, width), F32), ((8, width), F32)] + down_out,
        [((rows, inner), BF16)], mib=16, us=18,
    )

    s = after(s, dtwo)
    if lines:
        ups = Halves(half + size, wide + high + 16, half)
        up_out = [((blks, wide, half), BF16)] + [((blks, wide // 3, half), BF16)] * 3
        thin_out = [((blks, high + 16, half), BF16)] * 2
        proj_out = [((blks, cols, half), BF16)] + [((blks, cols, 128), BF16)] * (half // 128)
    else:
        up_out = [((width, inner), BF16)]
        thin_out = [((width, width), BF16), ((16, width), BF16)]
        proj_out = [((3 * width, width), BF16)]
    dpre, done = call(
        functools.partial(pre_back_kernel, blks), s, (dtwo, slope, w_down, w_up),
        [((rows, inner), BF16), ((rows, width), F32)], mib=8,
    )
    s = after(s, done)
    if lines:
        chip1 = down_first(s, down[0], swap(down[1], "batch", 1), lines)
        s = after(s, chip1[0])
    up = call(functools.partial(up_kernel, blks, lines), s, (dpre, upt), up_out, mib=8)
    s = after(s, up[0])
    dres, dctx, *thin = call(
        functools.partial(norm_back_kernel, blks, lines), s,
        (done, resid, gain1, gains, w_out, ctx), [((rows, width), F32), square] + thin_out, mib=8,
    )
    s = after(s, dctx)
    if lines:
        gots = [swap(part, "batch", 1) for part in (*up[1:], thin[1])]
        chip2 = ups.first(s, (up[0], thin[0]), gots)
        s = after(s, chip2[0])
    far_q, far_kv, *give = call(
        functools.partial(far_back_kernel, heads), s, (qkv, kv, ctx, dctx, far_lse, w_qkv),
        [((width // 2, rows), BF16), square, ((width - 64, rows), BF16), ((64, rows), BF16)],
        [((2 * width, rows), BF16)], mib=8,
    )
    s = after(s, far_q)
    if not lines:
        got_in = [swap(part, "blk", 1) for part in give]
    dqkv, *proj = call(
        functools.partial(near_back_kernel, heads, blks, lines), s,
        (qkv, ctx, dctx, near_lse, far_q, far_kv)
        + ((x_parts[0], down[2]) if lines else (x, xp)),
        [((3 * width, rows), BF16)] + proj_out, [square], mib=8,
    )
    s = after(s, dqkv)
    if lines:
        line1 = fourth(s, chip1)
        s = after(s, line1[0])
        pair2 = ups.second(s, chip2)
        s = after(s, pair2[0])
        got_in = [swap(part, "blk", 1) for part in lax.optimization_barrier((pair2[0], *give))[1:]]
        chip3 = proj_first(s, proj[0], [swap(part, "batch", 1) for part in proj[1:]])
        s = after(s, chip3[0])
        line2 = ups.third(s, pair2, wide, size, lines)
        s = after(s, line2[0])
        far1 = dealt(s, line1[0], swap(line1[1], "batch", 4))
        s = after(s, far1[0])
    (own,) = call(through_kernel, s, (w_qkv, dqkv), [((width, rows), F32)], mib=4)
    s = after(s, own)
    if lines:
        line3 = proj_second(s, chip3, lines)
        s = after(s, line3[0])
        last2 = fourth(s, line2)
        s = after(s, last2[0])
        last1 = paired(s, far1[0], swap(far1[1], "blk", 2))
        s = after(s, last1[0])
        last3 = fourth(s, line3)
        s = after(s, last3[0])
        (own_down,) = call(
            down_final_kernel, s, (last1[0], swap(last1[1], "blk", 1)),
            [((high, inner // batch), F32)], mib=4,
        )
        s = after(s, own_down)
        own_down = own_down.T
        own_up, own_out, thin = call(
            functools.partial(up_final_kernel, high, half, size), s,
            (last2[0], swap(last2[1], "batch", 4)),
            [((size, wide), F32), ((size, high), F32), ((8, 128), F32)], mib=4,
        )
        thin = thin[:4, :size]
        s = after(s, own_up)
    (grad_in,) = call(input_kernel, s, (own, *got_in, dres), [((rows, width), BF16)], mib=4)
    if lines:
        s = after(s, grad_in)
        (own_qkv,) = call(
            turned_final_kernel, s, (last3[0], swap(last3[1], "batch", 4)),
            [((size, cols), F32)], mib=4,
        )
    else:
        own_down = reduce_any([down[0].T])
        both = reduce_any([up[0], thin[0].T], thin[1][:4].T)
        own_up, own_out, thin = both[:, :wide], both[:, wide : wide + high], both[:, wide + high :].T
        own_qkv = reduce_any([proj[0].T])
    return (
        hid.reshape(hidden_in.shape),
        grad_in.reshape(hidden_in.shape),
        own_qkv,
        own_out,
        thin[0],
        thin[1],
        own_up,
        own_down,
        thin[2],
        thin[3],
    )


def solution(mesh):
    rows = P("blk", "batch", None, None)
    both = P("batch", "blk")
    return jax.shard_map(
        shards,
        mesh=mesh,
        in_specs=(rows, P(None, "batch")) + (P(),) * 9 + (rows,),
        out_specs=(rows, rows, both, both, P("batch"), P("batch"), both, both)
        + (P("batch"), P("batch")),
        check_vma=False,
    )
```
